32 devices in a mesh: member: 2 (over x), wide: 16 (over z, y, core).
Axes of the slice: x: 2, y: 2, z: 4, core: 2. Of those that a mesh axis runs over, the one named last changes fastest.
Arguments:
- stream_now: float32 [4, 256, 4096], P('member', 'wide'), parts along dimension 0, may hold values from -6 to 6
- vorticity: float32 [4, 256, 4096], P('member', 'wide'), parts along dimension 0, may hold values from -0.62 to 0.62
Outputs:
- vorticity_next: float32 [4, 256, 4096], P('member', 'wide'), parts along dimension 0
- stream_next: float32 [4, 256, 4096], P('member', 'wide'), parts along dimension 0
The draws below stay inside these ranges and needn't reach their ends.
There are 2 independent parts, one for each index of `member`. The reference program is written for one: setup_inputs(seed, part) draws one part's arguments, and reference() takes and returns one part's arrays. A program takes and returns all parts, laid end to end along the dimension named above; each array names one. Nothing has to cross between parts.
All inputs are finite; a program needn't handle non-finite values.
Results may differ from the reference program's by a relative error of at most 0.00002.
Values sent between devices are 32-bit elements; how exact they have to be, the bound alone decides.
No kernel may reach another device: no remote copies, remote signals or barrier semaphores. Data moves between devices by JAX's collectives and lax.ppermute only.
A program may use at most 128 MiB of HBM per device.

```python
import jax
import jax.numpy as jnp

COLS = 4096
LEVELS = 5
SWEEPS = 2
COARSE_SWEEPS = 8
NY = 256


def draw_vorticity(key, part):
    rough_key, phase_key = jax.random.split(jax.random.fold_in(key, 11))
    full_turn = 6.283185307179586
    phases = jax.random.uniform(phase_key, (2, 2), jnp.float32, 0.0, full_turn)
    row_frac = (jnp.arange(NY, dtype=jnp.float32) / NY)[None, :, None]
    col_frac = (jnp.arange(COLS, dtype=jnp.float32) / COLS)[None, None, :]
    wave = jnp.sin(full_turn * row_frac + phases[:, 0, None, None]) * jnp.cos(2.0 * full_turn * col_frac + phases[:, 1, None, None])
    rough = 0.1 * jnp.clip(jax.random.normal(rough_key, (2, NY, COLS), jnp.float32), -6.0, 6.0)
    smooth = 0.01 * wave
    return rough + smooth


def block_levels(rng, shape, cuts, low, largest):
    factor_of, own = 1.0, jax.random.fold_in(rng, 6)
    for axis_at, shards_of in cuts:
        steps = jnp.exp(jax.random.uniform(jax.random.fold_in(own, axis_at), (shards_of,), jnp.float32, low / len(cuts), largest / len(cuts)))
        factor_of = factor_of * jnp.repeat(steps, shape[axis_at] // shards_of).reshape([-1 if axis == axis_at else 1 for axis in range(len(shape))])
    return factor_of


def gaussian(stream_key, extent, scale, most, shards=(), kind=jnp.bfloat16):
    values = jax.random.normal(stream_key, extent, jnp.float32) * scale
    if len(shards) > 0:
        values = block_levels(stream_key, extent, shards, -0.22, 0.18) * values
    return jnp.clip(values, min=-most, max=most).astype(kind)


def setup_inputs(seed: int = 0, part: int = 0) -> dict:
    key_list = jax.random.split(jax.random.key(seed), 3)
    own_keys = jax.random.split(jax.random.fold_in(key_list[2], part), 3)
    return {
        "stream_now": gaussian(own_keys[0], (2, NY, COLS), 1.0, 6.0, ((1, 16),), jnp.float32),
        "vorticity": draw_vorticity(jax.random.fold_in(jax.random.fold_in(key_list[2], part), 71), part),
    }


relax_weight = 0.8
coupling_upper = 0.02
coupling_lower = 0.04
time_step = 0.5
beta_slope = 0.05
bottom_drag = 0.02


def coupling():
    return jnp.array([coupling_upper, coupling_lower], jnp.float32)[:, None, None]


def diagonal(spacing):
    return 4.0 / (spacing * spacing) + coupling()


def pad_rows(iterate):
    return jnp.pad(iterate, ((0, 0), (1, 1), (0, 0)))


def neighbours(padded):
    interior = padded[:, 1:-1, :]
    return padded[:, 2:, :] + padded[:, :-2, :] + jnp.roll(interior, 1, axis=2) + jnp.roll(interior, -1, axis=2)


def apply_operator(padded, spacing):
    interior = padded[:, 1:-1, :]
    return (4.0 * interior - neighbours(padded)) / (spacing * spacing) + coupling() * (interior - interior[::-1])


def jacobi(padded, source, spacing):
    return padded[:, 1:-1, :] + relax_weight * (source - apply_operator(padded, spacing)) / diagonal(spacing)


def shifted(padded, row_step, col_step):
    row_count = padded.shape[1] - 2
    return jnp.roll(padded[:, 1 + row_step:1 + row_step + row_count, :], -col_step, axis=2)


def arakawa(stream_padded, vorticity_padded):
    def stream_at(row_step, col_step):
        return shifted(stream_padded, row_step, col_step)

    def vorticity_at(row_step, col_step):
        return shifted(vorticity_padded, row_step, col_step)

    first_form = (stream_at(0, 1) - stream_at(0, -1)) * (vorticity_at(1, 0) - vorticity_at(-1, 0)) - (stream_at(1, 0) - stream_at(-1, 0)) * (vorticity_at(0, 1) - vorticity_at(0, -1))
    second_form = stream_at(0, 1) * (vorticity_at(1, 1) - vorticity_at(-1, 1)) - stream_at(0, -1) * (vorticity_at(1, -1) - vorticity_at(-1, -1)) - stream_at(1, 0) * (vorticity_at(1, 1) - vorticity_at(1, -1)) + stream_at(-1, 0) * (vorticity_at(-1, 1) - vorticity_at(-1, -1))
    third_form = vorticity_at(1, 0) * (stream_at(1, 1) - stream_at(1, -1)) - vorticity_at(-1, 0) * (stream_at(-1, 1) - stream_at(-1, -1)) - vorticity_at(0, 1) * (stream_at(1, 1) - stream_at(-1, 1)) + vorticity_at(0, -1) * (stream_at(1, -1) - stream_at(-1, -1))
    return (first_form + second_form + third_form) / 12.0


def advance(stream_padded, vorticity_padded, stream_now, vorticity):
    jacobian = arakawa(stream_padded, vorticity_padded)
    zonal_slope = (jnp.roll(stream_now, -1, axis=2) - jnp.roll(stream_now, 1, axis=2)) * 0.5
    drag_term = jnp.array([0.0, bottom_drag], jnp.float32)[:, None, None] * (neighbours(stream_padded) - 4.0 * stream_now)
    return vorticity - time_step * (jacobian + beta_slope * zonal_slope + drag_term)


def restrict(residual):
    return 0.25 * (((residual[:, 0::2, 0::2] + residual[:, 1::2, 0::2]) + residual[:, 0::2, 1::2]) + residual[:, 1::2, 1::2])


def prolong(correction):
    layers, row_count, col_count = correction.shape
    spread = jnp.broadcast_to(correction[:, :, None, :, None], (layers, row_count, 2, col_count, 2))
    return spread.reshape(layers, 2 * row_count, 2 * col_count)


def relax_sweeps(iterate, source, spacing, sweep_count, zero_start):
    for sweep_index in range(sweep_count):
        if zero_start and sweep_index == 0:
            iterate = relax_weight * source / diagonal(spacing)
        else:
            iterate = jacobi(pad_rows(iterate), source, spacing)
    return iterate


def vcycle(grid_level, iterate, source, zero_start):
    spacing = 2.0 ** grid_level
    if grid_level == LEVELS - 1:
        return relax_sweeps(source, source, spacing, COARSE_SWEEPS, True)
    iterate = relax_sweeps(iterate, source, spacing, SWEEPS, zero_start)
    residual = source - apply_operator(pad_rows(iterate), spacing)
    coarse_source = restrict(residual)
    correction = vcycle(grid_level + 1, coarse_source, coarse_source, True)
    iterate = iterate + prolong(correction)
    return relax_sweeps(iterate, source, spacing, SWEEPS, False)


def reference(stream_now, vorticity):
    vorticity_next = advance(pad_rows(stream_now), pad_rows(vorticity), stream_now, vorticity)
    stream_next = vcycle(0, stream_now, -vorticity_next, False)
    return vorticity_next, stream_next
```

```python
import functools

import jax
import jax.numpy as jnp
from jax import lax
from jax.experimental import pallas as pl
from jax.experimental.pallas import tpu as pltpu
from jax.sharding import PartitionSpec as P


LANES = 128
SUBS = 8
HALO = 4
RELAX = 0.8
COUPLING = (0.02, 0.04)
TIME_STEP = 0.5
BETA = 0.05
DRAG = (0.0, 0.02)
COARSE_SWEEPS = 8


class Level:
    def __init__(self, level, tiles, stride):
        h2 = (2.0**level) ** 2
        self.tiles, self.stride = tiles, stride
        diag = [4.0 / h2 + f for f in COUPLING]
        self.keep = 1.0 - RELAX
        self.near = [RELAX / (d * h2) for d in diag]
        self.other = [RELAX * f / d for f, d in zip(COUPLING, diag)]
        self.src = [RELAX / d for d in diag]
        self.diag = diag
        self.inv_h2 = 1.0 / h2
        self.size = tiles * SUBS


def lane_index():
    return lax.broadcasted_iota(jnp.int32, (SUBS, LANES), 1)


def at(level, row, tile=0):
    base = row * level.size
    if not isinstance(row, int):
        base = pl.multiple_of(base, SUBS)
    return pl.ds(base + tile * SUBS, SUBS)


def load(ref, level, layer, row):
    return [ref[layer, at(level, row, t), :] for t in range(level.tiles)]


def store(ref, level, layer, row, values):
    for t in range(level.tiles):
        ref[layer, at(level, row, t), :] = values[t]


def east(values, stride=1):
    rolled = [pltpu.roll(v, LANES - stride, 1) for v in values]
    after = rolled[1:] + [pltpu.roll(rolled[0], SUBS - 1, 0)]
    edge = lane_index() >= LANES - stride
    return [jnp.where(edge, a, r) for a, r in zip(after, rolled)]


def west(values, stride=1):
    rolled = [pltpu.roll(v, stride, 1) for v in values]
    before = [pltpu.roll(rolled[-1], 1, 0)] + rolled[:-1]
    edge = lane_index() < stride
    return [jnp.where(edge, b, r) for b, r in zip(before, rolled)]


def row_blocks(low, high, block, body):
    count = high - low if isinstance(low, int) else high
    whole = count // block
    if whole > 1:
        lax.fori_loop(0, whole, lambda i, c: (body(low + i * block, block), c)[1], 0)
    elif whole == 1:
        body(low, block)
    if count % block:
        body(low + whole * block, count % block)


def star(rows, k, layer, level):
    centre = rows[k][layer]
    e, w = east(centre, level.stride), west(centre, level.stride)
    return [
        (n + s) + (a + b)
        for n, s, a, b in zip(rows[k + 1][layer], rows[k - 1][layer], e, w)
    ]


def load_rows(ref, level, first, count, margin=1):
    return {
        k: [load(ref, level, layer, first + k) for layer in range(2)]
        for k in range(-margin, count + margin)
    }


def sweep_rows(level, rows, source, count):
    out = {}
    for k in range(count):
        out[k] = []
        for layer in range(2):
            near = star(rows, k, layer, level)
            out[k].append(
                [
                    (level.keep * c + level.near[layer] * n)
                    + (level.other[layer] * o + level.src[layer] * b)
                    for c, n, o, b in zip(
                        rows[k][layer], near, rows[k][1 - layer], source[k][layer]
                    )
                ]
            )
    return out


def residual_rows(level, rows, source, count):
    out = {}
    for k in range(count):
        out[k] = []
        for layer in range(2):
            near = star(rows, k, layer, level)
            out[k].append(
                [
                    (b - level.diag[layer] * c)
                    + (level.inv_h2 * n + COUPLING[layer] * o)
                    for c, n, o, b in zip(
                        rows[k][layer], near, rows[k][1 - layer], source[k][layer]
                    )
                ]
            )
    return out


def store_rows(ref, level, first, rows, count):
    for k in range(count):
        for layer in range(2):
            store(ref, level, layer, first + k, rows[k][layer])


def sweep(level, dst, dst_at, src, src_at, b, b_at, low, high, block):
    def body(first, count):
        rows = load_rows(src, level, first + src_at, count)
        source = load_rows(b, level, first + b_at, count, 0)
        store_rows(dst, level, first + dst_at, sweep_rows(level, rows, source, count), count)

    row_blocks(low, high, block, body)


def start(level, dst, dst_at, b, b_at, low, high, block):
    def body(first, count):
        source = load_rows(b, level, first + b_at, count, 0)
        out = {
            k: [[level.src[l] * x for x in source[k][l]] for l in range(2)]
            for k in range(count)
        }
        store_rows(dst, level, first + dst_at, out, count)

    row_blocks(low, high, block, body)


def pack_columns(values):
    lane = lane_index()
    pick = (2 * lane) % LANES
    sums = [v + pltpu.roll(v, LANES - 1, 1) for v in values]
    picked = [jnp.take_along_axis(s, pick, axis=1) for s in sums]
    return [
        jnp.where(lane < LANES // 2, picked[2 * t], picked[2 * t + 1])
        for t in range(len(values) // 2)
    ]


def spread_columns(values):
    lane = lane_index()
    out = []
    for v in values:
        out.append(jnp.take_along_axis(v, lane // 2, axis=1))
        out.append(jnp.take_along_axis(v, LANES // 2 + lane // 2, axis=1))
    return out


def merge_columns(values, stride):
    even = (lane_index() // stride) % 2 == 0
    return [
        v + jnp.where(even, pltpu.roll(v, LANES - stride, 1), pltpu.roll(v, stride, 1))
        for v in values
    ]


def restrict(fine, dst, dst_at, coarse, src, src_at, b, b_at, low, high, block):
    def body(first, count):
        rows = load_rows(src, fine, 2 * first + src_at, 2 * count)
        source = load_rows(b, fine, 2 * first + b_at, 2 * count, 0)
        res = residual_rows(fine, rows, source, 2 * count)
        out = {}
        for k in range(count):
            out[k] = []
            for layer in range(2):
                pair = [x + y for x, y in zip(res[2 * k][layer], res[2 * k + 1][layer])]
                if coarse.tiles < fine.tiles:
                    pair = pack_columns(pair)
                else:
                    pair = merge_columns(pair, fine.stride)
                out[k].append([0.25 * x for x in pair])
        store_rows(dst, coarse, first + dst_at, out, count)

    row_blocks(low, high, block, body)


def correct(fine, coarse, dst, dst_at, src, src_at, add, add_at, low, high, block):
    def body(first, count):
        coarse_rows = load_rows(add, coarse, first + add_at, count, 0)
        fine_rows = load_rows(src, fine, 2 * first + src_at, 2 * count, 0)
        out = {}
        for k in range(count):
            spread = [
                spread_columns(v) if coarse.tiles < fine.tiles else v for v in coarse_rows[k]
            ]
            for half in range(2):
                out[2 * k + half] = [
                    [x + y for x, y in zip(fine_rows[2 * k + half][l], spread[l])]
                    for l in range(2)
                ]
        store_rows(dst, fine, 2 * first + dst_at, out, 2 * count)

    row_blocks(low, high, block, body)


def clear(ref, level, low, high):
    ref[:, low * level.size : high * level.size, :] = jnp.zeros(
        (ref.shape[0], (high - low) * level.size, LANES), jnp.float32
    )


def place():
    me, count = lax.axis_index("wide"), lax.axis_size("wide")
    return me, lax.rem(me, 2), me == 0, me == count - 1


def to_native(dst, src, level, src_at, rows):
    for layer in range(2):
        for group in range(rows // SUBS):
            for t in range(level.tiles):
                for s in range(SUBS):
                    first = (src_at + group * SUBS) * level.size + t * SUBS + s
                    column = (s * level.tiles + t) * LANES
                    dst[layer, group * SUBS : (group + 1) * SUBS, column : column + LANES] = src[
                        layer, pl.ds(first, SUBS, stride=level.size), :
                    ]


def pack_kernel(level, rows, p_ref, q_ref, x_ref, near_ref, far_ref):
    for field, ref in enumerate((p_ref, q_ref)):
        for layer in range(2):
            for group in range(rows // SUBS):
                for t in range(level.tiles):
                    for s in range(SUBS):
                        first = group * SUBS * level.size + t * SUBS + s
                        column = (s * level.tiles + t) * LANES
                        x_ref[2 * field + layer, pl.ds(first, SUBS, stride=level.size), :] = ref[
                            layer, group * SUBS : (group + 1) * SUBS, column : column + LANES
                        ]
    send_edges(level, rows, x_ref, 0, near_ref, far_ref)


def send_edges(level, rows, src, src_at, near_ref, far_ref):
    _, odd, _, _ = place()
    size = HALO * level.size
    last = (src_at + rows - HALO) * level.size
    top = src_at * level.size
    near = pl.multiple_of(jnp.where(odd == 1, top, last), SUBS)
    far = pl.multiple_of(jnp.where(odd == 1, last, top), SUBS)
    near_ref[...] = src[:, pl.ds(near, size), :]
    far_ref[...] = src[:, pl.ds(far, size), :]


def join(level, rows, dst, own, near_ref, far_ref):
    _, odd, first, last = place()
    size = HALO * level.size
    low = (HALO + rows) * level.size
    near = pl.multiple_of(jnp.where(odd == 1, 0, low), SUBS)
    far = pl.multiple_of(jnp.where(odd == 1, low, 0), SUBS)
    dst[:, size : size + rows * level.size, :] = own[...]
    dst[:, pl.ds(near, size), :] = near_ref[...]
    outside = jnp.logical_or(first, last)
    dst[:, pl.ds(far, size), :] = jnp.where(outside, 0.0, far_ref[...])


def fine_kernel(
    level, coarse, rows, x_ref, near_ref, far_ref,
    next_ref, b_ref, v_ref, bc_ref, bc_near_ref, bc_far_ref,
    ext, e_ref, w_ref, b_all, v_one,
):
    _, _, is_first, is_last = place()
    total = rows + 2 * HALO
    join(level, rows, ext, x_ref, near_ref, far_ref)

    def shift_body(first, count):
        for k in range(count):
            for f in range(4):
                v = load(ext, level, f, first + k)
                store(e_ref, level, f, first + k, east(v))
                store(w_ref, level, f, first + k, west(v))

    row_blocks(0, total, 2, shift_body)

    def advance_body(first, count):
        for layer in range(2):
            for t in range(level.tiles):
                def grab(ref, field):
                    return {
                        k: ref[2 * field + layer, at(level, first + k, t), :]
                        for k in range(-1, count + 1)
                    }

                p, pe, pw = grab(ext, 0), grab(e_ref, 0), grab(w_ref, 0)
                q, qe, qw = grab(ext, 1), grab(e_ref, 1), grab(w_ref, 1)
                zonal = {k: pe[k] - pw[k] for k in p}
                for k in range(count):
                    n, s = k + 1, k - 1
                    v0, ve, vw = p[n] - p[s], pe[n] - pe[s], pw[n] - pw[s]
                    jac = q[n] * (zonal[k] + zonal[n]) - q[s] * (zonal[k] + zonal[s])
                    jac = jac - qe[k] * (v0 + ve) + qw[k] * (v0 + vw)
                    jac = jac + qe[n] * (pe[k] - p[n]) - qe[s] * (pe[k] - p[s])
                    jac = jac - qw[n] * (pw[k] - p[n]) + qw[s] * (pw[k] - p[s])
                    step = (TIME_STEP / 12.0) * jac + (0.5 * TIME_STEP * BETA) * zonal[k]
                    if layer == 1:
                        lap = (p[n] + p[s]) + (pe[k] + pw[k]) - 4.0 * p[k]
                        step = step + (TIME_STEP * DRAG[1]) * lap
                    b_all[layer, at(level, first + k, t), :] = step - q[k]

    row_blocks(1, total - 1, 2, advance_body)

    sweep(level, v_one, 0, ext, 0, b_all, 0, 1, total - 1, 2)

    @pl.when(is_first)
    def _():
        clear(v_one, level, 0, HALO)

    @pl.when(is_last)
    def _():
        clear(v_one, level, HALO + rows, total)

    sweep(level, v_ref, -2, v_one, 0, b_all, 0, 2, total - 2, 2)

    @pl.when(is_first)
    def _():
        clear(v_ref, level, 0, 2)

    @pl.when(is_last)
    def _():
        clear(v_ref, level, rows + 2, rows + 4)

    restrict(level, bc_ref, 0, coarse, v_ref, 2, b_all, HALO, 0, rows // 2, 1)
    send_edges(coarse, rows // 2, bc_ref, 0, bc_near_ref, bc_far_ref)
    b_ref[...] = b_all[:, 3 * level.size : (total - 3) * level.size, :]
    for layer in range(2):
        for group in range(rows // SUBS):
            for t in range(level.tiles):
                for s in range(SUBS):
                    first = (HALO + group * SUBS) * level.size + t * SUBS + s
                    column = (s * level.tiles + t) * LANES
                    next_ref[
                        layer, group * SUBS : (group + 1) * SUBS, column : column + LANES
                    ] = -b_all[layer, pl.ds(first, SUBS, stride=level.size), :]


def middle_kernel(
    level, coarse, rows, b_own, near_ref, far_ref, b_ref, v_ref, out_ref, v_one, bc
):
    _, _, is_first, is_last = place()
    total = rows + 2 * HALO
    join(level, rows, b_ref, b_own, near_ref, far_ref)
    start(level, v_one, 0, b_ref, 0, 0, total, 4)

    @pl.when(is_first)
    def _():
        clear(v_one, level, 0, HALO)

    @pl.when(is_last)
    def _():
        clear(v_one, level, HALO + rows, total)

    sweep(level, v_ref, 0, v_one, 0, b_ref, 0, 1, total - 1, 2)

    @pl.when(is_first)
    def _():
        clear(v_ref, level, 0, HALO)

    @pl.when(is_last)
    def _():
        clear(v_ref, level, HALO + rows, total)

    restrict(level, bc, 0, coarse, v_ref, HALO, b_ref, HALO, 0, rows // 2, 2)
    for copy in range(out_ref.shape[0]):
        out_ref[copy] = bc[...]


PAD = 4


def coarse_kernel(
    levels, rows, same_ref, other_ref, b1_ref, v1_ref, b0_ref, v0_ref, out_ref,
    b2, v2, w2, b3, v3, w3, b4, v4, w4, x1, y1, x0, y0,
):
    me, odd, is_first, is_last = place()
    fine, mid, two, three, four = levels
    own = rows // 4
    chips = same_ref.shape[0]
    n2, n3, n4 = 2 * chips * own, chips * own, chips * own // 2
    for ref, level, n in (
        (b2, two, n2), (v2, two, n2), (w2, two, n2), (b3, three, n3), (v3, three, n3),
        (w3, three, n3), (v4, four, n4), (w4, four, n4),
    ):
        clear(ref, level, 0, PAD)
        clear(ref, level, PAD + n, 2 * PAD + n)

    def gather_body(chip, carry):
        for ref, core in ((same_ref, odd), (other_ref, 1 - odd)):
            row = pl.multiple_of(((2 * chip + core) * own + PAD) * two.size, SUBS)
            b2[:, pl.ds(row, own * two.size), :] = ref[chip]
        return carry

    lax.fori_loop(0, chips, gather_body, 0, unroll=min(chips, 4))

    start(two, v2, PAD, b2, PAD, 0, n2, 8)
    sweep(two, w2, PAD, v2, PAD, b2, PAD, 0, n2, 8)
    restrict(two, b3, PAD, three, w2, PAD, b2, PAD, 0, n3, 4)
    start(three, v3, PAD, b3, PAD, 0, n3, 8)
    sweep(three, w3, PAD, v3, PAD, b3, PAD, 0, n3, 8)
    restrict(three, b4, 0, four, w3, PAD, b3, PAD, 0, n4, 4)
    start(four, v4, PAD, b4, 0, 0, n4, 8)
    src, dst = v4, w4
    for _ in range(COARSE_SWEEPS - 1):
        sweep(four, dst, PAD, src, PAD, b4, 0, 0, n4, 16)
        src, dst = dst, src

    def trim(ref, level, n):
        @pl.when(me < 2)
        def _():
            clear(ref, level, 0, PAD)

        @pl.when(me >= 2 * chips - 2)
        def _():
            clear(ref, level, PAD + n, 2 * PAD + n)

    half, quarter = own // 2, own // 4
    correct(three, four, v3, PAD, w3, PAD, src, PAD, me * quarter - 2, quarter + 4, 8)
    sweep(three, w3, PAD, v3, PAD, b3, PAD, me * half - 3, half + 6, 8)
    trim(w3, three, n3)
    sweep(three, v3, PAD, w3, PAD, b3, PAD, me * half - 2, half + 4, 8)
    trim(v3, three, n3)
    correct(two, three, v2, PAD, w2, PAD, v3, PAD, me * half - 2, half + 4, 8)
    sweep(two, w2, PAD, v2, PAD, b2, PAD, me * own - 3, own + 6, 8)
    trim(w2, two, n2)
    sweep(two, v2, PAD, w2, PAD, b2, PAD, me * own - 2, own + 4, 8)
    trim(v2, two, n2)

    n1 = rows // 2
    total = n1 + 2 * HALO

    def trim_own(ref, level, halo, n):
        @pl.when(is_first)
        def _():
            clear(ref, level, 0, halo)

        @pl.when(is_last)
        def _():
            clear(ref, level, halo + n, 2 * halo + n)

    correct(
        mid, two, x1, 0, v1_ref, 0, v2, PAD + me * own - HALO // 2, 0, total // 2, 2
    )
    sweep(mid, y1, 0, x1, 0, b1_ref, 0, 2, total - 2, 2)
    trim_own(y1, mid, HALO, n1)
    sweep(mid, x1, 0, y1, 0, b1_ref, 0, 3, total - 3, 2)
    trim_own(x1, mid, HALO, n1)

    correct(fine, mid, x0, 0, v0_ref, 0, x1, HALO - 1, 0, n1 + 2, 1)
    sweep(fine, y0, 0, x0, 0, b0_ref, -1, 1, rows + 3, 2)
    trim_own(y0, fine, 2, rows)
    sweep(fine, x0, 0, y0, 0, b0_ref, -1, 2, rows + 2, 2)
    to_native(out_ref, x0, fine, 2, rows)


def shape(*dims):
    return jax.ShapeDtypeStruct(dims, jnp.float32)


def scratch(layers, rows, level):
    return pltpu.VMEM((layers, rows * level.size, LANES), jnp.float32)


def call(kernel, out_shape, scratch_shapes=(), limit=48):
    return pl.pallas_call(
        kernel,
        out_shape=out_shape,
        scratch_shapes=list(scratch_shapes),
        compiler_params=pltpu.CompilerParams(vmem_limit_bytes=limit * 1024 * 1024),
    )


def shards(stream_now, vorticity):
    _, rows, columns = stream_now.shape
    count = lax.axis_size("wide")
    tiles = columns // (SUBS * LANES)
    fine, mid = Level(0, tiles, 1), Level(1, tiles // 2, 1)
    two, three, four = Level(2, tiles // 4, 1), Level(3, tiles // 4, 2), Level(4, tiles // 4, 4)
    core_swap = [(i, i ^ 1) for i in range(count)]
    chip_swap = [(i, ((i + 1) ^ 1) - 1) for i in range(1, count - 1)]
    chip_swap += [(0, count - 1), (count - 1, 0)]

    def exchange(near, far):
        return lax.ppermute(near, "wide", core_swap), lax.ppermute(far, "wide", chip_swap)

    x, near, far = call(
        functools.partial(pack_kernel, fine, rows),
        [shape(4, rows * fine.size, LANES)] + [shape(4, HALO * fine.size, LANES)] * 2,
    )(stream_now, vorticity)
    near, far = exchange(near, far)
    half = rows // 2
    total = rows + 2 * HALO
    vorticity_next, b0, v0, b1, near, far = call(
        functools.partial(fine_kernel, fine, mid, rows),
        [
            shape(2, rows, columns),
            shape(2, (rows + 2) * fine.size, LANES),
            shape(2, (rows + 4) * fine.size, LANES),
            shape(2, half * mid.size, LANES),
            shape(2, HALO * mid.size, LANES),
            shape(2, HALO * mid.size, LANES),
        ],
        [scratch(4, total, fine)] * 3 + [scratch(2, total, fine)] * 2,
    )(x, near, far)
    near, far = exchange(near, far)
    quarter = rows // 4
    chips = count // 2
    b1, v1, b2 = call(
        functools.partial(middle_kernel, mid, two, half),
        [
            shape(2, (half + 2 * HALO) * mid.size, LANES),
            shape(2, (half + 2 * HALO) * mid.size, LANES),
            shape(chips, 2, quarter * two.size, LANES),
        ],
        [scratch(2, half + 2 * HALO, mid), scratch(2, quarter, two)],
    )(b1, near, far)
    groups = [[i for i in range(count) if i % 2 == c] for c in range(2)]
    same = lax.all_to_all(b2, "wide", 0, 0, axis_index_groups=groups)
    other = lax.ppermute(same, "wide", core_swap)
    n2, n3, n4 = count * quarter, count * quarter // 2, count * quarter // 4
    stream_next = call(
        functools.partial(coarse_kernel, (fine, mid, two, three, four), rows),
        shape(2, rows, columns),
        [scratch(2, n2 + 2 * PAD, two)] * 3
        + [scratch(2, n3 + 2 * PAD, three)] * 3
        + [scratch(2, n4, four)]
        + [scratch(2, n4 + 2 * PAD, four)] * 2
        + [scratch(2, half + 2 * HALO, mid)] * 2
        + [scratch(2, rows + 4, fine)] * 2,
    )(same, other, b1, v1, b0, v0)
    return (vorticity_next, stream_next)


def solution(mesh):
    return jax.shard_map(
        shards,
        mesh=mesh,
        in_specs=(P("member", "wide", None), P("member", "wide", None)),
        out_specs=(P("member", "wide", None), P("member", "wide", None)),
        check_vma=False,
    )
```

```python
import functools

import jax
import jax.numpy as jnp
from jax import lax
from jax.experimental import pallas as pl
from jax.experimental.pallas import tpu as pltpu
from jax.sharding import PartitionSpec as P


LANES = 128
SUBS = 8
HALO = 3
MID_HALO = 4
RELAX = 0.8
COUPLING = (0.02, 0.04)
TIME_STEP = 0.5
BETA = 0.05
DRAG = (0.0, 0.02)
COARSE_SWEEPS = 8


class Level:
    def __init__(self, level, tiles, stride):
        h2 = (2.0**level) ** 2
        self.tiles, self.stride = tiles, stride
        diag = [4.0 / h2 + f for f in COUPLING]
        self.keep = 1.0 - RELAX
        self.near = [RELAX / (d * h2) for d in diag]
        self.other = [RELAX * f / d for f, d in zip(COUPLING, diag)]
        self.src = [RELAX / d for d in diag]
        self.diag = diag
        self.inv_h2 = 1.0 / h2
        self.size = tiles * SUBS


def lane_index():
    return lax.broadcasted_iota(jnp.int32, (SUBS, LANES), 1)


def at(level, row, tile=0):
    base = row * level.size
    if not isinstance(row, int):
        base = pl.multiple_of(base, SUBS)
    return pl.ds(base + tile * SUBS, SUBS)


def load(ref, level, layer, row):
    return [ref[layer, at(level, row, t), :] for t in range(level.tiles)]


def store(ref, level, layer, row, values):
    for t in range(level.tiles):
        ref[layer, at(level, row, t), :] = values[t]


def east(values, stride=1):
    rolled = [pltpu.roll(v, LANES - stride, 1) for v in values]
    after = rolled[1:] + [pltpu.roll(rolled[0], SUBS - 1, 0)]
    edge = lane_index() >= LANES - stride
    return [jnp.where(edge, a, r) for a, r in zip(after, rolled)]


def west(values, stride=1):
    rolled = [pltpu.roll(v, stride, 1) for v in values]
    before = [pltpu.roll(rolled[-1], 1, 0)] + rolled[:-1]
    edge = lane_index() < stride
    return [jnp.where(edge, b, r) for b, r in zip(before, rolled)]


def row_blocks(low, high, block, body):
    count = high - low if isinstance(low, int) else high
    whole = count // block
    if whole > 1:
        lax.fori_loop(0, whole, lambda i, c: (body(low + i * block, block), c)[1], 0)
    elif whole == 1:
        body(low, block)
    if count % block:
        body(low + whole * block, count % block)


def star(rows, k, layer, level):
    centre = rows[k][layer]
    e, w = east(centre, level.stride), west(centre, level.stride)
    return [
        (n + s) + (a + b)
        for n, s, a, b in zip(rows[k + 1][layer], rows[k - 1][layer], e, w)
    ]


def load_rows(ref, level, first, count, margin=1):
    return {
        k: [load(ref, level, layer, first + k) for layer in range(2)]
        for k in range(-margin, count + margin)
    }


def sweep_rows(level, rows, source, count):
    out = {}
    for k in range(count):
        out[k] = []
        for layer in range(2):
            near = star(rows, k, layer, level)
            out[k].append(
                [
                    (level.keep * c + level.near[layer] * n)
                    + (level.other[layer] * o + level.src[layer] * b)
                    for c, n, o, b in zip(
                        rows[k][layer], near, rows[k][1 - layer], source[k][layer]
                    )
                ]
            )
    return out


def residual_rows(level, rows, source, count):
    out = {}
    for k in range(count):
        out[k] = []
        for layer in range(2):
            near = star(rows, k, layer, level)
            out[k].append(
                [
                    (b - level.diag[layer] * c)
                    + (level.inv_h2 * n + COUPLING[layer] * o)
                    for c, n, o, b in zip(
                        rows[k][layer], near, rows[k][1 - layer], source[k][layer]
                    )
                ]
            )
    return out


def store_rows(ref, level, first, rows, count):
    for k in range(count):
        for layer in range(2):
            store(ref, level, layer, first + k, rows[k][layer])


def sweep(level, dst, dst_at, src, src_at, b, b_at, low, high, block):
    def body(first, count):
        rows = load_rows(src, level, first + src_at, count)
        source = load_rows(b, level, first + b_at, count, 0)
        store_rows(dst, level, first + dst_at, sweep_rows(level, rows, source, count), count)

    row_blocks(low, high, block, body)


def start(level, dst, dst_at, b, b_at, low, high, block):
    def body(first, count):
        source = load_rows(b, level, first + b_at, count, 0)
        out = {
            k: [[level.src[l] * x for x in source[k][l]] for l in range(2)]
            for k in range(count)
        }
        store_rows(dst, level, first + dst_at, out, count)

    row_blocks(low, high, block, body)


def pack_columns(values):
    lane = lane_index()
    pick = (2 * lane) % LANES
    sums = [v + pltpu.roll(v, LANES - 1, 1) for v in values]
    picked = [jnp.take_along_axis(s, pick, axis=1) for s in sums]
    return [
        jnp.where(lane < LANES // 2, picked[2 * t], picked[2 * t + 1])
        for t in range(len(values) // 2)
    ]


def spread_columns(values):
    lane = lane_index()
    out = []
    for v in values:
        out.append(jnp.take_along_axis(v, lane // 2, axis=1))
        out.append(jnp.take_along_axis(v, LANES // 2 + lane // 2, axis=1))
    return out


def merge_columns(values, stride):
    even = (lane_index() // stride) % 2 == 0
    return [
        v + jnp.where(even, pltpu.roll(v, LANES - stride, 1), pltpu.roll(v, stride, 1))
        for v in values
    ]


def restrict(fine, dst, dst_at, coarse, src, src_at, b, b_at, low, high, block):
    def body(first, count):
        rows = load_rows(src, fine, 2 * first + src_at, 2 * count)
        source = load_rows(b, fine, 2 * first + b_at, 2 * count, 0)
        res = residual_rows(fine, rows, source, 2 * count)
        out = {}
        for k in range(count):
            out[k] = []
            for layer in range(2):
                pair = [x + y for x, y in zip(res[2 * k][layer], res[2 * k + 1][layer])]
                if coarse.tiles < fine.tiles:
                    pair = pack_columns(pair)
                else:
                    pair = merge_columns(pair, fine.stride)
                out[k].append([0.25 * x for x in pair])
        store_rows(dst, coarse, first + dst_at, out, count)

    row_blocks(low, high, block, body)


def correct(fine, coarse, dst, dst_at, src, src_at, add, add_at, low, high, block):
    def body(first, count):
        coarse_rows = load_rows(add, coarse, first + add_at, count, 0)
        fine_rows = load_rows(src, fine, 2 * first + src_at, 2 * count, 0)
        out = {}
        for k in range(count):
            spread = [
                spread_columns(v) if coarse.tiles < fine.tiles else v for v in coarse_rows[k]
            ]
            for half in range(2):
                out[2 * k + half] = [
                    [x + y for x, y in zip(fine_rows[2 * k + half][l], spread[l])]
                    for l in range(2)
                ]
        store_rows(dst, fine, 2 * first + dst_at, out, 2 * count)

    row_blocks(low, high, block, body)


def clear(ref, level, low, high):
    ref[:, low * level.size : high * level.size, :] = jnp.zeros(
        (ref.shape[0], (high - low) * level.size, LANES), jnp.float32
    )


def place():
    me, count = lax.axis_index("wide"), lax.axis_size("wide")
    return me, lax.rem(me, 2), me == 0, me == count - 1


def pack_kernel(level, rows, p_ref, q_ref, ext_ref, near_ref, far_ref, native, sems):
    copies = []
    for field, ref in enumerate((p_ref, q_ref)):
        for layer in range(2):
            which = 2 * field + layer
            copies.append(
                pltpu.make_async_copy(ref.at[layer], native.at[which], sems.at[which])
            )
            copies[-1].start()
    for which in range(4):
        copies[which].wait()
        for group in range(rows // SUBS):
            for t in range(level.tiles):
                for s in range(SUBS):
                    first = (HALO + group * SUBS) * level.size + t * SUBS + s
                    column = (s * level.tiles + t) * LANES
                    ext_ref[which, pl.ds(first, SUBS, stride=level.size), :] = native[
                        which, group * SUBS : (group + 1) * SUBS, column : column + LANES
                    ]
    send_edges(level, HALO, HALO, rows, ext_ref, near_ref, far_ref)


def send_edges(level, width, src_at, rows, src, near_ref, far_ref):
    _, odd, _, _ = place()
    size = width * level.size
    last = (src_at + rows - width) * level.size
    top = src_at * level.size
    near = pl.multiple_of(jnp.where(odd == 1, top, last), SUBS)
    far = pl.multiple_of(jnp.where(odd == 1, last, top), SUBS)
    near_ref[:, 0:size, :] = src[:, pl.ds(near, size), :]
    far_ref[:, 0:size, :] = src[:, pl.ds(far, size), :]


def receive_edges(level, width, dst_at, rows, dst, near_ref, far_ref):
    _, odd, first, last = place()
    size = width * level.size
    low = (dst_at + rows) * level.size
    top = (dst_at - width) * level.size
    near = pl.multiple_of(jnp.where(odd == 1, top, low), SUBS)
    far = pl.multiple_of(jnp.where(odd == 1, low, top), SUBS)
    dst[:, pl.ds(near, size), :] = near_ref[:, 0:size, :]
    outside = jnp.logical_or(first, last)
    dst[:, pl.ds(far, size), :] = jnp.where(outside, 0.0, far_ref[:, 0:size, :])


def shift_rows(level, ext, e_ref, w_ref, low, high, block):
    def body(first, count):
        for k in range(count):
            for f in range(4):
                v = load(ext, level, f, first + k)
                store(e_ref, level, f, first + k, east(v))
                store(w_ref, level, f, first + k, west(v))

    row_blocks(low, high, block, body)


def advance_rows(level, b_ref, ext, e_ref, w_ref, low, high, block):
    def body(first, count):
        for layer in range(2):
            for t in range(level.tiles):
                def grab(ref, field):
                    return {
                        k: ref[2 * field + layer, at(level, first + k, t), :]
                        for k in range(-1, count + 1)
                    }

                p, pe, pw = grab(ext, 0), grab(e_ref, 0), grab(w_ref, 0)
                q, qe, qw = grab(ext, 1), grab(e_ref, 1), grab(w_ref, 1)
                zonal = {k: pe[k] - pw[k] for k in p}
                for k in range(count):
                    n, s = k + 1, k - 1
                    v0, ve, vw = p[n] - p[s], pe[n] - pe[s], pw[n] - pw[s]
                    jac = q[n] * (zonal[k] + zonal[n]) - q[s] * (zonal[k] + zonal[s])
                    jac = jac - qe[k] * (v0 + ve) + qw[k] * (v0 + vw)
                    jac = jac + qe[n] * (pe[k] - p[n]) - qe[s] * (pe[k] - p[s])
                    jac = jac - qw[n] * (pw[k] - p[n]) + qw[s] * (pw[k] - p[s])
                    step = (TIME_STEP / 12.0) * jac + (0.5 * TIME_STEP * BETA) * zonal[k]
                    if layer == 1:
                        lap = (p[n] + p[s]) + (pe[k] + pw[k]) - 4.0 * p[k]
                        step = step + (TIME_STEP * DRAG[1]) * lap
                    b_ref[layer, at(level, first + k, t), :] = step - q[k]

    row_blocks(low, high, block, body)


def inner_kernel(level, coarse, rows, ext, e_ref, w_ref, b_ref, v_one, v_two, bc_ref):
    low, high = HALO, HALO + rows
    shift_rows(level, ext, e_ref, w_ref, low, high, 4)
    advance_rows(level, b_ref, ext, e_ref, w_ref, low + 1, high - 1, 2)
    sweep(level, v_one, 0, ext, 0, b_ref, 0, low + 2, high - 2, 4)
    sweep(level, v_two, 0, v_one, 0, b_ref, 0, low + 3, high - 3, 4)
    restrict(level, bc_ref, 0, coarse, v_two, HALO, b_ref, HALO, 2, rows // 2 - 2, 2)


def outer_kernel(level, coarse, rows, *refs):
    near_ref, far_ref = refs[7:9]
    ext, e_ref, w_ref, b_ref, v_one, v_two, bc_ref, bc_near_ref, bc_far_ref = refs[9:]
    _, _, is_first, is_last = place()
    low, high = HALO, HALO + rows
    total = rows + 2 * HALO
    receive_edges(level, HALO, HALO, rows, ext, near_ref, far_ref)
    shift_rows(level, ext, e_ref, w_ref, 0, low, 3)
    shift_rows(level, ext, e_ref, w_ref, high, total, 3)
    advance_rows(level, b_ref, ext, e_ref, w_ref, 1, low + 1, 3)
    advance_rows(level, b_ref, ext, e_ref, w_ref, high - 1, total - 1, 3)
    sweep(level, v_one, 0, ext, 0, b_ref, 0, 1, low + 2, 4)
    sweep(level, v_one, 0, ext, 0, b_ref, 0, high - 2, total - 1, 4)

    def trim(ref):
        @pl.when(is_first)
        def _():
            clear(ref, level, 0, HALO)

        @pl.when(is_last)
        def _():
            clear(ref, level, high, total)

    trim(v_one)
    sweep(level, v_two, 0, v_one, 0, b_ref, 0, 2, low + 3, 4)
    sweep(level, v_two, 0, v_one, 0, b_ref, 0, high - 3, total - 2, 4)
    trim(v_two)
    half = rows // 2
    restrict(level, bc_ref, 0, coarse, v_two, HALO, b_ref, HALO, 0, 2, 2)
    restrict(level, bc_ref, 0, coarse, v_two, HALO, b_ref, HALO, half - 2, half, 2)
    send_edges(coarse, MID_HALO, 0, half, bc_ref, bc_near_ref, bc_far_ref)
    _, odd, _, _ = place()
    first = MID_HALO * coarse.size
    top, last = (low + 1) * level.size, (high - 2) * level.size
    near = pl.multiple_of(jnp.where(odd == 1, top, last), SUBS)
    far = pl.multiple_of(jnp.where(odd == 1, last, top), SUBS)
    bc_near_ref[:, first : first + level.size, :] = v_two[:, pl.ds(near, level.size), :]
    bc_far_ref[:, first : first + level.size, :] = v_two[:, pl.ds(far, level.size), :]


def emit_kernel(level, rows, b_ref, next_ref, native, sems):
    copies = []
    for layer in range(2):
        for group in range(rows // SUBS):
            rows_of = pl.ds(group * SUBS, SUBS)
            for t in range(level.tiles):
                for s in range(SUBS):
                    first = (HALO + group * SUBS) * level.size + t * SUBS + s
                    column = (s * level.tiles + t) * LANES
                    native[layer, rows_of, column : column + LANES] = -b_ref[
                        layer, pl.ds(first, SUBS, stride=level.size), :
                    ]
            copies.append(
                pltpu.make_async_copy(
                    native.at[layer, rows_of], next_ref.at[layer, rows_of],
                    sems.at[layer, group],
                )
            )
            copies[-1].start()
    for copy in copies:
        copy.wait()


def middle_kernel(
    fine, level, coarse, rows, b_own, near_ref, far_ref, v0_in,
    b_ref, v_ref, out_ref, v0_ref, v_one, bc,
):
    _, odd, is_first, is_last = place()
    total = rows + 2 * MID_HALO
    edge = MID_HALO * level.size
    b_ref[:, edge : edge + rows * level.size, :] = b_own[...]
    receive_edges(level, MID_HALO, MID_HALO, rows, b_ref, near_ref, far_ref)
    start(level, v_one, 0, b_ref, 0, 0, total, 4)

    def trim(ref):
        @pl.when(is_first)
        def _():
            clear(ref, level, 0, MID_HALO)

        @pl.when(is_last)
        def _():
            clear(ref, level, MID_HALO + rows, total)

    trim(v_one)
    sweep(level, v_ref, 0, v_one, 0, b_ref, 0, 1, total - 1, 7)
    trim(v_ref)
    restrict(level, bc, 0, coarse, v_ref, MID_HALO, b_ref, MID_HALO, 0, rows // 2, 4)
    for copy in range(out_ref.shape[0]):
        out_ref[copy] = bc[...]
    top, low = (HALO - 2) * fine.size, (HALO + 2 * rows + 1) * fine.size
    near = pl.multiple_of(jnp.where(odd == 1, top, low), SUBS)
    far = pl.multiple_of(jnp.where(odd == 1, low, top), SUBS)
    v0_ref[:, pl.ds(near, fine.size), :] = near_ref[:, edge : edge + fine.size, :]
    outside = jnp.logical_or(is_first, is_last)
    v0_ref[:, pl.ds(far, fine.size), :] = jnp.where(
        outside, 0.0, far_ref[:, edge : edge + fine.size, :]
    )


PAD = 4


def coarse_kernel(
    levels, rows, same_ref, other_ref, b1_ref, v1_ref, b0_ref, v0_ref, out_ref,
    b2, v2, w2, b3, v3, w3, b4, v4, w4, x1, y1, x0, y0, native, sems,
):
    me, odd, is_first, is_last = place()
    fine, mid, two, three, four = levels
    own = rows // 4
    chips = same_ref.shape[0]
    n2, n3, n4 = 2 * chips * own, chips * own, chips * own // 2
    for ref, level, n in (
        (b2, two, n2), (v2, two, n2), (w2, two, n2), (b3, three, n3), (v3, three, n3),
        (w3, three, n3), (v4, four, n4), (w4, four, n4),
    ):
        clear(ref, level, 0, PAD)
        clear(ref, level, PAD + n, 2 * PAD + n)

    def gather_body(chip, carry):
        for ref, core in ((same_ref, odd), (other_ref, 1 - odd)):
            row = pl.multiple_of(((2 * chip + core) * own + PAD) * two.size, SUBS)
            b2[:, pl.ds(row, own * two.size), :] = ref[chip]
        return carry

    lax.fori_loop(0, chips, gather_body, 0, unroll=min(chips, 4))

    start(two, v2, PAD, b2, PAD, 0, n2, 8)
    sweep(two, w2, PAD, v2, PAD, b2, PAD, 0, n2, 8)
    restrict(two, b3, PAD, three, w2, PAD, b2, PAD, 0, n3, 4)
    start(three, v3, PAD, b3, PAD, 0, n3, 8)
    sweep(three, w3, PAD, v3, PAD, b3, PAD, 0, n3, 8)
    restrict(three, b4, 0, four, w3, PAD, b3, PAD, 0, n4, 4)
    start(four, v4, PAD, b4, 0, 0, n4, 8)
    src, dst = v4, w4
    for _ in range(COARSE_SWEEPS - 1):
        sweep(four, dst, PAD, src, PAD, b4, 0, 0, n4, 16)
        src, dst = dst, src

    def trim(ref, level, n):
        @pl.when(me < 2)
        def _():
            clear(ref, level, 0, PAD)

        @pl.when(me >= 2 * chips - 2)
        def _():
            clear(ref, level, PAD + n, 2 * PAD + n)

    half, quarter = own // 2, own // 4
    correct(three, four, v3, PAD, w3, PAD, src, PAD, me * quarter - 2, quarter + 4, 8)
    sweep(three, w3, PAD, v3, PAD, b3, PAD, me * half - 3, half + 6, 8)
    trim(w3, three, n3)
    sweep(three, v3, PAD, w3, PAD, b3, PAD, me * half - 2, half + 4, 8)
    trim(v3, three, n3)
    correct(two, three, v2, PAD, w2, PAD, v3, PAD, me * half - 2, half + 4, 8)
    sweep(two, w2, PAD, v2, PAD, b2, PAD, me * own - 3, own + 6, 8)
    trim(w2, two, n2)
    sweep(two, v2, PAD, w2, PAD, b2, PAD, me * own - 2, own + 4, 8)
    trim(v2, two, n2)

    n1 = rows // 2
    total = n1 + 2 * MID_HALO

    def trim_own(ref, level, halo, n):
        @pl.when(is_first)
        def _():
            clear(ref, level, 0, halo)

        @pl.when(is_last)
        def _():
            clear(ref, level, halo + n, 2 * halo + n)

    correct(
        mid, two, x1, 0, v1_ref, 0, v2, PAD + me * own - MID_HALO // 2, 0, total // 2, 4
    )
    sweep(mid, y1, 0, x1, 0, b1_ref, 0, 2, total - 2, 6)
    trim_own(y1, mid, MID_HALO, n1)
    sweep(mid, x1, 0, y1, 0, b1_ref, 0, 3, total - 3, 5)
    trim_own(x1, mid, MID_HALO, n1)

    low, high = HALO, HALO + rows
    correct(fine, mid, x0, HALO - 2, v0_ref, HALO - 2, x1, MID_HALO - 1, 0, n1 + 2, 2)
    sweep(fine, y0, 0, x0, 0, b0_ref, 0, low - 1, high + 1, 4)
    trim_own(y0, fine, HALO, rows)
    copies = []
    for group in range(rows // SUBS):
        first_row = low + group * SUBS
        rows_of = pl.ds(group * SUBS, SUBS)
        sweep(fine, x0, 0, y0, 0, b0_ref, 0, first_row, first_row + SUBS, 4)
        for layer in range(2):
            for t in range(fine.tiles):
                for s in range(SUBS):
                    first = first_row * fine.size + t * SUBS + s
                    column = (s * fine.tiles + t) * LANES
                    native[layer, rows_of, column : column + LANES] = x0[
                        layer, pl.ds(first, SUBS, stride=fine.size), :
                    ]
            copies.append(
                pltpu.make_async_copy(
                    native.at[layer, rows_of], out_ref.at[layer, rows_of],
                    sems.at[layer, group],
                )
            )
            copies[-1].start()
    for copy in copies:
        copy.wait()


def shape(*dims):
    return jax.ShapeDtypeStruct(dims, jnp.float32)


def scratch(layers, rows, level):
    return pltpu.VMEM((layers, rows * level.size, LANES), jnp.float32)


HBM = pl.BlockSpec(memory_space=pltpu.HBM)
VMEM = pl.BlockSpec(memory_space=pltpu.VMEM)


def call(kernel, out_shape, scratch_shapes=(), cost=None, limit=24, **options):
    if cost is not None:
        cost = pl.CostEstimate(flops=cost, bytes_accessed=cost // 8, transcendentals=0)
    return pl.pallas_call(
        kernel,
        out_shape=out_shape,
        scratch_shapes=list(scratch_shapes),
        cost_estimate=cost,
        compiler_params=pltpu.CompilerParams(vmem_limit_bytes=limit * 1024 * 1024),
        **options,
    )


def shards(stream_now, vorticity):
    _, rows, columns = stream_now.shape
    count = lax.axis_size("wide")
    tiles = columns // (SUBS * LANES)
    fine, mid = Level(0, tiles, 1), Level(1, tiles // 2, 1)
    two, three, four = Level(2, tiles // 4, 1), Level(3, tiles // 4, 2), Level(4, tiles // 4, 4)
    core_swap = [(i, i ^ 1) for i in range(count)]
    chip_swap = [(i, ((i + 1) ^ 1) - 1) for i in range(1, count - 1)]
    chip_swap += [(0, count - 1), (count - 1, 0)]
    groups = rows // SUBS

    def exchange(near, far):
        return lax.ppermute(near, "wide", core_swap), lax.ppermute(far, "wide", chip_swap)

    half, quarter = rows // 2, rows // 4
    total = rows + 2 * HALO
    ext, near, far = call(
        functools.partial(pack_kernel, fine, rows),
        [shape(4, total * fine.size, LANES)] + [shape(4, HALO * fine.size, LANES)] * 2,
        [pltpu.VMEM((4, rows, columns), jnp.float32), pltpu.SemaphoreType.DMA((4,))],
        in_specs=[HBM, HBM],
    )(stream_now, vorticity)
    near, far = exchange(near, far)
    state = [
        shape(4, total * fine.size, LANES),
        shape(4, total * fine.size, LANES),
        shape(2, total * fine.size, LANES),
        shape(2, total * fine.size, LANES),
        shape(2, total * fine.size, LANES),
        shape(2, half * mid.size, LANES),
    ]
    inner = call(
        functools.partial(inner_kernel, fine, mid, rows),
        state,
        cost=8000000,
    )(ext)
    edge = shape(2, MID_HALO * mid.size + fine.size, LANES)
    outer = call(
        functools.partial(outer_kernel, fine, mid, rows),
        [shape(4, total * fine.size, LANES)] + state + [edge, edge],
        input_output_aliases={i: i for i in range(7)},
    )(ext, *inner, near, far)
    b0, v0, b1, near, far = outer[3], outer[5], outer[6], outer[7], outer[8]
    near, far = exchange(near, far)
    vorticity_next = call(
        functools.partial(emit_kernel, fine, rows),
        shape(2, rows, columns),
        [pltpu.VMEM((2, rows, columns), jnp.float32), pltpu.SemaphoreType.DMA((2, groups))],
        cost=4000000,
        out_specs=HBM,
    )(b0)
    chips = count // 2
    b1, v1, b2, v0 = call(
        functools.partial(middle_kernel, fine, mid, two, half),
        [
            shape(2, (half + 2 * MID_HALO) * mid.size, LANES),
            shape(2, (half + 2 * MID_HALO) * mid.size, LANES),
            shape(chips, 2, quarter * two.size, LANES),
            shape(2, total * fine.size, LANES),
        ],
        [scratch(2, half + 2 * MID_HALO, mid), scratch(2, quarter, two)],
        input_output_aliases={3: 3},
    )(b1, near, far, v0)
    cores = [[i for i in range(count) if i % 2 == c] for c in range(2)]
    same = lax.all_to_all(b2, "wide", 0, 0, axis_index_groups=cores)
    other = lax.ppermute(same, "wide", core_swap)
    n2, n3, n4 = count * quarter, count * quarter // 2, count * quarter // 4
    stream_next = call(
        functools.partial(coarse_kernel, (fine, mid, two, three, four), rows),
        shape(2, rows, columns),
        [scratch(2, n2 + 2 * PAD, two)] * 3
        + [scratch(2, n3 + 2 * PAD, three)] * 3
        + [scratch(2, n4, four)]
        + [scratch(2, n4 + 2 * PAD, four)] * 2
        + [scratch(2, half + 2 * MID_HALO, mid)] * 2
        + [scratch(2, total, fine)] * 2
        + [pltpu.VMEM((2, rows, columns), jnp.float32), pltpu.SemaphoreType.DMA((2, groups))],
        limit=40,
        out_specs=HBM,
    )(same, other, b1, v1, b0, v0)
    return (vorticity_next, stream_next)


def solution(mesh):
    return jax.shard_map(
        shards,
        mesh=mesh,
        in_specs=(P("member", "wide", None), P("member", "wide", None)),
        out_specs=(P("member", "wide", None), P("member", "wide", None)),
        check_vma=False,
    )
```

```python
import functools

import jax
import jax.numpy as jnp
from jax import lax
from jax.experimental import pallas as pl
from jax.experimental.pallas import tpu as pltpu
from jax.sharding import PartitionSpec as P


LANES = 128
SUBS = 8
HALO = 3
MID_HALO = 6
TWO_HALO = 4
RELAX = 0.8
COUPLING = (0.02, 0.04)
TIME_STEP = 0.5
BETA = 0.05
DRAG = (0.0, 0.02)
COARSE_SWEEPS = 8


class Level:
    def __init__(self, level, tiles, stride):
        h2 = (2.0**level) ** 2
        self.tiles, self.stride = tiles, stride
        diag = [4.0 / h2 + f for f in COUPLING]
        self.keep = 1.0 - RELAX
        self.near = [RELAX / (d * h2) for d in diag]
        self.other = [RELAX * f / d for f, d in zip(COUPLING, diag)]
        self.src = [RELAX / d for d in diag]
        self.diag = diag
        self.inv_h2 = 1.0 / h2
        self.size = tiles * SUBS


def lane_index():
    return lax.broadcasted_iota(jnp.int32, (SUBS, LANES), 1)


def at(level, row, tile=0):
    base = row * level.size
    if not isinstance(row, int):
        base = pl.multiple_of(base, SUBS)
    return pl.ds(base + tile * SUBS, SUBS)


def load(ref, level, layer, row):
    return [ref[layer, at(level, row, t), :] for t in range(level.tiles)]


def store(ref, level, layer, row, values):
    for t in range(level.tiles):
        ref[layer, at(level, row, t), :] = values[t]


def east(values, stride=1):
    rolled = [pltpu.roll(v, LANES - stride, 1) for v in values]
    after = rolled[1:] + [pltpu.roll(rolled[0], SUBS - 1, 0)]
    edge = lane_index() >= LANES - stride
    return [jnp.where(edge, a, r) for a, r in zip(after, rolled)]


def west(values, stride=1):
    rolled = [pltpu.roll(v, stride, 1) for v in values]
    before = [pltpu.roll(rolled[-1], 1, 0)] + rolled[:-1]
    edge = lane_index() < stride
    return [jnp.where(edge, b, r) for b, r in zip(before, rolled)]


def row_blocks(low, high, block, body):
    count = high - low if isinstance(low, int) else high
    whole = count // block
    if whole > 1:
        lax.fori_loop(0, whole, lambda i, c: (body(low + i * block, block), c)[1], 0)
    elif whole == 1:
        body(low, block)
    if count % block:
        body(low + whole * block, count % block)


def star(rows, k, layer, level):
    centre = rows[k][layer]
    e, w = east(centre, level.stride), west(centre, level.stride)
    return [
        (n + s) + (a + b)
        for n, s, a, b in zip(rows[k + 1][layer], rows[k - 1][layer], e, w)
    ]


def load_rows(ref, level, first, count, margin=1):
    return {
        k: [load(ref, level, layer, first + k) for layer in range(2)]
        for k in range(-margin, count + margin)
    }


def sweep_rows(level, rows, source, count):
    out = {}
    for k in range(count):
        out[k] = []
        for layer in range(2):
            near = star(rows, k, layer, level)
            out[k].append(
                [
                    (level.keep * c + level.near[layer] * n)
                    + (level.other[layer] * o + level.src[layer] * b)
                    for c, n, o, b in zip(
                        rows[k][layer], near, rows[k][1 - layer], source[k][layer]
                    )
                ]
            )
    return out


def residual_rows(level, rows, source, count):
    out = {}
    for k in range(count):
        out[k] = []
        for layer in range(2):
            near = star(rows, k, layer, level)
            out[k].append(
                [
                    (b - level.diag[layer] * c)
                    + (level.inv_h2 * n + COUPLING[layer] * o)
                    for c, n, o, b in zip(
                        rows[k][layer], near, rows[k][1 - layer], source[k][layer]
                    )
                ]
            )
    return out


def store_rows(ref, level, first, rows, count):
    for k in range(count):
        for layer in range(2):
            store(ref, level, layer, first + k, rows[k][layer])


def sweep(level, dst, dst_at, src, src_at, b, b_at, low, high, block):
    def body(first, count):
        rows = load_rows(src, level, first + src_at, count)
        source = load_rows(b, level, first + b_at, count, 0)
        store_rows(dst, level, first + dst_at, sweep_rows(level, rows, source, count), count)

    row_blocks(low, high, block, body)


def start(level, dst, dst_at, b, b_at, low, high, block):
    def body(first, count):
        source = load_rows(b, level, first + b_at, count, 0)
        out = {
            k: [[level.src[l] * x for x in source[k][l]] for l in range(2)]
            for k in range(count)
        }
        store_rows(dst, level, first + dst_at, out, count)

    row_blocks(low, high, block, body)


def pack_columns(values):
    lane = lane_index()
    pick = (2 * lane) % LANES
    sums = [v + pltpu.roll(v, LANES - 1, 1) for v in values]
    picked = [jnp.take_along_axis(s, pick, axis=1) for s in sums]
    return [
        jnp.where(lane < LANES // 2, picked[2 * t], picked[2 * t + 1])
        for t in range(len(values) // 2)
    ]


def spread_columns(values):
    lane = lane_index()
    out = []
    for v in values:
        out.append(jnp.take_along_axis(v, lane // 2, axis=1))
        out.append(jnp.take_along_axis(v, LANES // 2 + lane // 2, axis=1))
    return out


def merge_columns(values, stride):
    even = (lane_index() // stride) % 2 == 0
    return [
        v + jnp.where(even, pltpu.roll(v, LANES - stride, 1), pltpu.roll(v, stride, 1))
        for v in values
    ]


def restrict(fine, dst, dst_at, coarse, src, src_at, b, b_at, low, high, block):
    def body(first, count):
        rows = load_rows(src, fine, 2 * first + src_at, 2 * count)
        source = load_rows(b, fine, 2 * first + b_at, 2 * count, 0)
        res = residual_rows(fine, rows, source, 2 * count)
        out = {}
        for k in range(count):
            out[k] = []
            for layer in range(2):
                pair = [x + y for x, y in zip(res[2 * k][layer], res[2 * k + 1][layer])]
                if coarse.tiles < fine.tiles:
                    pair = pack_columns(pair)
                else:
                    pair = merge_columns(pair, fine.stride)
                out[k].append([0.25 * x for x in pair])
        store_rows(dst, coarse, first + dst_at, out, count)

    row_blocks(low, high, block, body)


def correct(fine, coarse, dst, dst_at, src, src_at, add, add_at, low, high, block):
    def body(first, count):
        coarse_rows = load_rows(add, coarse, first + add_at, count, 0)
        fine_rows = load_rows(src, fine, 2 * first + src_at, 2 * count, 0)
        out = {}
        for k in range(count):
            spread = [
                spread_columns(v) if coarse.tiles < fine.tiles else v for v in coarse_rows[k]
            ]
            for half in range(2):
                out[2 * k + half] = [
                    [x + y for x, y in zip(fine_rows[2 * k + half][l], spread[l])]
                    for l in range(2)
                ]
        store_rows(dst, fine, 2 * first + dst_at, out, 2 * count)

    row_blocks(low, high, block, body)


def clear(ref, level, low, high):
    ref[:, low * level.size : high * level.size, :] = jnp.zeros(
        (ref.shape[0], (high - low) * level.size, LANES), jnp.float32
    )


def place():
    me, count = lax.axis_index("wide"), lax.axis_size("wide")
    return me, lax.rem(me, 2), me == 0, me == count - 1


def pack_kernel(level, rows, p_ref, q_ref, ext_ref, near_ref, far_ref, native, sems):
    copies = []
    for field, ref in enumerate((p_ref, q_ref)):
        for layer in range(2):
            which = 2 * field + layer
            copies.append(
                pltpu.make_async_copy(ref.at[layer], native.at[which], sems.at[which])
            )
            copies[-1].start()
    for which in range(4):
        copies[which].wait()
        for group in range(rows // SUBS):
            for t in range(level.tiles):
                for s in range(SUBS):
                    first = (HALO + group * SUBS) * level.size + t * SUBS + s
                    column = (s * level.tiles + t) * LANES
                    ext_ref[which, pl.ds(first, SUBS, stride=level.size), :] = native[
                        which, group * SUBS : (group + 1) * SUBS, column : column + LANES
                    ]
    send_edges(level, HALO, HALO, rows, ext_ref, near_ref, far_ref)


def send_edges(level, width, src_at, rows, src, near_ref, far_ref):
    _, odd, _, _ = place()
    size = width * level.size
    last = (src_at + rows - width) * level.size
    top = src_at * level.size
    near = pl.multiple_of(jnp.where(odd == 1, top, last), SUBS)
    far = pl.multiple_of(jnp.where(odd == 1, last, top), SUBS)
    near_ref[:, 0:size, :] = src[:, pl.ds(near, size), :]
    far_ref[:, 0:size, :] = src[:, pl.ds(far, size), :]


def receive_edges(level, width, dst_at, rows, dst, near_ref, far_ref):
    _, odd, first, last = place()
    size = width * level.size
    low = (dst_at + rows) * level.size
    top = (dst_at - width) * level.size
    near = pl.multiple_of(jnp.where(odd == 1, top, low), SUBS)
    far = pl.multiple_of(jnp.where(odd == 1, low, top), SUBS)
    dst[:, pl.ds(near, size), :] = near_ref[:, 0:size, :]
    outside = jnp.logical_or(first, last)
    dst[:, pl.ds(far, size), :] = jnp.where(outside, 0.0, far_ref[:, 0:size, :])


def shift_rows(level, ext, e_ref, w_ref, low, high, block):
    def body(first, count):
        for k in range(count):
            for f in range(4):
                v = load(ext, level, f, first + k)
                store(e_ref, level, f, first + k, east(v))
                store(w_ref, level, f, first + k, west(v))

    row_blocks(low, high, block, body)


def advance_rows(level, b_ref, ext, e_ref, w_ref, low, high, block):
    def body(first, count):
        for layer in range(2):
            for t in range(level.tiles):
                def grab(ref, field):
                    return {
                        k: ref[2 * field + layer, at(level, first + k, t), :]
                        for k in range(-1, count + 1)
                    }

                p, pe, pw = grab(ext, 0), grab(e_ref, 0), grab(w_ref, 0)
                q, qe, qw = grab(ext, 1), grab(e_ref, 1), grab(w_ref, 1)
                zonal = {k: pe[k] - pw[k] for k in p}
                for k in range(count):
                    n, s = k + 1, k - 1
                    v0, ve, vw = p[n] - p[s], pe[n] - pe[s], pw[n] - pw[s]
                    jac = q[n] * (zonal[k] + zonal[n]) - q[s] * (zonal[k] + zonal[s])
                    jac = jac - qe[k] * (v0 + ve) + qw[k] * (v0 + vw)
                    jac = jac + qe[n] * (pe[k] - p[n]) - qe[s] * (pe[k] - p[s])
                    jac = jac - qw[n] * (pw[k] - p[n]) + qw[s] * (pw[k] - p[s])
                    step = (TIME_STEP / 12.0) * jac + (0.5 * TIME_STEP * BETA) * zonal[k]
                    if layer == 1:
                        lap = (p[n] + p[s]) + (pe[k] + pw[k]) - 4.0 * p[k]
                        step = step + (TIME_STEP * DRAG[1]) * lap
                    b_ref[layer, at(level, first + k, t), :] = step - q[k]

    row_blocks(low, high, block, body)


def inner_kernel(level, coarse, rows, ext, e_ref, w_ref, b_ref, v_one, v_two, bc_ref):
    low, high = HALO, HALO + rows
    shift_rows(level, ext, e_ref, w_ref, low, high, 4)
    advance_rows(level, b_ref, ext, e_ref, w_ref, low + 1, high - 1, 2)
    sweep(level, v_one, 0, ext, 0, b_ref, 0, low + 2, high - 2, 4)
    sweep(level, v_two, 0, v_one, 0, b_ref, 0, low + 3, high - 3, 4)
    restrict(level, bc_ref, 0, coarse, v_two, HALO, b_ref, HALO, 2, rows // 2 - 2, 2)


def outer_kernel(level, coarse, rows, *refs):
    near_ref, far_ref = refs[7:9]
    ext, e_ref, w_ref, b_ref, v_one, v_two, bc_ref, bc_near_ref, bc_far_ref = refs[9:]
    _, _, is_first, is_last = place()
    low, high = HALO, HALO + rows
    total = rows + 2 * HALO
    receive_edges(level, HALO, HALO, rows, ext, near_ref, far_ref)
    shift_rows(level, ext, e_ref, w_ref, 0, low, 3)
    shift_rows(level, ext, e_ref, w_ref, high, total, 3)
    advance_rows(level, b_ref, ext, e_ref, w_ref, 1, low + 1, 3)
    advance_rows(level, b_ref, ext, e_ref, w_ref, high - 1, total - 1, 3)
    sweep(level, v_one, 0, ext, 0, b_ref, 0, 1, low + 2, 4)
    sweep(level, v_one, 0, ext, 0, b_ref, 0, high - 2, total - 1, 4)

    def trim(ref):
        @pl.when(is_first)
        def _():
            clear(ref, level, 0, HALO)

        @pl.when(is_last)
        def _():
            clear(ref, level, high, total)

    trim(v_one)
    sweep(level, v_two, 0, v_one, 0, b_ref, 0, 2, low + 3, 4)
    sweep(level, v_two, 0, v_one, 0, b_ref, 0, high - 3, total - 2, 4)
    trim(v_two)
    half = rows // 2
    restrict(level, bc_ref, 0, coarse, v_two, HALO, b_ref, HALO, 0, 2, 2)
    restrict(level, bc_ref, 0, coarse, v_two, HALO, b_ref, HALO, half - 2, half, 2)
    send_edges(coarse, MID_HALO, 0, half, bc_ref, bc_near_ref, bc_far_ref)
    _, odd, _, _ = place()
    first = MID_HALO * coarse.size
    top, last = (low + 1) * level.size, (high - 2) * level.size
    near = pl.multiple_of(jnp.where(odd == 1, top, last), SUBS)
    far = pl.multiple_of(jnp.where(odd == 1, last, top), SUBS)
    bc_near_ref[:, first : first + level.size, :] = v_two[:, pl.ds(near, level.size), :]
    bc_far_ref[:, first : first + level.size, :] = v_two[:, pl.ds(far, level.size), :]


def emit_kernel(level, rows, b_ref, next_ref, native, sems):
    copies = []
    for layer in range(2):
        for group in range(rows // SUBS):
            rows_of = pl.ds(group * SUBS, SUBS)
            for t in range(level.tiles):
                for s in range(SUBS):
                    first = (HALO + group * SUBS) * level.size + t * SUBS + s
                    column = (s * level.tiles + t) * LANES
                    native[layer, rows_of, column : column + LANES] = -b_ref[
                        layer, pl.ds(first, SUBS, stride=level.size), :
                    ]
            copies.append(
                pltpu.make_async_copy(
                    native.at[layer, rows_of], next_ref.at[layer, rows_of],
                    sems.at[layer, group],
                )
            )
            copies[-1].start()
    for copy in copies:
        copy.wait()


def middle_kernel(
    fine, level, two, three, rows, b_own, near_ref, far_ref, v0_in,
    b_ref, v_ref, b2_ref, v2_ref, out_ref, two_near_ref, two_far_ref, v0_ref,
    v_one, w_two, b3,
):
    _, odd, is_first, is_last = place()
    total = rows + 2 * MID_HALO
    own = rows // 2
    edge = MID_HALO * level.size
    b_ref[:, edge : edge + rows * level.size, :] = b_own[...]
    receive_edges(level, MID_HALO, MID_HALO, rows, b_ref, near_ref, far_ref)
    start(level, v_one, 0, b_ref, 0, 0, total, 4)

    def trim(ref, of, halo, n):
        @pl.when(is_first)
        def _():
            clear(ref, of, 0, halo)

        @pl.when(is_last)
        def _():
            clear(ref, of, halo + n, 2 * halo + n)

    trim(v_one, level, MID_HALO, rows)
    sweep(level, v_ref, 0, v_one, 0, b_ref, 0, 1, total - 1, 6)
    trim(v_ref, level, MID_HALO, rows)
    restrict(
        level, b2_ref, TWO_HALO, two, v_ref, MID_HALO, b_ref, MID_HALO, -2, own + 2, 4
    )
    start(two, w_two, TWO_HALO, b2_ref, TWO_HALO, -2, own + 2, 8)
    trim(w_two, two, TWO_HALO, own)
    sweep(two, v2_ref, TWO_HALO, w_two, TWO_HALO, b2_ref, TWO_HALO, -1, own + 1, 6)
    trim(v2_ref, two, TWO_HALO, own)
    restrict(
        two, b3, 0, three, v2_ref, TWO_HALO, b2_ref, TWO_HALO, 0, own // 2, 2
    )
    even = lane_index() % 2 == 0
    for layer in range(2):
        for pair in range(own // 4):
            row = jnp.where(
                even,
                b3[layer, at(three, 2 * pair), :],
                b3[layer, at(three, 2 * pair + 1), :],
            )
            for copy in range(out_ref.shape[0]):
                out_ref[copy, layer, at(three, pair), :] = row
    up, down = pl.ds((TWO_HALO + 1) * two.size, 3 * two.size), pl.ds(
        own * two.size, 3 * two.size
    )
    up_b, down_b = at(two, TWO_HALO + 2), at(two, TWO_HALO + own - 3)
    last = pl.ds(3 * two.size, two.size)

    def send(ref, rows_v, row_b):
        ref[:, 0 : 3 * two.size, :] = v2_ref[:, rows_v, :]
        ref[:, last, :] = b2_ref[:, row_b, :]

    @pl.when(odd == 1)
    def _():
        send(two_near_ref, up, up_b)
        send(two_far_ref, down, down_b)

    @pl.when(odd == 0)
    def _():
        send(two_near_ref, down, down_b)
        send(two_far_ref, up, up_b)

    top, low = (HALO - 2) * fine.size, (HALO + 2 * rows + 1) * fine.size
    near = pl.multiple_of(jnp.where(odd == 1, top, low), SUBS)
    far = pl.multiple_of(jnp.where(odd == 1, low, top), SUBS)
    v0_ref[:, pl.ds(near, fine.size), :] = near_ref[:, edge : edge + fine.size, :]
    outside = jnp.logical_or(is_first, is_last)
    v0_ref[:, pl.ds(far, fine.size), :] = jnp.where(
        outside, 0.0, far_ref[:, edge : edge + fine.size, :]
    )


PAD = 4


def coarse_kernel(
    levels, rows, same_ref, other_ref, near_ref, far_ref,
    b2_ref, v2_ref, b1_ref, v1_ref, b0_ref, v0_ref, out_ref,
    b2, v2, x2, y2, b3, v3, w3, b4, v4, w4, x1, y1, x0, y0, native, sems,
):
    me, odd, is_first, is_last = place()
    fine, mid, two, three, four = levels
    own = rows // 4
    chips = same_ref.shape[0]
    n3, n4 = chips * own, chips * own // 2
    for ref, level, n in ((b3, three, n3), (v3, three, n3), (w3, three, n3), (v4, four, n4), (w4, four, n4)):
        clear(ref, level, 0, PAD)
        clear(ref, level, PAD + n, 2 * PAD + n)
    even = lane_index() % 2 == 0

    def gather_body(chip, carry):
        for ref, core in ((same_ref, odd), (other_ref, 1 - odd)):
            row = (2 * chip + core) * (own // 2) + PAD
            for layer in range(2):
                for pair in range(own // 4):
                    both = ref[chip, layer, at(three, pair), :]
                    first = jnp.where(even, both, pltpu.roll(both, 1, 1))
                    second = jnp.where(even, pltpu.roll(both, LANES - 1, 1), both)
                    b3[layer, at(three, row + 2 * pair), :] = first
                    b3[layer, at(three, row + 2 * pair + 1), :] = second
        return carry

    lax.fori_loop(0, chips, gather_body, 0, unroll=min(chips, 8))

    b2[...] = b2_ref[...]
    v2[...] = v2_ref[...]

    def take(ref, zero):
        top_v, low_v = pl.ds(0, 3 * two.size), pl.ds((TWO_HALO + own + 1) * two.size, 3 * two.size)
        top_b, low_b = at(two, TWO_HALO - 3), at(two, TWO_HALO + own + 2)
        last = pl.ds(3 * two.size, two.size)

        def put(rows_v, row_b):
            values = ref[:, 0 : 3 * two.size, :]
            v2[:, rows_v, :] = jnp.where(zero, 0.0, values) if zero is not None else values
            b2[:, row_b, :] = ref[:, last, :]

        return lambda: put(top_v, top_b), lambda: put(low_v, low_b)

    near_top, near_low = take(near_ref, None)
    far_top, far_low = take(far_ref, jnp.logical_or(is_first, is_last))

    @pl.when(odd == 1)
    def _():
        near_top()
        far_low()

    @pl.when(odd == 0)
    def _():
        near_low()
        far_top()

    start(three, v3, PAD, b3, PAD, 0, n3, 8)
    sweep(three, w3, PAD, v3, PAD, b3, PAD, 0, n3, 16)
    restrict(three, b4, 0, four, w3, PAD, b3, PAD, 0, n4, 8)
    start(four, v4, PAD, b4, 0, 0, n4, 16)
    src, dst = v4, w4
    for _ in range(COARSE_SWEEPS - 1):
        sweep(four, dst, PAD, src, PAD, b4, 0, 0, n4, 16)
        src, dst = dst, src

    def trim(ref, level, n):
        @pl.when(me < 2)
        def _():
            clear(ref, level, 0, PAD)

        @pl.when(me >= 2 * chips - 2)
        def _():
            clear(ref, level, PAD + n, 2 * PAD + n)

    half, quarter = own // 2, own // 4
    correct(three, four, v3, PAD, w3, PAD, src, PAD, me * quarter - 2, quarter + 4, 8)
    sweep(three, w3, PAD, v3, PAD, b3, PAD, me * half - 3, half + 6, 8)
    trim(w3, three, n3)
    sweep(three, v3, PAD, w3, PAD, b3, PAD, me * half - 2, half + 4, 8)
    trim(v3, three, n3)

    def trim_own(ref, level, halo, n):
        @pl.when(is_first)
        def _():
            clear(ref, level, 0, halo)

        @pl.when(is_last)
        def _():
            clear(ref, level, halo + n, 2 * halo + n)

    total = own + 2 * TWO_HALO
    correct(two, three, x2, 0, v2, 0, v3, PAD + me * half - TWO_HALO // 2, 0, total // 2, 8)
    sweep(two, y2, 0, x2, 0, b2, 0, 1, total - 1, 10)
    trim_own(y2, two, TWO_HALO, own)
    sweep(two, x2, 0, y2, 0, b2, 0, 2, total - 2, 8)
    trim_own(x2, two, TWO_HALO, own)

    n1 = rows // 2
    total = n1 + 2 * MID_HALO

    correct(
        mid, two, x1, MID_HALO - 4, v1_ref, MID_HALO - 4, x2, TWO_HALO - 2, 0, n1 // 2 + 4, 4
    )
    sweep(mid, y1, 0, x1, 0, b1_ref, 0, MID_HALO - 2, MID_HALO + n1 + 2, 6)
    trim_own(y1, mid, MID_HALO, n1)
    sweep(mid, x1, 0, y1, 0, b1_ref, 0, MID_HALO - 1, MID_HALO + n1 + 1, 5)
    trim_own(x1, mid, MID_HALO, n1)

    low, high = HALO, HALO + rows
    correct(fine, mid, x0, HALO - 2, v0_ref, HALO - 2, x1, MID_HALO - 1, 0, n1 + 2, 2)
    sweep(fine, y0, 0, x0, 0, b0_ref, 0, low - 1, high + 1, 4)
    trim_own(y0, fine, HALO, rows)
    copies = []
    for group in range(rows // SUBS):
        first_row = low + group * SUBS
        rows_of = pl.ds(group * SUBS, SUBS)
        sweep(fine, x0, 0, y0, 0, b0_ref, 0, first_row, first_row + SUBS, 4)
        for layer in range(2):
            for t in range(fine.tiles):
                for s in range(SUBS):
                    first = first_row * fine.size + t * SUBS + s
                    column = (s * fine.tiles + t) * LANES
                    native[layer, rows_of, column : column + LANES] = x0[
                        layer, pl.ds(first, SUBS, stride=fine.size), :
                    ]
            copies.append(
                pltpu.make_async_copy(
                    native.at[layer, rows_of], out_ref.at[layer, rows_of],
                    sems.at[layer, group],
                )
            )
            copies[-1].start()
    for copy in copies:
        copy.wait()


def shape(*dims):
    return jax.ShapeDtypeStruct(dims, jnp.float32)


def scratch(layers, rows, level):
    return pltpu.VMEM((layers, rows * level.size, LANES), jnp.float32)


HBM = pl.BlockSpec(memory_space=pltpu.HBM)
VMEM = pl.BlockSpec(memory_space=pltpu.VMEM)


def call(kernel, out_shape, scratch_shapes=(), cost=None, limit=24, **options):
    if cost is not None:
        cost = pl.CostEstimate(flops=cost, bytes_accessed=cost // 8, transcendentals=0)
    return pl.pallas_call(
        kernel,
        out_shape=out_shape,
        scratch_shapes=list(scratch_shapes),
        cost_estimate=cost,
        compiler_params=pltpu.CompilerParams(vmem_limit_bytes=limit * 1024 * 1024),
        **options,
    )


def shards(stream_now, vorticity):
    _, rows, columns = stream_now.shape
    count = lax.axis_size("wide")
    tiles = columns // (SUBS * LANES)
    fine, mid = Level(0, tiles, 1), Level(1, tiles // 2, 1)
    two, three, four = Level(2, tiles // 4, 1), Level(3, tiles // 4, 2), Level(4, tiles // 4, 4)
    core_swap = [(i, i ^ 1) for i in range(count)]
    chip_swap = [(i, ((i + 1) ^ 1) - 1) for i in range(1, count - 1)]
    chip_swap += [(0, count - 1), (count - 1, 0)]
    groups = rows // SUBS

    def exchange(near, far):
        return lax.ppermute(near, "wide", core_swap), lax.ppermute(far, "wide", chip_swap)

    half, quarter = rows // 2, rows // 4
    total = rows + 2 * HALO
    ext, near, far = call(
        functools.partial(pack_kernel, fine, rows),
        [shape(4, total * fine.size, LANES)] + [shape(4, HALO * fine.size, LANES)] * 2,
        [pltpu.VMEM((4, rows, columns), jnp.float32), pltpu.SemaphoreType.DMA((4,))],
        in_specs=[HBM, HBM],
    )(stream_now, vorticity)
    near, far = exchange(near, far)
    state = [
        shape(4, total * fine.size, LANES),
        shape(4, total * fine.size, LANES),
        shape(2, total * fine.size, LANES),
        shape(2, total * fine.size, LANES),
        shape(2, total * fine.size, LANES),
        shape(2, half * mid.size, LANES),
    ]
    inner = call(
        functools.partial(inner_kernel, fine, mid, rows),
        state,
        cost=8000000,
    )(ext)
    edge = shape(2, MID_HALO * mid.size + fine.size, LANES)
    outer = call(
        functools.partial(outer_kernel, fine, mid, rows),
        [shape(4, total * fine.size, LANES)] + state + [edge, edge],
        input_output_aliases={i: i for i in range(7)},
    )(ext, *inner, near, far)
    b0, v0, b1, near, far = outer[3], outer[5], outer[6], outer[7], outer[8]
    near, far = exchange(near, far)
    vorticity_next = call(
        functools.partial(emit_kernel, fine, rows),
        shape(2, rows, columns),
        [pltpu.VMEM((2, rows, columns), jnp.float32), pltpu.SemaphoreType.DMA((2, groups))],
        cost=4000000,
        out_specs=HBM,
    )(b0)
    chips = count // 2
    eighth = rows // 8
    two_edge = shape(2, 4 * two.size, LANES)
    two_all = shape(2, (quarter + 2 * TWO_HALO) * two.size, LANES)
    b1, v1, b2, v2, b3, near, far, v0 = call(
        functools.partial(middle_kernel, fine, mid, two, three, half),
        [
            shape(2, (half + 2 * MID_HALO) * mid.size, LANES),
            shape(2, (half + 2 * MID_HALO) * mid.size, LANES),
            two_all,
            two_all,
            shape(chips, 2, eighth // 2 * three.size, LANES),
            two_edge,
            two_edge,
            shape(2, total * fine.size, LANES),
        ],
        [
            scratch(2, half + 2 * MID_HALO, mid),
            scratch(2, quarter + 2 * TWO_HALO, two),
            scratch(2, eighth, three),
        ],
        input_output_aliases={3: 7},
    )(b1, near, far, v0)
    near = lax.ppermute(near, "wide", core_swap)
    far = lax.ppermute(far, "wide", chip_swap)
    cores = [[i for i in range(count) if i % 2 == c] for c in range(2)]
    same = lax.all_to_all(b3, "wide", 0, 0, axis_index_groups=cores)
    other = lax.ppermute(same, "wide", core_swap)
    n3, n4 = count * eighth, count * eighth // 2
    stream_next = call(
        functools.partial(coarse_kernel, (fine, mid, two, three, four), rows),
        shape(2, rows, columns),
        [scratch(2, quarter + 2 * TWO_HALO, two)] * 4
        + [scratch(2, n3 + 2 * PAD, three)] * 3
        + [scratch(2, n4, four)]
        + [scratch(2, n4 + 2 * PAD, four)] * 2
        + [scratch(2, half + 2 * MID_HALO, mid)] * 2
        + [scratch(2, total, fine)] * 2
        + [pltpu.VMEM((2, rows, columns), jnp.float32), pltpu.SemaphoreType.DMA((2, groups))],
        out_specs=HBM,
    )(same, other, near, far, b2, v2, b1, v1, b0, v0)
    return (vorticity_next, stream_next)


def solution(mesh):
    return jax.shard_map(
        shards,
        mesh=mesh,
        in_specs=(P("member", "wide", None), P("member", "wide", None)),
        out_specs=(P("member", "wide", None), P("member", "wide", None)),
        check_vma=False,
    )
```

```python
import functools

import jax
import jax.numpy as jnp
from jax import lax
from jax.experimental import pallas as pl
from jax.experimental.pallas import tpu as pltpu
from jax.sharding import PartitionSpec as P


LANES = 128
SUBS = 8
HALO = 3
MID_HALO = 6
TWO_HALO = 4
RELAX = 0.8
COUPLING = (0.02, 0.04)
TIME_STEP = 0.5
BETA = 0.05
DRAG = (0.0, 0.02)
COARSE_SWEEPS = 8


class Level:
    def __init__(self, level, tiles, stride):
        h2 = (2.0**level) ** 2
        self.tiles, self.stride = tiles, stride
        diag = [4.0 / h2 + f for f in COUPLING]
        self.keep = 1.0 - RELAX
        self.near = [RELAX / (d * h2) for d in diag]
        self.other = [RELAX * f / d for f, d in zip(COUPLING, diag)]
        self.src = [RELAX / d for d in diag]
        self.diag = diag
        self.inv_h2 = 1.0 / h2
        self.size = tiles * SUBS


def lane_index():
    return lax.broadcasted_iota(jnp.int32, (SUBS, LANES), 1)


def at(level, row, tile=0):
    base = row * level.size
    if not isinstance(row, int):
        base = pl.multiple_of(base, SUBS)
    return pl.ds(base + tile * SUBS, SUBS)


def load(ref, level, layer, row):
    return [ref[layer, at(level, row, t), :] for t in range(level.tiles)]


def store(ref, level, layer, row, values):
    for t in range(level.tiles):
        ref[layer, at(level, row, t), :] = values[t]


def east(values, stride=1):
    rolled = [pltpu.roll(v, LANES - stride, 1) for v in values]
    after = rolled[1:] + [pltpu.roll(rolled[0], SUBS - 1, 0)]
    edge = lane_index() >= LANES - stride
    return [jnp.where(edge, a, r) for a, r in zip(after, rolled)]


def west(values, stride=1):
    rolled = [pltpu.roll(v, stride, 1) for v in values]
    before = [pltpu.roll(rolled[-1], 1, 0)] + rolled[:-1]
    edge = lane_index() < stride
    return [jnp.where(edge, b, r) for b, r in zip(before, rolled)]


def row_blocks(low, high, block, body):
    count = high - low if isinstance(low, int) else high
    whole = count // block
    if whole > 1:
        lax.fori_loop(0, whole, lambda i, c: (body(low + i * block, block), c)[1], 0)
    elif whole == 1:
        body(low, block)
    if count % block:
        body(low + whole * block, count % block)


def star(rows, k, layer, level):
    centre = rows[k][layer]
    e, w = east(centre, level.stride), west(centre, level.stride)
    return [
        (n + s) + (a + b)
        for n, s, a, b in zip(rows[k + 1][layer], rows[k - 1][layer], e, w)
    ]


def load_rows(ref, level, first, count, margin=1):
    return {
        k: [load(ref, level, layer, first + k) for layer in range(2)]
        for k in range(-margin, count + margin)
    }


def sweep_rows(level, rows, source, count):
    out = {}
    for k in range(count):
        out[k] = []
        for layer in range(2):
            near = star(rows, k, layer, level)
            out[k].append(
                [
                    (level.keep * c + level.near[layer] * n)
                    + (level.other[layer] * o + level.src[layer] * b)
                    for c, n, o, b in zip(
                        rows[k][layer], near, rows[k][1 - layer], source[k][layer]
                    )
                ]
            )
    return out


def residual_rows(level, rows, source, count):
    out = {}
    for k in range(count):
        out[k] = []
        for layer in range(2):
            near = star(rows, k, layer, level)
            out[k].append(
                [
                    (b - level.diag[layer] * c)
                    + (level.inv_h2 * n + COUPLING[layer] * o)
                    for c, n, o, b in zip(
                        rows[k][layer], near, rows[k][1 - layer], source[k][layer]
                    )
                ]
            )
    return out


def store_rows(ref, level, first, rows, count):
    for k in range(count):
        for layer in range(2):
            store(ref, level, layer, first + k, rows[k][layer])


def sweep(level, dst, dst_at, src, src_at, b, b_at, low, high, block):
    def body(first, count):
        rows = load_rows(src, level, first + src_at, count)
        source = load_rows(b, level, first + b_at, count, 0)
        store_rows(dst, level, first + dst_at, sweep_rows(level, rows, source, count), count)

    row_blocks(low, high, block, body)


def start(level, dst, dst_at, b, b_at, low, high, block):
    def body(first, count):
        source = load_rows(b, level, first + b_at, count, 0)
        out = {
            k: [[level.src[l] * x for x in source[k][l]] for l in range(2)]
            for k in range(count)
        }
        store_rows(dst, level, first + dst_at, out, count)

    row_blocks(low, high, block, body)


def pack_columns(values):
    lane = lane_index()
    pick = (2 * lane) % LANES
    sums = [v + pltpu.roll(v, LANES - 1, 1) for v in values]
    picked = [jnp.take_along_axis(s, pick, axis=1) for s in sums]
    return [
        jnp.where(lane < LANES // 2, picked[2 * t], picked[2 * t + 1])
        for t in range(len(values) // 2)
    ]


def spread_columns(values):
    lane = lane_index()
    out = []
    for v in values:
        out.append(jnp.take_along_axis(v, lane // 2, axis=1))
        out.append(jnp.take_along_axis(v, LANES // 2 + lane // 2, axis=1))
    return out


def merge_columns(values, stride):
    even = (lane_index() // stride) % 2 == 0
    return [
        v + jnp.where(even, pltpu.roll(v, LANES - stride, 1), pltpu.roll(v, stride, 1))
        for v in values
    ]


def restrict(fine, dst, dst_at, coarse, src, src_at, b, b_at, low, high, block):
    def body(first, count):
        rows = load_rows(src, fine, 2 * first + src_at, 2 * count)
        source = load_rows(b, fine, 2 * first + b_at, 2 * count, 0)
        res = residual_rows(fine, rows, source, 2 * count)
        out = {}
        for k in range(count):
            out[k] = []
            for layer in range(2):
                pair = [x + y for x, y in zip(res[2 * k][layer], res[2 * k + 1][layer])]
                if coarse.tiles < fine.tiles:
                    pair = pack_columns(pair)
                else:
                    pair = merge_columns(pair, fine.stride)
                out[k].append([0.25 * x for x in pair])
        store_rows(dst, coarse, first + dst_at, out, count)

    row_blocks(low, high, block, body)


def correct(fine, coarse, dst, dst_at, src, src_at, add, add_at, low, high, block):
    def body(first, count):
        coarse_rows = load_rows(add, coarse, first + add_at, count, 0)
        fine_rows = load_rows(src, fine, 2 * first + src_at, 2 * count, 0)
        out = {}
        for k in range(count):
            spread = [
                spread_columns(v) if coarse.tiles < fine.tiles else v for v in coarse_rows[k]
            ]
            for half in range(2):
                out[2 * k + half] = [
                    [x + y for x, y in zip(fine_rows[2 * k + half][l], spread[l])]
                    for l in range(2)
                ]
        store_rows(dst, fine, 2 * first + dst_at, out, 2 * count)

    row_blocks(low, high, block, body)


def clear(ref, level, low, high):
    ref[:, low * level.size : high * level.size, :] = jnp.zeros(
        (ref.shape[0], (high - low) * level.size, LANES), jnp.float32
    )


def place():
    me, count = lax.axis_index("wide"), lax.axis_size("wide")
    return me, lax.rem(me, 2), me == 0, me == count - 1


def pack_kernel(level, rows, p_ref, q_ref, ext_ref, near_ref, far_ref, native, sems):
    copies = []
    for field, ref in enumerate((p_ref, q_ref)):
        for layer in range(2):
            which = 2 * field + layer
            copies.append(
                pltpu.make_async_copy(ref.at[layer], native.at[which], sems.at[which])
            )
            copies[-1].start()
    for which in range(4):
        copies[which].wait()
        for group in range(rows // SUBS):
            for t in range(level.tiles):
                for s in range(SUBS):
                    first = (HALO + group * SUBS) * level.size + t * SUBS + s
                    column = (s * level.tiles + t) * LANES
                    ext_ref[which, pl.ds(first, SUBS, stride=level.size), :] = native[
                        which, group * SUBS : (group + 1) * SUBS, column : column + LANES
                    ]
    send_edges(level, HALO, HALO, rows, ext_ref, near_ref, far_ref)


def send_edges(level, width, src_at, rows, src, near_ref, far_ref):
    _, odd, _, _ = place()
    size = width * level.size
    last = (src_at + rows - width) * level.size
    top = src_at * level.size
    near = pl.multiple_of(jnp.where(odd == 1, top, last), SUBS)
    far = pl.multiple_of(jnp.where(odd == 1, last, top), SUBS)
    near_ref[:, 0:size, :] = src[:, pl.ds(near, size), :]
    far_ref[:, 0:size, :] = src[:, pl.ds(far, size), :]


def receive_edges(level, width, dst_at, rows, dst, near_ref, far_ref):
    _, odd, first, last = place()
    size = width * level.size
    low = (dst_at + rows) * level.size
    top = (dst_at - width) * level.size
    near = pl.multiple_of(jnp.where(odd == 1, top, low), SUBS)
    far = pl.multiple_of(jnp.where(odd == 1, low, top), SUBS)
    dst[:, pl.ds(near, size), :] = near_ref[:, 0:size, :]
    outside = jnp.logical_or(first, last)
    dst[:, pl.ds(far, size), :] = jnp.where(outside, 0.0, far_ref[:, 0:size, :])


def shift_rows(level, ext, e_ref, w_ref, low, high, block):
    def body(first, count):
        for k in range(count):
            for f in range(4):
                v = load(ext, level, f, first + k)
                store(e_ref, level, f, first + k, east(v))
                store(w_ref, level, f, first + k, west(v))

    row_blocks(low, high, block, body)


def advance_rows(level, b_ref, ext, e_ref, w_ref, low, high, block):
    def body(first, count):
        for layer in range(2):
            for t in range(level.tiles):
                def grab(ref, field):
                    return {
                        k: ref[2 * field + layer, at(level, first + k, t), :]
                        for k in range(-1, count + 1)
                    }

                p, pe, pw = grab(ext, 0), grab(e_ref, 0), grab(w_ref, 0)
                q, qe, qw = grab(ext, 1), grab(e_ref, 1), grab(w_ref, 1)
                zonal = {k: pe[k] - pw[k] for k in p}
                for k in range(count):
                    n, s = k + 1, k - 1
                    v0, ve, vw = p[n] - p[s], pe[n] - pe[s], pw[n] - pw[s]
                    jac = q[n] * (zonal[k] + zonal[n]) - q[s] * (zonal[k] + zonal[s])
                    jac = jac - qe[k] * (v0 + ve) + qw[k] * (v0 + vw)
                    jac = jac + qe[n] * (pe[k] - p[n]) - qe[s] * (pe[k] - p[s])
                    jac = jac - qw[n] * (pw[k] - p[n]) + qw[s] * (pw[k] - p[s])
                    step = (TIME_STEP / 12.0) * jac + (0.5 * TIME_STEP * BETA) * zonal[k]
                    if layer == 1:
                        lap = (p[n] + p[s]) + (pe[k] + pw[k]) - 4.0 * p[k]
                        step = step + (TIME_STEP * DRAG[1]) * lap
                    b_ref[layer, at(level, first + k, t), :] = step - q[k]

    row_blocks(low, high, block, body)


def inner_kernel(level, coarse, rows, ext, e_ref, w_ref, b_ref, v_one, v_two, bc_ref):
    low, high = HALO, HALO + rows
    shift_rows(level, ext, e_ref, w_ref, low, high, 4)
    advance_rows(level, b_ref, ext, e_ref, w_ref, low + 1, high - 1, 2)
    sweep(level, v_one, 0, ext, 0, b_ref, 0, low + 2, high - 2, 4)
    sweep(level, v_two, 0, v_one, 0, b_ref, 0, low + 3, high - 3, 4)
    restrict(level, bc_ref, 0, coarse, v_two, HALO, b_ref, HALO, 2, rows // 2 - 2, 2)


def outer_kernel(level, coarse, rows, *refs):
    near_ref, far_ref = refs[7:9]
    ext, e_ref, w_ref, b_ref, v_one, v_two, bc_ref, bc_near_ref, bc_far_ref = refs[9:]
    _, _, is_first, is_last = place()
    low, high = HALO, HALO + rows
    total = rows + 2 * HALO
    receive_edges(level, HALO, HALO, rows, ext, near_ref, far_ref)
    shift_rows(level, ext, e_ref, w_ref, 0, low, 3)
    shift_rows(level, ext, e_ref, w_ref, high, total, 3)
    advance_rows(level, b_ref, ext, e_ref, w_ref, 1, low + 1, 3)
    advance_rows(level, b_ref, ext, e_ref, w_ref, high - 1, total - 1, 3)
    sweep(level, v_one, 0, ext, 0, b_ref, 0, 1, low + 2, 4)
    sweep(level, v_one, 0, ext, 0, b_ref, 0, high - 2, total - 1, 4)

    def trim(ref):
        @pl.when(is_first)
        def _():
            clear(ref, level, 0, HALO)

        @pl.when(is_last)
        def _():
            clear(ref, level, high, total)

    trim(v_one)
    sweep(level, v_two, 0, v_one, 0, b_ref, 0, 2, low + 3, 4)
    sweep(level, v_two, 0, v_one, 0, b_ref, 0, high - 3, total - 2, 4)
    trim(v_two)
    half = rows // 2
    restrict(level, bc_ref, 0, coarse, v_two, HALO, b_ref, HALO, 0, 2, 2)
    restrict(level, bc_ref, 0, coarse, v_two, HALO, b_ref, HALO, half - 2, half, 2)
    send_edges(coarse, MID_HALO, 0, half, bc_ref, bc_near_ref, bc_far_ref)
    _, odd, _, _ = place()
    first = MID_HALO * coarse.size
    top, last = (low + 1) * level.size, (high - 2) * level.size
    near = pl.multiple_of(jnp.where(odd == 1, top, last), SUBS)
    far = pl.multiple_of(jnp.where(odd == 1, last, top), SUBS)
    bc_near_ref[:, first : first + level.size, :] = v_two[:, pl.ds(near, level.size), :]
    bc_far_ref[:, first : first + level.size, :] = v_two[:, pl.ds(far, level.size), :]


def emit_kernel(level, rows, b_ref, next_ref, native, sems):
    copies = []
    for layer in range(2):
        for group in range(rows // SUBS):
            rows_of = pl.ds(group * SUBS, SUBS)
            for t in range(level.tiles):
                for s in range(SUBS):
                    first = (HALO + group * SUBS) * level.size + t * SUBS + s
                    column = (s * level.tiles + t) * LANES
                    native[layer, rows_of, column : column + LANES] = -b_ref[
                        layer, pl.ds(first, SUBS, stride=level.size), :
                    ]
            copies.append(
                pltpu.make_async_copy(
                    native.at[layer, rows_of], next_ref.at[layer, rows_of],
                    sems.at[layer, group],
                )
            )
            copies[-1].start()
    for copy in copies:
        copy.wait()


def middle_kernel(
    fine, level, two, three, rows, b_own, near_ref, far_ref, v0_in,
    b_ref, v_ref, b2_ref, v2_ref, out_ref, two_near_ref, two_far_ref, v0_ref,
    v_one, w_two, b3,
):
    _, odd, is_first, is_last = place()
    total = rows + 2 * MID_HALO
    own = rows // 2
    edge = MID_HALO * level.size
    b_ref[:, edge : edge + rows * level.size, :] = b_own[...]
    receive_edges(level, MID_HALO, MID_HALO, rows, b_ref, near_ref, far_ref)
    start(level, v_one, 0, b_ref, 0, 0, total, 4)

    def trim(ref, of, halo, n):
        @pl.when(is_first)
        def _():
            clear(ref, of, 0, halo)

        @pl.when(is_last)
        def _():
            clear(ref, of, halo + n, 2 * halo + n)

    trim(v_one, level, MID_HALO, rows)
    sweep(level, v_ref, 0, v_one, 0, b_ref, 0, 1, total - 1, 6)
    trim(v_ref, level, MID_HALO, rows)
    restrict(
        level, b2_ref, TWO_HALO, two, v_ref, MID_HALO, b_ref, MID_HALO, -2, own + 2, 4
    )
    start(two, w_two, TWO_HALO, b2_ref, TWO_HALO, -2, own + 2, 8)
    trim(w_two, two, TWO_HALO, own)
    sweep(two, v2_ref, TWO_HALO, w_two, TWO_HALO, b2_ref, TWO_HALO, -1, own + 1, 6)
    trim(v2_ref, two, TWO_HALO, own)
    restrict(
        two, b3, 0, three, v2_ref, TWO_HALO, b2_ref, TWO_HALO, 0, own // 2, 2
    )
    even = lane_index() % 2 == 0
    for layer in range(2):
        for pair in range(own // 4):
            row = jnp.where(
                even,
                b3[layer, at(three, 2 * pair), :],
                b3[layer, at(three, 2 * pair + 1), :],
            )
            for copy in range(out_ref.shape[0]):
                out_ref[copy, layer, at(three, pair), :] = row
    up, down = pl.ds((TWO_HALO + 1) * two.size, 3 * two.size), pl.ds(
        own * two.size, 3 * two.size
    )
    up_b, down_b = at(two, TWO_HALO + 2), at(two, TWO_HALO + own - 3)
    last = pl.ds(3 * two.size, two.size)

    def send(ref, rows_v, row_b):
        ref[:, 0 : 3 * two.size, :] = v2_ref[:, rows_v, :]
        ref[:, last, :] = b2_ref[:, row_b, :]

    @pl.when(odd == 1)
    def _():
        send(two_near_ref, up, up_b)
        send(two_far_ref, down, down_b)

    @pl.when(odd == 0)
    def _():
        send(two_near_ref, down, down_b)
        send(two_far_ref, up, up_b)

    top, low = (HALO - 2) * fine.size, (HALO + 2 * rows + 1) * fine.size
    near = pl.multiple_of(jnp.where(odd == 1, top, low), SUBS)
    far = pl.multiple_of(jnp.where(odd == 1, low, top), SUBS)
    v0_ref[:, pl.ds(near, fine.size), :] = near_ref[:, edge : edge + fine.size, :]
    outside = jnp.logical_or(is_first, is_last)
    v0_ref[:, pl.ds(far, fine.size), :] = jnp.where(
        outside, 0.0, far_ref[:, edge : edge + fine.size, :]
    )


PAD = 4


def coarse_kernel(
    levels, rows, same_ref, other_ref, near_ref, far_ref,
    b2_ref, v2_ref, b1_ref, v1_ref, b0_ref, v0_ref, out_ref,
    b2, v2, x2, y2, b3, v3, w3, b4, v4, w4, x1, y1, x0, y0, native, sems,
):
    me, odd, is_first, is_last = place()
    fine, mid, two, three, four = levels
    own = rows // 4
    chips = same_ref.shape[0]
    n3, n4 = chips * own, chips * own // 2
    for ref, level, n in ((b3, three, n3), (v3, three, n3), (w3, three, n3), (v4, four, n4), (w4, four, n4)):
        clear(ref, level, 0, PAD)
        clear(ref, level, PAD + n, 2 * PAD + n)
    even = lane_index() % 2 == 0

    def gather_body(chip, carry):
        for ref, core in ((same_ref, odd), (other_ref, 1 - odd)):
            row = (2 * chip + core) * (own // 2) + PAD
            for layer in range(2):
                for pair in range(own // 4):
                    both = ref[chip, layer, at(three, pair), :]
                    first = jnp.where(even, both, pltpu.roll(both, 1, 1))
                    second = jnp.where(even, pltpu.roll(both, LANES - 1, 1), both)
                    b3[layer, at(three, row + 2 * pair), :] = first
                    b3[layer, at(three, row + 2 * pair + 1), :] = second
        return carry

    lax.fori_loop(0, chips, gather_body, 0, unroll=min(chips, 8))

    b2[...] = b2_ref[...]
    v2[...] = v2_ref[...]

    def take(ref, zero):
        top_v, low_v = pl.ds(0, 3 * two.size), pl.ds((TWO_HALO + own + 1) * two.size, 3 * two.size)
        top_b, low_b = at(two, TWO_HALO - 3), at(two, TWO_HALO + own + 2)
        last = pl.ds(3 * two.size, two.size)

        def put(rows_v, row_b):
            values = ref[:, 0 : 3 * two.size, :]
            v2[:, rows_v, :] = jnp.where(zero, 0.0, values) if zero is not None else values
            b2[:, row_b, :] = ref[:, last, :]

        return lambda: put(top_v, top_b), lambda: put(low_v, low_b)

    near_top, near_low = take(near_ref, None)
    far_top, far_low = take(far_ref, jnp.logical_or(is_first, is_last))

    @pl.when(odd == 1)
    def _():
        near_top()
        far_low()

    @pl.when(odd == 0)
    def _():
        near_low()
        far_top()

    start(three, v3, PAD, b3, PAD, 0, n3, 8)
    sweep(three, w3, PAD, v3, PAD, b3, PAD, 0, n3, 16)
    restrict(three, b4, 0, four, w3, PAD, b3, PAD, 0, n4, 8)
    start(four, v4, PAD, b4, 0, 0, n4, 16)
    src, dst = v4, w4
    for _ in range(COARSE_SWEEPS - 1):
        sweep(four, dst, PAD, src, PAD, b4, 0, 0, n4, 16)
        src, dst = dst, src

    def trim(ref, level, n):
        @pl.when(me < 2)
        def _():
            clear(ref, level, 0, PAD)

        @pl.when(me >= 2 * chips - 2)
        def _():
            clear(ref, level, PAD + n, 2 * PAD + n)

    half, quarter = own // 2, own // 4
    correct(three, four, v3, PAD, w3, PAD, src, PAD, me * quarter - 2, quarter + 4, 8)
    sweep(three, w3, PAD, v3, PAD, b3, PAD, me * half - 3, half + 6, 8)
    trim(w3, three, n3)
    sweep(three, v3, PAD, w3, PAD, b3, PAD, me * half - 2, half + 4, 8)
    trim(v3, three, n3)

    def trim_own(ref, level, halo, n):
        @pl.when(is_first)
        def _():
            clear(ref, level, 0, halo)

        @pl.when(is_last)
        def _():
            clear(ref, level, halo + n, 2 * halo + n)

    total = own + 2 * TWO_HALO
    correct(two, three, x2, 0, v2, 0, v3, PAD + me * half - TWO_HALO // 2, 0, total // 2, 8)
    sweep(two, y2, 0, x2, 0, b2, 0, 1, total - 1, 10)
    trim_own(y2, two, TWO_HALO, own)
    sweep(two, x2, 0, y2, 0, b2, 0, 2, total - 2, 8)
    trim_own(x2, two, TWO_HALO, own)

    n1 = rows // 2
    total = n1 + 2 * MID_HALO

    correct(
        mid, two, x1, MID_HALO - 4, v1_ref, MID_HALO - 4, x2, TWO_HALO - 2, 0, n1 // 2 + 4, 4
    )
    sweep(mid, y1, 0, x1, 0, b1_ref, 0, MID_HALO - 2, MID_HALO + n1 + 2, 6)
    trim_own(y1, mid, MID_HALO, n1)
    sweep(mid, x1, 0, y1, 0, b1_ref, 0, MID_HALO - 1, MID_HALO + n1 + 1, 5)
    trim_own(x1, mid, MID_HALO, n1)

    low, high = HALO, HALO + rows
    correct(fine, mid, x0, HALO - 2, v0_ref, HALO - 2, x1, MID_HALO - 1, 0, n1 + 2, 2)
    sweep(fine, y0, 0, x0, 0, b0_ref, 0, low - 1, high + 1, 4)
    trim_own(y0, fine, HALO, rows)
    copies = []
    for group in range(rows // SUBS):
        first_row = low + group * SUBS
        rows_of = pl.ds(group * SUBS, SUBS)
        sweep(fine, x0, 0, y0, 0, b0_ref, 0, first_row, first_row + SUBS, 4)
        for layer in range(2):
            for t in range(fine.tiles):
                for s in range(SUBS):
                    first = first_row * fine.size + t * SUBS + s
                    column = (s * fine.tiles + t) * LANES
                    native[layer, rows_of, column : column + LANES] = x0[
                        layer, pl.ds(first, SUBS, stride=fine.size), :
                    ]
            copies.append(
                pltpu.make_async_copy(
                    native.at[layer, rows_of], out_ref.at[layer, rows_of],
                    sems.at[layer, group],
                )
            )
            copies[-1].start()
    for copy in copies:
        copy.wait()


def shape(*dims):
    return jax.ShapeDtypeStruct(dims, jnp.float32)


def scratch(layers, rows, level):
    return pltpu.VMEM((layers, rows * level.size, LANES), jnp.float32)


HBM = pl.BlockSpec(memory_space=pltpu.HBM)
VMEM = pl.BlockSpec(memory_space=pltpu.VMEM)


def call(kernel, out_shape, scratch_shapes=(), cost=None, limit=24, **options):
    if cost is not None:
        cost = pl.CostEstimate(flops=cost, bytes_accessed=cost // 8, transcendentals=0)
    return pl.pallas_call(
        kernel,
        out_shape=out_shape,
        scratch_shapes=list(scratch_shapes),
        cost_estimate=cost,
        compiler_params=pltpu.CompilerParams(vmem_limit_bytes=limit * 1024 * 1024),
        **options,
    )


def shards(stream_now, vorticity):
    _, rows, columns = stream_now.shape
    count = lax.axis_size("wide")
    tiles = columns // (SUBS * LANES)
    fine, mid = Level(0, tiles, 1), Level(1, tiles // 2, 1)
    two, three, four = Level(2, tiles // 4, 1), Level(3, tiles // 4, 2), Level(4, tiles // 4, 4)
    core_swap = [(i, i ^ 1) for i in range(count)]
    members = lax.axis_size("member")
    inside = [(i, ((i + 1) ^ 1) - 1) for i in range(1, count - 1)]
    if members % 2:
        ends = [(0, count - 1), (count - 1, 0)]
        chip_swap = [(m * count + i, m * count + j) for m in range(members) for i, j in ends]
    else:
        chip_swap = [
            (m * count + i, (m ^ 1) * count + i) for m in range(members) for i in (0, count - 1)
        ]
    chip_swap += [(m * count + i, m * count + j) for m in range(members) for i, j in inside]
    groups = rows // SUBS

    def exchange(near, far):
        return lax.ppermute(near, "wide", core_swap), lax.ppermute(far, ("member", "wide"), chip_swap)

    half, quarter = rows // 2, rows // 4
    total = rows + 2 * HALO
    ext, near, far = call(
        functools.partial(pack_kernel, fine, rows),
        [shape(4, total * fine.size, LANES)] + [shape(4, HALO * fine.size, LANES)] * 2,
        [pltpu.VMEM((4, rows, columns), jnp.float32), pltpu.SemaphoreType.DMA((4,))],
        in_specs=[HBM, HBM],
    )(stream_now, vorticity)
    near, far = exchange(near, far)
    state = [
        shape(4, total * fine.size, LANES),
        shape(4, total * fine.size, LANES),
        shape(2, total * fine.size, LANES),
        shape(2, total * fine.size, LANES),
        shape(2, total * fine.size, LANES),
        shape(2, half * mid.size, LANES),
    ]
    inner = call(
        functools.partial(inner_kernel, fine, mid, rows),
        state,
        cost=8000000,
    )(ext)
    edge = shape(2, MID_HALO * mid.size + fine.size, LANES)
    outer = call(
        functools.partial(outer_kernel, fine, mid, rows),
        [shape(4, total * fine.size, LANES)] + state + [edge, edge],
        input_output_aliases={i: i for i in range(7)},
    )(ext, *inner, near, far)
    b0, v0, b1, near, far = outer[3], outer[5], outer[6], outer[7], outer[8]
    near, far = exchange(near, far)
    vorticity_next = call(
        functools.partial(emit_kernel, fine, rows),
        shape(2, rows, columns),
        [pltpu.VMEM((2, rows, columns), jnp.float32), pltpu.SemaphoreType.DMA((2, groups))],
        cost=4000000,
        out_specs=HBM,
    )(b0)
    chips = count // 2
    eighth = rows // 8
    two_edge = shape(2, 4 * two.size, LANES)
    two_all = shape(2, (quarter + 2 * TWO_HALO) * two.size, LANES)
    b1, v1, b2, v2, b3, near, far, v0 = call(
        functools.partial(middle_kernel, fine, mid, two, three, half),
        [
            shape(2, (half + 2 * MID_HALO) * mid.size, LANES),
            shape(2, (half + 2 * MID_HALO) * mid.size, LANES),
            two_all,
            two_all,
            shape(chips, 2, eighth // 2 * three.size, LANES),
            two_edge,
            two_edge,
            shape(2, total * fine.size, LANES),
        ],
        [
            scratch(2, half + 2 * MID_HALO, mid),
            scratch(2, quarter + 2 * TWO_HALO, two),
            scratch(2, eighth, three),
        ],
        input_output_aliases={3: 7},
    )(b1, near, far, v0)
    near = lax.ppermute(near, "wide", core_swap)
    far = lax.ppermute(far, ("member", "wide"), chip_swap)
    cores = [[i for i in range(count) if i % 2 == c] for c in range(2)]
    same = lax.all_to_all(b3, "wide", 0, 0, axis_index_groups=cores)
    other = lax.ppermute(same, "wide", core_swap)
    n3, n4 = count * eighth, count * eighth // 2
    stream_next = call(
        functools.partial(coarse_kernel, (fine, mid, two, three, four), rows),
        shape(2, rows, columns),
        [scratch(2, quarter + 2 * TWO_HALO, two)] * 4
        + [scratch(2, n3 + 2 * PAD, three)] * 3
        + [scratch(2, n4, four)]
        + [scratch(2, n4 + 2 * PAD, four)] * 2
        + [scratch(2, half + 2 * MID_HALO, mid)] * 2
        + [scratch(2, total, fine)] * 2
        + [pltpu.VMEM((2, rows, columns), jnp.float32), pltpu.SemaphoreType.DMA((2, groups))],
        out_specs=HBM,
    )(same, other, near, far, b2, v2, b1, v1, b0, v0)
    return (vorticity_next, stream_next)


def solution(mesh):
    return jax.shard_map(
        shards,
        mesh=mesh,
        in_specs=(P("member", "wide", None), P("member", "wide", None)),
        out_specs=(P("member", "wide", None), P("member", "wide", None)),
        check_vma=False,
    )
```

```python
import functools

import jax
import jax.numpy as jnp
from jax import lax
from jax.experimental import pallas as pl
from jax.experimental.pallas import tpu as pltpu
from jax.sharding import PartitionSpec as P


LANES = 128
SUBS = 8
HALO = 3
MID_HALO = 6
TWO_HALO = 4
RELAX = 0.8
COUPLING = (0.02, 0.04)
TIME_STEP = 0.5
BETA = 0.05
DRAG = (0.0, 0.02)
COARSE_SWEEPS = 8


class Level:
    def __init__(self, level, tiles, stride):
        h2 = (2.0**level) ** 2
        self.tiles, self.stride = tiles, stride
        diag = [4.0 / h2 + f for f in COUPLING]
        self.keep = 1.0 - RELAX
        self.near = [RELAX / (d * h2) for d in diag]
        self.other = [RELAX * f / d for f, d in zip(COUPLING, diag)]
        self.src = [RELAX / d for d in diag]
        self.diag = diag
        self.inv_h2 = 1.0 / h2
        self.size = tiles * SUBS


def lane_index():
    return lax.broadcasted_iota(jnp.int32, (SUBS, LANES), 1)


def at(level, row, tile=0):
    base = row * level.size
    if not isinstance(row, int):
        base = pl.multiple_of(base, SUBS)
    return pl.ds(base + tile * SUBS, SUBS)


def load(ref, level, layer, row):
    return [ref[layer, at(level, row, t), :] for t in range(level.tiles)]


def store(ref, level, layer, row, values):
    for t in range(level.tiles):
        ref[layer, at(level, row, t), :] = values[t]


def east(values, stride=1):
    rolled = [pltpu.roll(v, LANES - stride, 1) for v in values]
    after = rolled[1:] + [pltpu.roll(rolled[0], SUBS - 1, 0)]
    edge = lane_index() >= LANES - stride
    return [jnp.where(edge, a, r) for a, r in zip(after, rolled)]


def west(values, stride=1):
    rolled = [pltpu.roll(v, stride, 1) for v in values]
    before = [pltpu.roll(rolled[-1], 1, 0)] + rolled[:-1]
    edge = lane_index() < stride
    return [jnp.where(edge, b, r) for b, r in zip(before, rolled)]


def transpose_tiles(tiles):
    sub = lax.broadcasted_iota(jnp.int32, (SUBS, LANES), 0)
    for k in (1, 2, 4):
        keep = (sub & k) == 0
        out = list(tiles)
        for i in range(SUBS):
            if not i & k:
                a, b = tiles[i], tiles[i + k]
                out[i] = jnp.where(keep, a, pltpu.roll(b, k, 0))
                out[i + k] = jnp.where(keep, pltpu.roll(a, SUBS - k, 0), b)
        tiles = out
    return tiles


def column_of(level, t, s):
    first = (s * level.tiles + t) * LANES
    return slice(first, first + LANES)


def to_native(level, dst, dst_row, src, layer, src_row, sign=1):
    for t in range(level.tiles):
        tiles = [src[layer, at(level, src_row + r, t), :] for r in range(SUBS)]
        for s, tile in enumerate(transpose_tiles(tiles)):
            dst[layer, dst_row : dst_row + SUBS, column_of(level, t, s)] = (
                tile if sign > 0 else -tile
            )


def row_blocks(low, high, block, body):
    count = high - low if isinstance(low, int) else high
    whole = count // block
    if whole > 1:
        lax.fori_loop(0, whole, lambda i, c: (body(low + i * block, block), c)[1], 0)
    elif whole == 1:
        body(low, block)
    if count % block:
        body(low + whole * block, count % block)


def star(rows, k, layer, level):
    centre = rows[k][layer]
    e, w = east(centre, level.stride), west(centre, level.stride)
    return [
        (n + s) + (a + b)
        for n, s, a, b in zip(rows[k + 1][layer], rows[k - 1][layer], e, w)
    ]


def load_rows(ref, level, first, count, margin=1):
    return {
        k: [load(ref, level, layer, first + k) for layer in range(2)]
        for k in range(-margin, count + margin)
    }


def sweep_rows(level, rows, source, count):
    out = {}
    for k in range(count):
        out[k] = []
        for layer in range(2):
            near = star(rows, k, layer, level)
            out[k].append(
                [
                    (level.keep * c + level.near[layer] * n)
                    + (level.other[layer] * o + level.src[layer] * b)
                    for c, n, o, b in zip(
                        rows[k][layer], near, rows[k][1 - layer], source[k][layer]
                    )
                ]
            )
    return out


def residual_rows(level, rows, source, count):
    out = {}
    for k in range(count):
        out[k] = []
        for layer in range(2):
            near = star(rows, k, layer, level)
            out[k].append(
                [
                    (b - level.diag[layer] * c)
                    + (level.inv_h2 * n + COUPLING[layer] * o)
                    for c, n, o, b in zip(
                        rows[k][layer], near, rows[k][1 - layer], source[k][layer]
                    )
                ]
            )
    return out


def store_rows(ref, level, first, rows, count):
    for k in range(count):
        for layer in range(2):
            store(ref, level, layer, first + k, rows[k][layer])


def sweep(level, dst, dst_at, src, src_at, b, b_at, low, high, block):
    def body(first, count):
        rows = load_rows(src, level, first + src_at, count)
        source = load_rows(b, level, first + b_at, count, 0)
        store_rows(dst, level, first + dst_at, sweep_rows(level, rows, source, count), count)

    row_blocks(low, high, block, body)


def start(level, dst, dst_at, b, b_at, low, high, block):
    def body(first, count):
        source = load_rows(b, level, first + b_at, count, 0)
        out = {
            k: [[level.src[l] * x for x in source[k][l]] for l in range(2)]
            for k in range(count)
        }
        store_rows(dst, level, first + dst_at, out, count)

    row_blocks(low, high, block, body)


def pack_columns(values):
    lane = lane_index()
    pick = (2 * lane) % LANES
    sums = [v + pltpu.roll(v, LANES - 1, 1) for v in values]
    picked = [jnp.take_along_axis(s, pick, axis=1) for s in sums]
    return [
        jnp.where(lane < LANES // 2, picked[2 * t], picked[2 * t + 1])
        for t in range(len(values) // 2)
    ]


def spread_columns(values):
    lane = lane_index()
    out = []
    for v in values:
        out.append(jnp.take_along_axis(v, lane // 2, axis=1))
        out.append(jnp.take_along_axis(v, LANES // 2 + lane // 2, axis=1))
    return out


def merge_columns(values, stride):
    even = (lane_index() // stride) % 2 == 0
    return [
        v + jnp.where(even, pltpu.roll(v, LANES - stride, 1), pltpu.roll(v, stride, 1))
        for v in values
    ]


def restrict(fine, dst, dst_at, coarse, src, src_at, b, b_at, low, high, block):
    def body(first, count):
        rows = load_rows(src, fine, 2 * first + src_at, 2 * count)
        source = load_rows(b, fine, 2 * first + b_at, 2 * count, 0)
        res = residual_rows(fine, rows, source, 2 * count)
        out = {}
        for k in range(count):
            out[k] = []
            for layer in range(2):
                pair = [x + y for x, y in zip(res[2 * k][layer], res[2 * k + 1][layer])]
                if coarse.tiles < fine.tiles:
                    pair = pack_columns(pair)
                else:
                    pair = merge_columns(pair, fine.stride)
                out[k].append([0.25 * x for x in pair])
        store_rows(dst, coarse, first + dst_at, out, count)

    row_blocks(low, high, block, body)


def correct(fine, coarse, dst, dst_at, src, src_at, add, add_at, low, high, block):
    def body(first, count):
        coarse_rows = load_rows(add, coarse, first + add_at, count, 0)
        fine_rows = load_rows(src, fine, 2 * first + src_at, 2 * count, 0)
        out = {}
        for k in range(count):
            spread = [
                spread_columns(v) if coarse.tiles < fine.tiles else v for v in coarse_rows[k]
            ]
            for half in range(2):
                out[2 * k + half] = [
                    [x + y for x, y in zip(fine_rows[2 * k + half][l], spread[l])]
                    for l in range(2)
                ]
        store_rows(dst, fine, 2 * first + dst_at, out, 2 * count)

    row_blocks(low, high, block, body)


def clear(ref, level, low, high):
    ref[:, low * level.size : high * level.size, :] = jnp.zeros(
        (ref.shape[0], (high - low) * level.size, LANES), jnp.float32
    )


def place():
    me, count = lax.axis_index("wide"), lax.axis_size("wide")
    return me, lax.rem(me, 2), me == 0, me == count - 1


def pack_kernel(level, rows, p_ref, q_ref, ext_ref, near_ref, far_ref, native, sems):
    copies = []
    for field, ref in enumerate((p_ref, q_ref)):
        for layer in range(2):
            which = 2 * field + layer
            copies.append(
                pltpu.make_async_copy(ref.at[layer], native.at[which], sems.at[which])
            )
            copies[-1].start()
    for which in range(4):
        copies[which].wait()
        for group in range(rows // SUBS):
            for t in range(level.tiles):
                tiles = [
                    native[which, group * SUBS : (group + 1) * SUBS, column_of(level, t, s)]
                    for s in range(SUBS)
                ]
                for r, tile in enumerate(transpose_tiles(tiles)):
                    ext_ref[which, at(level, HALO + group * SUBS + r, t), :] = tile
    send_edges(level, HALO, HALO, rows, ext_ref, near_ref, far_ref)


def send_edges(level, width, src_at, rows, src, near_ref, far_ref):
    _, odd, _, _ = place()
    size = width * level.size
    last = (src_at + rows - width) * level.size
    top = src_at * level.size
    near = pl.multiple_of(jnp.where(odd == 1, top, last), SUBS)
    far = pl.multiple_of(jnp.where(odd == 1, last, top), SUBS)
    near_ref[:, 0:size, :] = src[:, pl.ds(near, size), :]
    far_ref[:, 0:size, :] = src[:, pl.ds(far, size), :]


def receive_edges(level, width, dst_at, rows, dst, near_ref, far_ref):
    _, odd, first, last = place()
    size = width * level.size
    low = (dst_at + rows) * level.size
    top = (dst_at - width) * level.size
    near = pl.multiple_of(jnp.where(odd == 1, top, low), SUBS)
    far = pl.multiple_of(jnp.where(odd == 1, low, top), SUBS)
    dst[:, pl.ds(near, size), :] = near_ref[:, 0:size, :]
    outside = jnp.logical_or(first, last)
    dst[:, pl.ds(far, size), :] = jnp.where(outside, 0.0, far_ref[:, 0:size, :])


def shift_rows(level, ext, e_ref, w_ref, low, high, block):
    def body(first, count):
        for k in range(count):
            for f in range(4):
                v = load(ext, level, f, first + k)
                store(e_ref, level, f, first + k, east(v))
                store(w_ref, level, f, first + k, west(v))

    row_blocks(low, high, block, body)


def advance_rows(level, b_ref, ext, e_ref, w_ref, low, high, block):
    def body(first, count):
        for layer in range(2):
            for t in range(level.tiles):
                def grab(ref, field):
                    return {
                        k: ref[2 * field + layer, at(level, first + k, t), :]
                        for k in range(-1, count + 1)
                    }

                p, pe, pw = grab(ext, 0), grab(e_ref, 0), grab(w_ref, 0)
                q, qe, qw = grab(ext, 1), grab(e_ref, 1), grab(w_ref, 1)
                zonal = {k: pe[k] - pw[k] for k in p}
                for k in range(count):
                    n, s = k + 1, k - 1
                    v0, ve, vw = p[n] - p[s], pe[n] - pe[s], pw[n] - pw[s]
                    jac = q[n] * (zonal[k] + zonal[n]) - q[s] * (zonal[k] + zonal[s])
                    jac = jac - qe[k] * (v0 + ve) + qw[k] * (v0 + vw)
                    jac = jac + qe[n] * (pe[k] - p[n]) - qe[s] * (pe[k] - p[s])
                    jac = jac - qw[n] * (pw[k] - p[n]) + qw[s] * (pw[k] - p[s])
                    step = (TIME_STEP / 12.0) * jac + (0.5 * TIME_STEP * BETA) * zonal[k]
                    if layer == 1:
                        lap = (p[n] + p[s]) + (pe[k] + pw[k]) - 4.0 * p[k]
                        step = step + (TIME_STEP * DRAG[1]) * lap
                    b_ref[layer, at(level, first + k, t), :] = step - q[k]

    row_blocks(low, high, block, body)


def inner_kernel(level, coarse, rows, ext, e_ref, w_ref, b_ref, v_one, v_two, bc_ref):
    low, high = HALO, HALO + rows
    shift_rows(level, ext, e_ref, w_ref, low, high, 4)
    advance_rows(level, b_ref, ext, e_ref, w_ref, low + 1, high - 1, 2)
    sweep(level, v_one, 0, ext, 0, b_ref, 0, low + 2, high - 2, 4)
    sweep(level, v_two, 0, v_one, 0, b_ref, 0, low + 3, high - 3, 4)
    restrict(level, bc_ref, 0, coarse, v_two, HALO, b_ref, HALO, 2, rows // 2 - 2, 2)


def outer_kernel(level, coarse, rows, *refs):
    near_ref, far_ref = refs[7:9]
    ext, e_ref, w_ref, b_ref, v_one, v_two, bc_ref, bc_near_ref, bc_far_ref = refs[9:]
    _, _, is_first, is_last = place()
    low, high = HALO, HALO + rows
    total = rows + 2 * HALO
    receive_edges(level, HALO, HALO, rows, ext, near_ref, far_ref)
    shift_rows(level, ext, e_ref, w_ref, 0, low, 3)
    shift_rows(level, ext, e_ref, w_ref, high, total, 3)
    advance_rows(level, b_ref, ext, e_ref, w_ref, 1, low + 1, 3)
    advance_rows(level, b_ref, ext, e_ref, w_ref, high - 1, total - 1, 3)
    sweep(level, v_one, 0, ext, 0, b_ref, 0, 1, low + 2, 4)
    sweep(level, v_one, 0, ext, 0, b_ref, 0, high - 2, total - 1, 4)

    def trim(ref):
        @pl.when(is_first)
        def _():
            clear(ref, level, 0, HALO)

        @pl.when(is_last)
        def _():
            clear(ref, level, high, total)

    trim(v_one)
    sweep(level, v_two, 0, v_one, 0, b_ref, 0, 2, low + 3, 4)
    sweep(level, v_two, 0, v_one, 0, b_ref, 0, high - 3, total - 2, 4)
    trim(v_two)
    half = rows // 2
    restrict(level, bc_ref, 0, coarse, v_two, HALO, b_ref, HALO, 0, 2, 2)
    restrict(level, bc_ref, 0, coarse, v_two, HALO, b_ref, HALO, half - 2, half, 2)
    send_edges(coarse, MID_HALO, 0, half, bc_ref, bc_near_ref, bc_far_ref)


def emit_kernel(level, rows, b_ref, next_ref, native, sems):
    copies = []
    for layer in range(2):
        for group in range(rows // SUBS):
            rows_of = pl.ds(group * SUBS, SUBS)
            to_native(level, native, group * SUBS, b_ref, layer, HALO + group * SUBS, -1)
            copies.append(
                pltpu.make_async_copy(
                    native.at[layer, rows_of], next_ref.at[layer, rows_of],
                    sems.at[layer, group],
                )
            )
            copies[-1].start()
    for copy in copies:
        copy.wait()


def middle_kernel(
    fine, level, two, three, rows, b_own, near_ref, far_ref, v0_ref,
    b_ref, v_ref, b2_ref, v2_ref, out_ref, two_near_ref, two_far_ref,
    v_one, w_two, b3,
):
    _, odd, is_first, is_last = place()
    total = rows + 2 * MID_HALO
    own = rows // 2
    edge = MID_HALO * level.size
    b_ref[:, edge : edge + rows * level.size, :] = b_own[...]
    receive_edges(level, MID_HALO, MID_HALO, rows, b_ref, near_ref, far_ref)
    start(level, v_one, 0, b_ref, 0, 0, total, 4)

    def trim(ref, of, halo, n):
        @pl.when(is_first)
        def _():
            clear(ref, of, 0, halo)

        @pl.when(is_last)
        def _():
            clear(ref, of, halo + n, 2 * halo + n)

    trim(v_one, level, MID_HALO, rows)
    sweep(level, v_ref, 0, v_one, 0, b_ref, 0, 1, total - 1, 6)
    trim(v_ref, level, MID_HALO, rows)
    restrict(
        level, b2_ref, TWO_HALO, two, v_ref, MID_HALO, b_ref, MID_HALO, -2, own + 2, 4
    )
    start(two, w_two, TWO_HALO, b2_ref, TWO_HALO, -2, own + 2, 8)
    trim(w_two, two, TWO_HALO, own)
    sweep(two, v2_ref, TWO_HALO, w_two, TWO_HALO, b2_ref, TWO_HALO, -1, own + 1, 6)
    trim(v2_ref, two, TWO_HALO, own)
    restrict(
        two, b3, 0, three, v2_ref, TWO_HALO, b2_ref, TWO_HALO, 0, own // 2, 2
    )
    even = lane_index() % 2 == 0
    for layer in range(2):
        for pair in range(own // 4):
            row = jnp.where(
                even,
                b3[layer, at(three, 2 * pair), :],
                b3[layer, at(three, 2 * pair + 1), :],
            )
            for copy in range(out_ref.shape[0]):
                out_ref[copy, layer, at(three, pair), :] = row
    up, down = pl.ds((TWO_HALO + 1) * two.size, 3 * two.size), pl.ds(
        own * two.size, 3 * two.size
    )
    up_b, down_b = at(two, TWO_HALO + 2), at(two, TWO_HALO + own - 3)
    last = pl.ds(3 * two.size, two.size)

    tail = pl.ds(4 * two.size, fine.size)
    up_0 = pl.ds((HALO + 1) * fine.size, fine.size)
    down_0 = pl.ds((HALO + 2 * rows - 2) * fine.size, fine.size)

    def send(ref, rows_v, row_b, row_0):
        ref[:, 0 : 3 * two.size, :] = v2_ref[:, rows_v, :]
        ref[:, last, :] = b2_ref[:, row_b, :]
        ref[:, tail, :] = v0_ref[:, row_0, :]

    @pl.when(odd == 1)
    def _():
        send(two_near_ref, up, up_b, up_0)
        send(two_far_ref, down, down_b, down_0)

    @pl.when(odd == 0)
    def _():
        send(two_near_ref, down, down_b, down_0)
        send(two_far_ref, up, up_b, up_0)


PAD = 4


def coarse_solve(level, dst, dst_at, b_ref, n):
    groups = level.stride
    m = n // groups
    part = lane_index() % groups
    source = []
    for layer in range(2):
        source.append([])
        for k in range(m):
            tile = load(b_ref, level, layer, k)[0]
            for g in range(1, groups):
                tile = jnp.where(part == g, load(b_ref, level, layer, g * m + k)[0], tile)
            source[layer].append(level.src[layer] * tile)
    values = source
    for _ in range(COARSE_SWEEPS - 1):
        new = []
        for layer in range(2):
            v, o = values[layer], values[1 - layer]
            below = jnp.where(part == groups - 1, 0.0, pltpu.roll(v[0], LANES - 1, 1))
            above = jnp.where(part == 0, 0.0, pltpu.roll(v[-1], 1, 1))
            out = []
            for k in range(m):
                n_row = v[k + 1] if k + 1 < m else below
                s_row = v[k - 1] if k else above
                e, w = east([v[k]], groups)[0], west([v[k]], groups)[0]
                out.append(
                    (level.keep * v[k] + level.near[layer] * ((n_row + s_row) + (e + w)))
                    + (level.other[layer] * o[k] + source[layer][k])
                )
            new.append(out)
        values = new
    for layer in range(2):
        for k in range(m):
            moved = {
                d: pltpu.roll(values[layer][k], d % LANES, 1) if d else values[layer][k]
                for d in range(1 - groups, groups)
            }
            for g in range(groups):
                tile = moved[-g]
                for j in range(1, groups):
                    tile = jnp.where(part == j, moved[j - g], tile)
                dst[layer, at(level, dst_at + g * m + k), :] = tile


def coarse_kernel(
    levels, rows, same_ref, other_ref, near_ref, far_ref,
    b2_ref, v2_ref, b1_ref, v1_ref, b0_ref, v0_in, out_ref, v0_ref,
    b2, v2, x2, y2, b3, v3, w3, b4, v4, x1, y1, x0, y0, native, sems,
):
    me, odd, is_first, is_last = place()
    fine, mid, two, three, four = levels
    own = rows // 4
    chips = same_ref.shape[0]
    n3, n4 = chips * own, chips * own // 2
    for ref, level, n in ((b3, three, n3), (v3, three, n3), (w3, three, n3), (v4, four, n4)):
        clear(ref, level, 0, PAD)
        clear(ref, level, PAD + n, 2 * PAD + n)
    even = lane_index() % 2 == 0

    def gather_body(chip, carry):
        for ref, core in ((same_ref, odd), (other_ref, 1 - odd)):
            row = (2 * chip + core) * (own // 2) + PAD
            for layer in range(2):
                for pair in range(own // 4):
                    both = ref[chip, layer, at(three, pair), :]
                    first = jnp.where(even, both, pltpu.roll(both, 1, 1))
                    second = jnp.where(even, pltpu.roll(both, LANES - 1, 1), both)
                    b3[layer, at(three, row + 2 * pair), :] = first
                    b3[layer, at(three, row + 2 * pair + 1), :] = second
        return carry

    lax.fori_loop(0, chips, gather_body, 0, unroll=min(chips, 8))

    b2[...] = b2_ref[...]
    v2[...] = v2_ref[...]

    def take(ref, zero):
        top_v, low_v = pl.ds(0, 3 * two.size), pl.ds((TWO_HALO + own + 1) * two.size, 3 * two.size)
        top_b, low_b = at(two, TWO_HALO - 3), at(two, TWO_HALO + own + 2)
        last = pl.ds(3 * two.size, two.size)

        tail = pl.ds(4 * two.size, fine.size)
        top_0 = pl.ds((HALO - 2) * fine.size, fine.size)
        low_0 = pl.ds((HALO + rows + 1) * fine.size, fine.size)

        def drop(values):
            return values if zero is None else jnp.where(zero, 0.0, values)

        def put(rows_v, row_b, row_0):
            v2[:, rows_v, :] = drop(ref[:, 0 : 3 * two.size, :])
            b2[:, row_b, :] = ref[:, last, :]
            v0_ref[:, row_0, :] = drop(ref[:, tail, :])

        return lambda: put(top_v, top_b, top_0), lambda: put(low_v, low_b, low_0)

    near_top, near_low = take(near_ref, None)
    far_top, far_low = take(far_ref, jnp.logical_or(is_first, is_last))

    @pl.when(odd == 1)
    def _():
        near_top()
        far_low()

    @pl.when(odd == 0)
    def _():
        near_low()
        far_top()

    start(three, v3, PAD, b3, PAD, 0, n3, 8)
    sweep(three, w3, PAD, v3, PAD, b3, PAD, 0, n3, 16)
    restrict(three, b4, 0, four, w3, PAD, b3, PAD, 0, n4, 8)
    coarse_solve(four, v4, PAD, b4, n4)

    def trim(ref, level, n):
        @pl.when(me < 2)
        def _():
            clear(ref, level, 0, PAD)

        @pl.when(me >= 2 * chips - 2)
        def _():
            clear(ref, level, PAD + n, 2 * PAD + n)

    half, quarter = own // 2, own // 4
    correct(three, four, v3, PAD, w3, PAD, v4, PAD, me * quarter - 2, quarter + 4, 8)
    sweep(three, w3, PAD, v3, PAD, b3, PAD, me * half - 3, half + 6, 8)
    trim(w3, three, n3)
    sweep(three, v3, PAD, w3, PAD, b3, PAD, me * half - 2, half + 4, 8)
    trim(v3, three, n3)

    def trim_own(ref, level, halo, n):
        @pl.when(is_first)
        def _():
            clear(ref, level, 0, halo)

        @pl.when(is_last)
        def _():
            clear(ref, level, halo + n, 2 * halo + n)

    total = own + 2 * TWO_HALO
    correct(two, three, x2, 0, v2, 0, v3, PAD + me * half - TWO_HALO // 2, 0, total // 2, 8)
    sweep(two, y2, 0, x2, 0, b2, 0, 1, total - 1, 10)
    trim_own(y2, two, TWO_HALO, own)
    sweep(two, x2, 0, y2, 0, b2, 0, 2, total - 2, 8)
    trim_own(x2, two, TWO_HALO, own)

    n1 = rows // 2
    total = n1 + 2 * MID_HALO

    correct(
        mid, two, x1, MID_HALO - 4, v1_ref, MID_HALO - 4, x2, TWO_HALO - 2, 0, n1 // 2 + 4, 4
    )
    sweep(mid, y1, 0, x1, 0, b1_ref, 0, MID_HALO - 2, MID_HALO + n1 + 2, 6)
    trim_own(y1, mid, MID_HALO, n1)
    sweep(mid, x1, 0, y1, 0, b1_ref, 0, MID_HALO - 1, MID_HALO + n1 + 1, 5)
    trim_own(x1, mid, MID_HALO, n1)

    low, high = HALO, HALO + rows
    correct(fine, mid, x0, HALO - 2, v0_ref, HALO - 2, x1, MID_HALO - 1, 0, n1 + 2, 2)
    sweep(fine, y0, 0, x0, 0, b0_ref, 0, low - 1, high + 1, 4)
    trim_own(y0, fine, HALO, rows)
    copies = []
    for group in range(rows // SUBS):
        first_row = low + group * SUBS
        rows_of = pl.ds(group * SUBS, SUBS)
        sweep(fine, x0, 0, y0, 0, b0_ref, 0, first_row, first_row + SUBS, 4)
        for layer in range(2):
            to_native(fine, native, group * SUBS, x0, layer, first_row)
            copies.append(
                pltpu.make_async_copy(
                    native.at[layer, rows_of], out_ref.at[layer, rows_of],
                    sems.at[layer, group],
                )
            )
            copies[-1].start()
    for copy in copies:
        copy.wait()


def shape(*dims):
    return jax.ShapeDtypeStruct(dims, jnp.float32)


def scratch(layers, rows, level):
    return pltpu.VMEM((layers, rows * level.size, LANES), jnp.float32)


HBM = pl.BlockSpec(memory_space=pltpu.HBM)
VMEM = pl.BlockSpec(memory_space=pltpu.VMEM)


def call(kernel, out_shape, scratch_shapes=(), cost=None, limit=24, **options):
    if cost is not None:
        cost = pl.CostEstimate(flops=cost, bytes_accessed=cost // 8, transcendentals=0)
    return pl.pallas_call(
        kernel,
        out_shape=out_shape,
        scratch_shapes=list(scratch_shapes),
        cost_estimate=cost,
        compiler_params=pltpu.CompilerParams(vmem_limit_bytes=limit * 1024 * 1024),
        **options,
    )


def shards(stream_now, vorticity):
    _, rows, columns = stream_now.shape
    count = lax.axis_size("wide")
    tiles = columns // (SUBS * LANES)
    fine, mid = Level(0, tiles, 1), Level(1, tiles // 2, 1)
    two, three, four = Level(2, tiles // 4, 1), Level(3, tiles // 4, 2), Level(4, tiles // 4, 4)
    core_swap = [(i, i ^ 1) for i in range(count)]
    members = lax.axis_size("member")
    inside = [(i, ((i + 1) ^ 1) - 1) for i in range(1, count - 1)]
    if members % 2:
        ends = [(0, count - 1), (count - 1, 0)]
        chip_swap = [(m * count + i, m * count + j) for m in range(members) for i, j in ends]
    else:
        chip_swap = [
            (m * count + i, (m ^ 1) * count + i) for m in range(members) for i in (0, count - 1)
        ]
    chip_swap += [(m * count + i, m * count + j) for m in range(members) for i, j in inside]
    groups = rows // SUBS

    def exchange(near, far):
        far = lax.ppermute(far, ("member", "wide"), chip_swap)
        near = lax.ppermute(near, "wide", core_swap)
        return near, far

    half, quarter = rows // 2, rows // 4
    total = rows + 2 * HALO
    ext, near, far = call(
        functools.partial(pack_kernel, fine, rows),
        [shape(4, total * fine.size, LANES)] + [shape(4, HALO * fine.size, LANES)] * 2,
        [pltpu.VMEM((4, rows, columns), jnp.float32), pltpu.SemaphoreType.DMA((4,))],
        in_specs=[HBM, HBM],
    )(*(pltpu.with_memory_space_constraint(x, pltpu.HBM) for x in (stream_now, vorticity)))
    near, far = exchange(near, far)
    state = [
        shape(4, total * fine.size, LANES),
        shape(4, total * fine.size, LANES),
        shape(2, total * fine.size, LANES),
        shape(2, total * fine.size, LANES),
        shape(2, total * fine.size, LANES),
        shape(2, half * mid.size, LANES),
    ]
    inner = call(
        functools.partial(inner_kernel, fine, mid, rows),
        state,
        cost=8000000,
    )(ext)
    edge = shape(2, MID_HALO * mid.size, LANES)
    outer = call(
        functools.partial(outer_kernel, fine, mid, rows),
        [shape(4, total * fine.size, LANES)] + state + [edge, edge],
        input_output_aliases={i: i for i in range(7)},
    )(ext, *inner, near, far)
    b0, v0, b1, near, far = outer[3], outer[5], outer[6], outer[7], outer[8]
    near, far = exchange(near, far)
    vorticity_next = call(
        functools.partial(emit_kernel, fine, rows),
        shape(2, rows, columns),
        [pltpu.VMEM((2, rows, columns), jnp.float32), pltpu.SemaphoreType.DMA((2, groups))],
        cost=4000000,
        out_specs=HBM,
    )(b0)
    chips = count // 2
    eighth = rows // 8
    two_edge = shape(2, 4 * two.size + fine.size, LANES)
    two_all = shape(2, (quarter + 2 * TWO_HALO) * two.size, LANES)
    b1, v1, b2, v2, b3, near, far = call(
        functools.partial(middle_kernel, fine, mid, two, three, half),
        [
            shape(2, (half + 2 * MID_HALO) * mid.size, LANES),
            shape(2, (half + 2 * MID_HALO) * mid.size, LANES),
            two_all,
            two_all,
            shape(chips, 2, eighth // 2 * three.size, LANES),
            two_edge,
            two_edge,
        ],
        [
            scratch(2, half + 2 * MID_HALO, mid),
            scratch(2, quarter + 2 * TWO_HALO, two),
            scratch(2, eighth, three),
        ],
    )(b1, near, far, v0)
    near, far = exchange(near, far)
    cores = [[i for i in range(count) if i % 2 == c] for c in range(2)]
    same = lax.all_to_all(b3, "wide", 0, 0, axis_index_groups=cores)
    other = lax.ppermute(same, "wide", core_swap)
    n3, n4 = count * eighth, count * eighth // 2
    stream_next, _ = call(
        functools.partial(coarse_kernel, (fine, mid, two, three, four), rows),
        [shape(2, rows, columns), shape(2, total * fine.size, LANES)],
        [scratch(2, quarter + 2 * TWO_HALO, two)] * 4
        + [scratch(2, n3 + 2 * PAD, three)] * 3
        + [scratch(2, n4, four)]
        + [scratch(2, n4 + 2 * PAD, four)]
        + [scratch(2, half + 2 * MID_HALO, mid)] * 2
        + [scratch(2, total, fine)] * 2
        + [pltpu.VMEM((2, rows, columns), jnp.float32), pltpu.SemaphoreType.DMA((2, groups))],
        out_specs=[HBM, VMEM],
        input_output_aliases={9: 1},
    )(same, other, near, far, b2, v2, b1, v1, b0, v0)
    return (vorticity_next, stream_next)


def solution(mesh):
    return jax.shard_map(
        shards,
        mesh=mesh,
        in_specs=(P("member", "wide", None), P("member", "wide", None)),
        out_specs=(P("member", "wide", None), P("member", "wide", None)),
        check_vma=False,
    )
```

```python
import functools

import jax
import jax.numpy as jnp
from jax import lax
from jax.experimental import pallas as pl
from jax.experimental.pallas import tpu as pltpu
from jax.sharding import PartitionSpec as P


LANES = 128
SUBS = 8
HALO = 3
MID_HALO = 6
TWO_HALO = 4
RELAX = 0.8
COUPLING = (0.02, 0.04)
TIME_STEP = 0.5
BETA = 0.05
DRAG = (0.0, 0.02)
COARSE_SWEEPS = 8


class Level:
    def __init__(self, level, tiles, stride):
        h2 = (2.0**level) ** 2
        self.tiles, self.stride = tiles, stride
        diag = [4.0 / h2 + f for f in COUPLING]
        self.keep = 1.0 - RELAX
        self.near = [RELAX / (d * h2) for d in diag]
        self.other = [RELAX * f / d for f, d in zip(COUPLING, diag)]
        self.src = [RELAX / d for d in diag]
        self.diag = diag
        self.inv_h2 = 1.0 / h2
        self.size = tiles * SUBS


def lane_index():
    return lax.broadcasted_iota(jnp.int32, (SUBS, LANES), 1)


def at(level, row, tile=0):
    base = row * level.size
    if not isinstance(row, int):
        base = pl.multiple_of(base, SUBS)
    return pl.ds(base + tile * SUBS, SUBS)


def load(ref, level, layer, row):
    return [ref[layer, at(level, row, t), :] for t in range(level.tiles)]


def store(ref, level, layer, row, values):
    for t in range(level.tiles):
        ref[layer, at(level, row, t), :] = values[t]


def east(values, stride=1):
    rolled = [pltpu.roll(v, LANES - stride, 1) for v in values]
    after = rolled[1:] + [pltpu.roll(rolled[0], SUBS - 1, 0)]
    edge = lane_index() >= LANES - stride
    return [jnp.where(edge, a, r) for a, r in zip(after, rolled)]


def west(values, stride=1):
    rolled = [pltpu.roll(v, stride, 1) for v in values]
    before = [pltpu.roll(rolled[-1], 1, 0)] + rolled[:-1]
    edge = lane_index() < stride
    return [jnp.where(edge, b, r) for b, r in zip(before, rolled)]


def transpose_tiles(tiles):
    sub = lax.broadcasted_iota(jnp.int32, (SUBS, LANES), 0)
    for k in (1, 2, 4):
        keep = (sub & k) == 0
        out = list(tiles)
        for i in range(SUBS):
            if not i & k:
                a, b = tiles[i], tiles[i + k]
                out[i] = jnp.where(keep, a, pltpu.roll(b, k, 0))
                out[i + k] = jnp.where(keep, pltpu.roll(a, SUBS - k, 0), b)
        tiles = out
    return tiles


def column_of(level, t, s):
    first = (s * level.tiles + t) * LANES
    return slice(first, first + LANES)


def to_native(level, dst, dst_row, src, layer, src_row, sign=1):
    for t in range(level.tiles):
        tiles = [src[layer, at(level, src_row + r, t), :] for r in range(SUBS)]
        for s, tile in enumerate(transpose_tiles(tiles)):
            dst[layer, dst_row : dst_row + SUBS, column_of(level, t, s)] = (
                tile if sign > 0 else -tile
            )


def row_blocks(low, high, block, body):
    count = high - low if isinstance(low, int) else high
    whole = count // block
    if whole > 1:
        lax.fori_loop(0, whole, lambda i, c: (body(low + i * block, block), c)[1], 0)
    elif whole == 1:
        body(low, block)
    if count % block:
        body(low + whole * block, count % block)


def star(rows, k, layer, level):
    centre = rows[k][layer]
    e, w = east(centre, level.stride), west(centre, level.stride)
    return [
        (n + s) + (a + b)
        for n, s, a, b in zip(rows[k + 1][layer], rows[k - 1][layer], e, w)
    ]


def load_rows(ref, level, first, count, margin=1):
    return {
        k: [load(ref, level, layer, first + k) for layer in range(2)]
        for k in range(-margin, count + margin)
    }


def sweep_rows(level, rows, source, count):
    out = {}
    for k in range(count):
        out[k] = []
        for layer in range(2):
            near = star(rows, k, layer, level)
            out[k].append(
                [
                    (level.keep * c + level.near[layer] * n)
                    + (level.other[layer] * o + level.src[layer] * b)
                    for c, n, o, b in zip(
                        rows[k][layer], near, rows[k][1 - layer], source[k][layer]
                    )
                ]
            )
    return out


def residual_rows(level, rows, source, count):
    out = {}
    for k in range(count):
        out[k] = []
        for layer in range(2):
            near = star(rows, k, layer, level)
            out[k].append(
                [
                    (b - level.diag[layer] * c)
                    + (level.inv_h2 * n + COUPLING[layer] * o)
                    for c, n, o, b in zip(
                        rows[k][layer], near, rows[k][1 - layer], source[k][layer]
                    )
                ]
            )
    return out


def store_rows(ref, level, first, rows, count):
    for k in range(count):
        for layer in range(2):
            store(ref, level, layer, first + k, rows[k][layer])


def sweep(level, dst, dst_at, src, src_at, b, b_at, low, high, block):
    def body(first, count):
        rows = load_rows(src, level, first + src_at, count)
        source = load_rows(b, level, first + b_at, count, 0)
        store_rows(dst, level, first + dst_at, sweep_rows(level, rows, source, count), count)

    row_blocks(low, high, block, body)


def start(level, dst, dst_at, b, b_at, low, high, block):
    def body(first, count):
        source = load_rows(b, level, first + b_at, count, 0)
        out = {
            k: [[level.src[l] * x for x in source[k][l]] for l in range(2)]
            for k in range(count)
        }
        store_rows(dst, level, first + dst_at, out, count)

    row_blocks(low, high, block, body)


def pack_columns(values):
    lane = lane_index()
    pick = (2 * lane) % LANES
    sums = [v + pltpu.roll(v, LANES - 1, 1) for v in values]
    picked = [jnp.take_along_axis(s, pick, axis=1) for s in sums]
    return [
        jnp.where(lane < LANES // 2, picked[2 * t], picked[2 * t + 1])
        for t in range(len(values) // 2)
    ]


def spread_columns(values):
    lane = lane_index()
    out = []
    for v in values:
        out.append(jnp.take_along_axis(v, lane // 2, axis=1))
        out.append(jnp.take_along_axis(v, LANES // 2 + lane // 2, axis=1))
    return out


def merge_columns(values, stride):
    even = (lane_index() // stride) % 2 == 0
    return [
        v + jnp.where(even, pltpu.roll(v, LANES - stride, 1), pltpu.roll(v, stride, 1))
        for v in values
    ]


def restrict(fine, dst, dst_at, coarse, src, src_at, b, b_at, low, high, block):
    def body(first, count):
        rows = load_rows(src, fine, 2 * first + src_at, 2 * count)
        source = load_rows(b, fine, 2 * first + b_at, 2 * count, 0)
        res = residual_rows(fine, rows, source, 2 * count)
        out = {}
        for k in range(count):
            out[k] = []
            for layer in range(2):
                pair = [x + y for x, y in zip(res[2 * k][layer], res[2 * k + 1][layer])]
                if coarse.tiles < fine.tiles:
                    pair = pack_columns(pair)
                else:
                    pair = merge_columns(pair, fine.stride)
                out[k].append([0.25 * x for x in pair])
        store_rows(dst, coarse, first + dst_at, out, count)

    row_blocks(low, high, block, body)


def correct(fine, coarse, dst, dst_at, src, src_at, add, add_at, low, high, block):
    def body(first, count):
        coarse_rows = load_rows(add, coarse, first + add_at, count, 0)
        fine_rows = load_rows(src, fine, 2 * first + src_at, 2 * count, 0)
        out = {}
        for k in range(count):
            spread = [
                spread_columns(v) if coarse.tiles < fine.tiles else v for v in coarse_rows[k]
            ]
            for half in range(2):
                out[2 * k + half] = [
                    [x + y for x, y in zip(fine_rows[2 * k + half][l], spread[l])]
                    for l in range(2)
                ]
        store_rows(dst, fine, 2 * first + dst_at, out, 2 * count)

    row_blocks(low, high, block, body)


def clear(ref, level, low, high):
    ref[:, low * level.size : high * level.size, :] = jnp.zeros(
        (ref.shape[0], (high - low) * level.size, LANES), jnp.float32
    )


def place():
    me, count = lax.axis_index("wide"), lax.axis_size("wide")
    return me, lax.rem(me, 2), me == 0, me == count - 1


def pack_kernel(level, rows, p_ref, q_ref, ext_ref, near_ref, far_ref, native, sems):
    copies = []
    for field, ref in enumerate((p_ref, q_ref)):
        for layer in range(2):
            which = 2 * field + layer
            copies.append(
                pltpu.make_async_copy(ref.at[layer], native.at[which], sems.at[which])
            )
            copies[-1].start()
    for which in range(4):
        copies[which].wait()
        for group in range(rows // SUBS):
            for t in range(level.tiles):
                tiles = [
                    native[which, group * SUBS : (group + 1) * SUBS, column_of(level, t, s)]
                    for s in range(SUBS)
                ]
                for r, tile in enumerate(transpose_tiles(tiles)):
                    ext_ref[which, at(level, HALO + group * SUBS + r, t), :] = tile
    send_edges(level, HALO, HALO, rows, ext_ref, near_ref, far_ref)


def send_edges(level, width, src_at, rows, src, near_ref, far_ref):
    _, odd, _, _ = place()
    size = width * level.size
    last = (src_at + rows - width) * level.size
    top = src_at * level.size
    near = pl.multiple_of(jnp.where(odd == 1, top, last), SUBS)
    far = pl.multiple_of(jnp.where(odd == 1, last, top), SUBS)
    near_ref[:, 0:size, :] = src[:, pl.ds(near, size), :]
    far_ref[:, 0:size, :] = src[:, pl.ds(far, size), :]


def receive_edges(level, width, dst_at, rows, dst, near_ref, far_ref):
    _, odd, first, last = place()
    size = width * level.size
    low = (dst_at + rows) * level.size
    top = (dst_at - width) * level.size
    near = pl.multiple_of(jnp.where(odd == 1, top, low), SUBS)
    far = pl.multiple_of(jnp.where(odd == 1, low, top), SUBS)
    dst[:, pl.ds(near, size), :] = near_ref[:, 0:size, :]
    outside = jnp.logical_or(first, last)
    dst[:, pl.ds(far, size), :] = jnp.where(outside, 0.0, far_ref[:, 0:size, :])


def shift_rows(level, ext, e_ref, w_ref, low, high, block):
    def body(first, count):
        for k in range(count):
            for f in range(4):
                v = load(ext, level, f, first + k)
                store(e_ref, level, f, first + k, east(v))
                store(w_ref, level, f, first + k, west(v))

    row_blocks(low, high, block, body)


def advance_rows(level, b_ref, ext, e_ref, w_ref, low, high, block):
    def body(first, count):
        for layer in range(2):
            for t in range(level.tiles):
                def grab(ref, field):
                    return {
                        k: ref[2 * field + layer, at(level, first + k, t), :]
                        for k in range(-1, count + 1)
                    }

                p, pe, pw = grab(ext, 0), grab(e_ref, 0), grab(w_ref, 0)
                q, qe, qw = grab(ext, 1), grab(e_ref, 1), grab(w_ref, 1)
                zonal = {k: pe[k] - pw[k] for k in p}
                for k in range(count):
                    n, s = k + 1, k - 1
                    v0, ve, vw = p[n] - p[s], pe[n] - pe[s], pw[n] - pw[s]
                    jac = q[n] * (zonal[k] + zonal[n]) - q[s] * (zonal[k] + zonal[s])
                    jac = jac - qe[k] * (v0 + ve) + qw[k] * (v0 + vw)
                    jac = jac + qe[n] * (pe[k] - p[n]) - qe[s] * (pe[k] - p[s])
                    jac = jac - qw[n] * (pw[k] - p[n]) + qw[s] * (pw[k] - p[s])
                    step = (TIME_STEP / 12.0) * jac + (0.5 * TIME_STEP * BETA) * zonal[k]
                    if layer == 1:
                        lap = (p[n] + p[s]) + (pe[k] + pw[k]) - 4.0 * p[k]
                        step = step + (TIME_STEP * DRAG[1]) * lap
                    b_ref[layer, at(level, first + k, t), :] = step - q[k]

    row_blocks(low, high, block, body)


def inner_kernel(level, coarse, rows, ext, e_ref, w_ref, b_ref, v_one, v_two, bc_ref):
    low, high = HALO, HALO + rows
    shift_rows(level, ext, e_ref, w_ref, low, high, 4)
    advance_rows(level, b_ref, ext, e_ref, w_ref, low + 1, high - 1, 2)
    sweep(level, v_one, 0, ext, 0, b_ref, 0, low + 2, high - 2, 4)
    sweep(level, v_two, 0, v_one, 0, b_ref, 0, low + 3, high - 3, 4)
    restrict(level, bc_ref, 0, coarse, v_two, HALO, b_ref, HALO, 2, rows // 2 - 2, 2)


def outer_kernel(level, coarse, rows, *refs):
    near_ref, far_ref = refs[7:9]
    ext, e_ref, w_ref, b_ref, v_one, v_two, bc_ref, bc_near_ref, bc_far_ref = refs[9:]
    _, _, is_first, is_last = place()
    low, high = HALO, HALO + rows
    total = rows + 2 * HALO
    receive_edges(level, HALO, HALO, rows, ext, near_ref, far_ref)
    shift_rows(level, ext, e_ref, w_ref, 0, low, 3)
    shift_rows(level, ext, e_ref, w_ref, high, total, 3)
    advance_rows(level, b_ref, ext, e_ref, w_ref, 1, low + 1, 3)
    advance_rows(level, b_ref, ext, e_ref, w_ref, high - 1, total - 1, 3)
    sweep(level, v_one, 0, ext, 0, b_ref, 0, 1, low + 2, 4)
    sweep(level, v_one, 0, ext, 0, b_ref, 0, high - 2, total - 1, 4)

    def trim(ref):
        @pl.when(is_first)
        def _():
            clear(ref, level, 0, HALO)

        @pl.when(is_last)
        def _():
            clear(ref, level, high, total)

    trim(v_one)
    sweep(level, v_two, 0, v_one, 0, b_ref, 0, 2, low + 3, 4)
    sweep(level, v_two, 0, v_one, 0, b_ref, 0, high - 3, total - 2, 4)
    trim(v_two)
    half = rows // 2
    restrict(level, bc_ref, 0, coarse, v_two, HALO, b_ref, HALO, 0, 2, 2)
    restrict(level, bc_ref, 0, coarse, v_two, HALO, b_ref, HALO, half - 2, half, 2)
    send_edges(coarse, MID_HALO, 0, half, bc_ref, bc_near_ref, bc_far_ref)


def emit_kernel(level, rows, b_ref, next_ref, native, sems):
    copies = []
    for layer in range(2):
        for group in range(rows // SUBS):
            rows_of = pl.ds(group * SUBS, SUBS)
            to_native(level, native, group * SUBS, b_ref, layer, HALO + group * SUBS, -1)
            copies.append(
                pltpu.make_async_copy(
                    native.at[layer, rows_of], next_ref.at[layer, rows_of],
                    sems.at[layer, group],
                )
            )
            copies[-1].start()
    for copy in copies:
        copy.wait()


def middle_kernel(
    fine, level, two, three, rows, b_own, near_ref, far_ref, v0_ref,
    b_ref, v_ref, b2_ref, v2_ref, out_ref, two_near_ref, two_far_ref,
    v_one, w_two, b3,
):
    _, odd, is_first, is_last = place()
    total = rows + 2 * MID_HALO
    own = rows // 2
    edge = MID_HALO * level.size
    b_ref[:, edge : edge + rows * level.size, :] = b_own[...]
    receive_edges(level, MID_HALO, MID_HALO, rows, b_ref, near_ref, far_ref)
    start(level, v_one, 0, b_ref, 0, 0, total, 4)

    def trim(ref, of, halo, n):
        @pl.when(is_first)
        def _():
            clear(ref, of, 0, halo)

        @pl.when(is_last)
        def _():
            clear(ref, of, halo + n, 2 * halo + n)

    trim(v_one, level, MID_HALO, rows)
    sweep(level, v_ref, 0, v_one, 0, b_ref, 0, 1, total - 1, 6)
    trim(v_ref, level, MID_HALO, rows)
    restrict(
        level, b2_ref, TWO_HALO, two, v_ref, MID_HALO, b_ref, MID_HALO, -2, own + 2, 4
    )
    start(two, w_two, TWO_HALO, b2_ref, TWO_HALO, -2, own + 2, 8)
    trim(w_two, two, TWO_HALO, own)
    sweep(two, v2_ref, TWO_HALO, w_two, TWO_HALO, b2_ref, TWO_HALO, -1, own + 1, 6)
    trim(v2_ref, two, TWO_HALO, own)
    restrict(
        two, b3, 0, three, v2_ref, TWO_HALO, b2_ref, TWO_HALO, 0, own // 2, 2
    )
    even = lane_index() % 2 == 0
    for layer in range(2):
        for pair in range(own // 4):
            row = jnp.where(
                even,
                b3[layer, at(three, 2 * pair), :],
                b3[layer, at(three, 2 * pair + 1), :],
            )
            for copy in range(out_ref.shape[0]):
                out_ref[copy, layer, at(three, pair), :] = row
    up, down = pl.ds((TWO_HALO + 1) * two.size, 3 * two.size), pl.ds(
        own * two.size, 3 * two.size
    )
    up_b, down_b = at(two, TWO_HALO + 2), at(two, TWO_HALO + own - 3)
    last = pl.ds(3 * two.size, two.size)

    tail = pl.ds(4 * two.size, fine.size)
    up_0 = pl.ds((HALO + 1) * fine.size, fine.size)
    down_0 = pl.ds((HALO + 2 * rows - 2) * fine.size, fine.size)

    def send(ref, rows_v, row_b, row_0):
        ref[:, 0 : 3 * two.size, :] = v2_ref[:, rows_v, :]
        ref[:, last, :] = b2_ref[:, row_b, :]
        ref[:, tail, :] = v0_ref[:, row_0, :]

    @pl.when(odd == 1)
    def _():
        send(two_near_ref, up, up_b, up_0)
        send(two_far_ref, down, down_b, down_0)

    @pl.when(odd == 0)
    def _():
        send(two_near_ref, down, down_b, down_0)
        send(two_far_ref, up, up_b, up_0)


PAD = 4


def coarse_solve(level, dst, dst_at, b_ref, n):
    groups = level.stride
    m = n // groups
    part = lane_index() % groups
    source = []
    for layer in range(2):
        source.append([])
        for k in range(m):
            tile = load(b_ref, level, layer, k)[0]
            for g in range(1, groups):
                tile = jnp.where(part == g, load(b_ref, level, layer, g * m + k)[0], tile)
            source[layer].append(level.src[layer] * tile)
    values = source
    for _ in range(COARSE_SWEEPS - 1):
        new = []
        for layer in range(2):
            v, o = values[layer], values[1 - layer]
            below = jnp.where(part == groups - 1, 0.0, pltpu.roll(v[0], LANES - 1, 1))
            above = jnp.where(part == 0, 0.0, pltpu.roll(v[-1], 1, 1))
            out = []
            for k in range(m):
                n_row = v[k + 1] if k + 1 < m else below
                s_row = v[k - 1] if k else above
                e, w = east([v[k]], groups)[0], west([v[k]], groups)[0]
                out.append(
                    (level.keep * v[k] + level.near[layer] * ((n_row + s_row) + (e + w)))
                    + (level.other[layer] * o[k] + source[layer][k])
                )
            new.append(out)
        values = new
    for layer in range(2):
        for k in range(m):
            moved = {
                d: pltpu.roll(values[layer][k], d % LANES, 1) if d else values[layer][k]
                for d in range(1 - groups, groups)
            }
            for g in range(groups):
                tile = moved[-g]
                for j in range(1, groups):
                    tile = jnp.where(part == j, moved[j - g], tile)
                dst[layer, at(level, dst_at + g * m + k), :] = tile


def coarse_kernel(levels, rows, same_ref, other_ref, out_ref, b3, v3, w3, b4, v4):
    me, odd, is_first, is_last = place()
    three, four = levels
    own = rows // 4
    chips = same_ref.shape[0]
    n3, n4 = chips * own, chips * own // 2
    for ref, level, n in ((b3, three, n3), (v3, three, n3), (w3, three, n3), (v4, four, n4)):
        clear(ref, level, 0, PAD)
        clear(ref, level, PAD + n, 2 * PAD + n)
    even = lane_index() % 2 == 0

    def gather_body(chip, carry):
        for ref, core in ((same_ref, odd), (other_ref, 1 - odd)):
            row = (2 * chip + core) * (own // 2) + PAD
            for layer in range(2):
                for pair in range(own // 4):
                    both = ref[chip, layer, at(three, pair), :]
                    first = jnp.where(even, both, pltpu.roll(both, 1, 1))
                    second = jnp.where(even, pltpu.roll(both, LANES - 1, 1), both)
                    b3[layer, at(three, row + 2 * pair), :] = first
                    b3[layer, at(three, row + 2 * pair + 1), :] = second
        return carry

    lax.fori_loop(0, chips, gather_body, 0, unroll=min(chips, 8))

    start(three, v3, PAD, b3, PAD, 0, n3, 8)
    sweep(three, w3, PAD, v3, PAD, b3, PAD, 0, n3, 16)
    restrict(three, b4, 0, four, w3, PAD, b3, PAD, 0, n4, 8)
    coarse_solve(four, v4, PAD, b4, n4)

    def trim(ref, level, n):
        @pl.when(me < 2)
        def _():
            clear(ref, level, 0, PAD)

        @pl.when(me >= 2 * chips - 2)
        def _():
            clear(ref, level, PAD + n, 2 * PAD + n)

    half, quarter = own // 2, own // 4
    correct(three, four, v3, PAD, w3, PAD, v4, PAD, me * quarter - 2, quarter + 4, 8)
    sweep(three, w3, PAD, v3, PAD, b3, PAD, me * half - 3, half + 6, 8)
    trim(w3, three, n3)
    sweep(three, out_ref, 2 - me * half, w3, PAD, b3, PAD, me * half - 2, half + 4, 8)

    @pl.when(is_first)
    def _():
        clear(out_ref, three, 0, 2)

    @pl.when(is_last)
    def _():
        clear(out_ref, three, half + 2, half + 4)


def rise_kernel(
    levels, rows, v3_ref, near_ref, far_ref,
    b2_ref, v2_ref, b1_ref, v1_ref, b0_ref, v0_in, out_ref, v0_ref,
    b2, v2, x2, y2, x1, y1, x0, y0, z0, native, sems,
):
    _, odd, is_first, is_last = place()
    fine, mid, two, three = levels
    own = rows // 4

    b2[...] = b2_ref[...]
    v2[...] = v2_ref[...]

    def take(ref, zero):
        top_v, low_v = pl.ds(0, 3 * two.size), pl.ds((TWO_HALO + own + 1) * two.size, 3 * two.size)
        top_b, low_b = at(two, TWO_HALO - 3), at(two, TWO_HALO + own + 2)
        last = pl.ds(3 * two.size, two.size)

        tail = pl.ds(4 * two.size, fine.size)
        top_0 = pl.ds((HALO - 2) * fine.size, fine.size)
        low_0 = pl.ds((HALO + rows + 1) * fine.size, fine.size)

        def drop(values):
            return values if zero is None else jnp.where(zero, 0.0, values)

        def put(rows_v, row_b, row_0):
            v2[:, rows_v, :] = drop(ref[:, 0 : 3 * two.size, :])
            b2[:, row_b, :] = ref[:, last, :]
            v0_ref[:, row_0, :] = drop(ref[:, tail, :])

        return lambda: put(top_v, top_b, top_0), lambda: put(low_v, low_b, low_0)

    near_top, near_low = take(near_ref, None)
    far_top, far_low = take(far_ref, jnp.logical_or(is_first, is_last))

    @pl.when(odd == 1)
    def _():
        near_top()
        far_low()

    @pl.when(odd == 0)
    def _():
        near_low()
        far_top()

    def trim_own(ref, level, halo, n):
        @pl.when(is_first)
        def _():
            clear(ref, level, 0, halo)

        @pl.when(is_last)
        def _():
            clear(ref, level, halo + n, 2 * halo + n)

    total = own + 2 * TWO_HALO
    correct(two, three, x2, 0, v2, 0, v3_ref, 0, 0, total // 2, 8)
    sweep(two, y2, 0, x2, 0, b2, 0, 1, total - 1, 10)
    trim_own(y2, two, TWO_HALO, own)
    sweep(two, x2, 0, y2, 0, b2, 0, 2, total - 2, 8)
    trim_own(x2, two, TWO_HALO, own)

    n1 = rows // 2
    total = n1 + 2 * MID_HALO

    correct(
        mid, two, x1, MID_HALO - 4, v1_ref, MID_HALO - 4, x2, TWO_HALO - 2, 0, n1 // 2 + 4, 4
    )
    sweep(mid, y1, 0, x1, 0, b1_ref, 0, MID_HALO - 2, MID_HALO + n1 + 2, 6)
    trim_own(y1, mid, MID_HALO, n1)
    sweep(mid, x1, 0, y1, 0, b1_ref, 0, MID_HALO - 1, MID_HALO + n1 + 1, 5)
    trim_own(x1, mid, MID_HALO, n1)

    low, done, swept = HALO, 0, HALO - 1
    copies = []
    for group in range(rows // SUBS):
        first_row = low + group * SUBS
        rows_of = pl.ds(group * SUBS, SUBS)
        ready = SUBS // 2 * (group + 1) + 2
        correct(fine, mid, x0, HALO - 2, v0_ref, HALO - 2, x1, MID_HALO - 1, done, ready, 2)
        sweep(fine, y0, 0, x0, 0, b0_ref, 0, swept, first_row + SUBS + 1, 5 - group)
        trim_own(y0, fine, HALO, rows)
        done, swept = ready, first_row + SUBS + 1
        sweep(fine, z0, 0, y0, 0, b0_ref, 0, first_row, first_row + SUBS, 4)
        for layer in range(2):
            to_native(fine, native, group * SUBS, z0, layer, first_row)
            copies.append(
                pltpu.make_async_copy(
                    native.at[layer, rows_of], out_ref.at[layer, rows_of],
                    sems.at[layer, group],
                )
            )
            copies[-1].start()
    for copy in copies:
        copy.wait()


def shape(*dims):
    return jax.ShapeDtypeStruct(dims, jnp.float32)


def scratch(layers, rows, level):
    return pltpu.VMEM((layers, rows * level.size, LANES), jnp.float32)


HBM = pl.BlockSpec(memory_space=pltpu.HBM)
VMEM = pl.BlockSpec(memory_space=pltpu.VMEM)


def call(kernel, out_shape, scratch_shapes=(), cost=None, limit=24, **options):
    if cost is not None:
        cost = pl.CostEstimate(flops=cost, bytes_accessed=cost // 8, transcendentals=0)
    return pl.pallas_call(
        kernel,
        out_shape=out_shape,
        scratch_shapes=list(scratch_shapes),
        cost_estimate=cost,
        compiler_params=pltpu.CompilerParams(vmem_limit_bytes=limit * 1024 * 1024),
        **options,
    )


def shards(stream_now, vorticity):
    _, rows, columns = stream_now.shape
    count = lax.axis_size("wide")
    tiles = columns // (SUBS * LANES)
    fine, mid = Level(0, tiles, 1), Level(1, tiles // 2, 1)
    two, three, four = Level(2, tiles // 4, 1), Level(3, tiles // 4, 2), Level(4, tiles // 4, 4)
    core_swap = [(i, i ^ 1) for i in range(count)]
    members = lax.axis_size("member")
    inside = [(i, ((i + 1) ^ 1) - 1) for i in range(1, count - 1)]
    if members % 2:
        ends = [(0, count - 1), (count - 1, 0)]
        chip_swap = [(m * count + i, m * count + j) for m in range(members) for i, j in ends]
    else:
        chip_swap = [
            (m * count + i, (m ^ 1) * count + i) for m in range(members) for i in (0, count - 1)
        ]
    chip_swap += [(m * count + i, m * count + j) for m in range(members) for i, j in inside]
    groups = rows // SUBS

    def exchange(near, far):
        far = lax.ppermute(far, ("member", "wide"), chip_swap)
        near = lax.ppermute(near, "wide", core_swap)
        return near, far

    half, quarter = rows // 2, rows // 4
    total = rows + 2 * HALO
    ext, near, far = call(
        functools.partial(pack_kernel, fine, rows),
        [shape(4, total * fine.size, LANES)] + [shape(4, HALO * fine.size, LANES)] * 2,
        [pltpu.VMEM((4, rows, columns), jnp.float32), pltpu.SemaphoreType.DMA((4,))],
        in_specs=[HBM, HBM],
    )(*(pltpu.with_memory_space_constraint(x, pltpu.HBM) for x in (stream_now, vorticity)))
    near, far = exchange(near, far)
    state = [
        shape(4, total * fine.size, LANES),
        shape(4, total * fine.size, LANES),
        shape(2, total * fine.size, LANES),
        shape(2, total * fine.size, LANES),
        shape(2, total * fine.size, LANES),
        shape(2, half * mid.size, LANES),
    ]
    inner = call(
        functools.partial(inner_kernel, fine, mid, rows),
        state,
        cost=8000000,
    )(ext)
    edge = shape(2, MID_HALO * mid.size, LANES)
    outer = call(
        functools.partial(outer_kernel, fine, mid, rows),
        [shape(4, total * fine.size, LANES)] + state + [edge, edge],
        input_output_aliases={i: i for i in range(7)},
    )(ext, *inner, near, far)
    b0, v0, b1, near, far = outer[3], outer[5], outer[6], outer[7], outer[8]
    near, far = exchange(near, far)
    vorticity_next = call(
        functools.partial(emit_kernel, fine, rows),
        shape(2, rows, columns),
        [pltpu.VMEM((2, rows, columns), jnp.float32), pltpu.SemaphoreType.DMA((2, groups))],
        cost=4000000,
        out_specs=HBM,
    )(b0)
    chips = count // 2
    eighth = rows // 8
    two_edge = shape(2, 4 * two.size + fine.size, LANES)
    two_all = shape(2, (quarter + 2 * TWO_HALO) * two.size, LANES)
    b1, v1, b2, v2, b3, near, far = call(
        functools.partial(middle_kernel, fine, mid, two, three, half),
        [
            shape(2, (half + 2 * MID_HALO) * mid.size, LANES),
            shape(2, (half + 2 * MID_HALO) * mid.size, LANES),
            two_all,
            two_all,
            shape(chips, 2, eighth // 2 * three.size, LANES),
            two_edge,
            two_edge,
        ],
        [
            scratch(2, half + 2 * MID_HALO, mid),
            scratch(2, quarter + 2 * TWO_HALO, two),
            scratch(2, eighth, three),
        ],
    )(b1, near, far, v0)
    cores = [[i for i in range(count) if i % 2 == c] for c in range(2)]
    same = lax.all_to_all(b3, "wide", 0, 0, axis_index_groups=cores)
    other = lax.ppermute(same, "wide", core_swap)
    near, far = exchange(near, far)
    n3, n4 = count * eighth, count * eighth // 2
    v3 = call(
        functools.partial(coarse_kernel, (three, four), rows),
        shape(2, (eighth + 4) * three.size, LANES),
        [scratch(2, n3 + 2 * PAD, three)] * 3
        + [scratch(2, n4, four), scratch(2, n4 + 2 * PAD, four)],
        cost=5000000,
    )(same, other)
    stream_next, _ = call(
        functools.partial(rise_kernel, (fine, mid, two, three), rows),
        [shape(2, rows, columns), shape(2, total * fine.size, LANES)],
        [scratch(2, quarter + 2 * TWO_HALO, two)] * 4
        + [scratch(2, half + 2 * MID_HALO, mid)] * 2
        + [scratch(2, total, fine)] * 3
        + [pltpu.VMEM((2, rows, columns), jnp.float32), pltpu.SemaphoreType.DMA((2, groups))],
        out_specs=[HBM, VMEM],
        input_output_aliases={8: 1},
    )(v3, near, far, b2, v2, b1, v1, b0, v0)
    return (vorticity_next, stream_next)


def solution(mesh):
    return jax.shard_map(
        shards,
        mesh=mesh,
        in_specs=(P("member", "wide", None), P("member", "wide", None)),
        out_specs=(P("member", "wide", None), P("member", "wide", None)),
        check_vma=False,
    )
```

```python
import functools

import jax
import jax.numpy as jnp
from jax import lax
from jax.experimental import pallas as pl
from jax.experimental.pallas import tpu as pltpu
from jax.sharding import PartitionSpec as P


LANES = 128
SUBS = 8
HALO = 3
MID_HALO = 6
TWO_HALO = 4
RELAX = 0.8
COUPLING = (0.02, 0.04)
TIME_STEP = 0.5
BETA = 0.05
DRAG = (0.0, 0.02)
COARSE_SWEEPS = 8


class Level:
    def __init__(self, level, tiles, stride):
        h2 = (2.0**level) ** 2
        self.tiles, self.stride = tiles, stride
        diag = [4.0 / h2 + f for f in COUPLING]
        self.keep = 1.0 - RELAX
        self.near = [RELAX / (d * h2) for d in diag]
        self.other = [RELAX * f / d for f, d in zip(COUPLING, diag)]
        self.src = [RELAX / d for d in diag]
        self.diag = diag
        self.inv_h2 = 1.0 / h2
        self.size = tiles * SUBS


def lane_index():
    return lax.broadcasted_iota(jnp.int32, (SUBS, LANES), 1)


def at(level, row, tile=0):
    base = row * level.size
    if not isinstance(row, int):
        base = pl.multiple_of(base, SUBS)
    return pl.ds(base + tile * SUBS, SUBS)


def load(ref, level, layer, row):
    return [ref[layer, at(level, row, t), :] for t in range(level.tiles)]


def store(ref, level, layer, row, values):
    for t in range(level.tiles):
        ref[layer, at(level, row, t), :] = values[t]


def east(values, stride=1):
    rolled = [pltpu.roll(v, LANES - stride, 1) for v in values]
    after = rolled[1:] + [pltpu.roll(rolled[0], SUBS - 1, 0)]
    edge = lane_index() >= LANES - stride
    return [jnp.where(edge, a, r) for a, r in zip(after, rolled)]


def west(values, stride=1):
    rolled = [pltpu.roll(v, stride, 1) for v in values]
    before = [pltpu.roll(rolled[-1], 1, 0)] + rolled[:-1]
    edge = lane_index() < stride
    return [jnp.where(edge, b, r) for b, r in zip(before, rolled)]


def transpose_tiles(tiles):
    sub = lax.broadcasted_iota(jnp.int32, (SUBS, LANES), 0)
    for k in (1, 2, 4):
        keep = (sub & k) == 0
        out = list(tiles)
        for i in range(SUBS):
            if not i & k:
                a, b = tiles[i], tiles[i + k]
                out[i] = jnp.where(keep, a, pltpu.roll(b, k, 0))
                out[i + k] = jnp.where(keep, pltpu.roll(a, SUBS - k, 0), b)
        tiles = out
    return tiles


def column_of(level, t, s):
    first = (s * level.tiles + t) * LANES
    return slice(first, first + LANES)


def to_native(level, dst, dst_row, src, layer, src_row, sign=1):
    for t in range(level.tiles):
        tiles = [src[layer, at(level, src_row + r, t), :] for r in range(SUBS)]
        for s, tile in enumerate(transpose_tiles(tiles)):
            dst[layer, dst_row : dst_row + SUBS, column_of(level, t, s)] = (
                tile if sign > 0 else -tile
            )


def row_blocks(low, high, block, body):
    count = high - low if isinstance(low, int) else high
    whole = count // block
    if whole > 1:
        lax.fori_loop(0, whole, lambda i, c: (body(low + i * block, block), c)[1], 0)
    elif whole == 1:
        body(low, block)
    if count % block:
        body(low + whole * block, count % block)


def star(rows, k, layer, level, sides=None):
    centre = rows[k][layer]
    if sides:
        e, w = sides[0][k][layer], sides[1][k][layer]
    else:
        e, w = east(centre, level.stride), west(centre, level.stride)
    return [
        (n + s) + (a + b)
        for n, s, a, b in zip(rows[k + 1][layer], rows[k - 1][layer], e, w)
    ]


def load_rows(ref, level, first, count, margin=1):
    return {
        k: [load(ref, level, layer, first + k) for layer in range(2)]
        for k in range(-margin, count + margin)
    }


def sweep_rows(level, rows, source, count, sides=None):
    out = {}
    for k in range(count):
        out[k] = []
        for layer in range(2):
            near = star(rows, k, layer, level, sides)
            out[k].append(
                [
                    (level.keep * c + level.near[layer] * n)
                    + (level.other[layer] * o + level.src[layer] * b)
                    for c, n, o, b in zip(
                        rows[k][layer], near, rows[k][1 - layer], source[k][layer]
                    )
                ]
            )
    return out


def residual_rows(level, rows, source, count):
    out = {}
    for k in range(count):
        out[k] = []
        for layer in range(2):
            near = star(rows, k, layer, level)
            out[k].append(
                [
                    (b - level.diag[layer] * c)
                    + (level.inv_h2 * n + COUPLING[layer] * o)
                    for c, n, o, b in zip(
                        rows[k][layer], near, rows[k][1 - layer], source[k][layer]
                    )
                ]
            )
    return out


def store_rows(ref, level, first, rows, count):
    for k in range(count):
        for layer in range(2):
            store(ref, level, layer, first + k, rows[k][layer])


def sweep(level, dst, dst_at, src, src_at, b, b_at, low, high, block, shifted=None):
    def body(first, count):
        rows = load_rows(src, level, first + src_at, count)
        source = load_rows(b, level, first + b_at, count, 0)
        sides = None
        if shifted:
            sides = [load_rows(ref, level, first + src_at, count, 0) for ref in shifted]
        out = sweep_rows(level, rows, source, count, sides)
        store_rows(dst, level, first + dst_at, out, count)

    row_blocks(low, high, block, body)


def start(level, dst, dst_at, b, b_at, low, high, block):
    def body(first, count):
        source = load_rows(b, level, first + b_at, count, 0)
        out = {
            k: [[level.src[l] * x for x in source[k][l]] for l in range(2)]
            for k in range(count)
        }
        store_rows(dst, level, first + dst_at, out, count)

    row_blocks(low, high, block, body)


def pack_columns(values):
    lane = lane_index()
    pick = (2 * lane) % LANES
    sums = [v + pltpu.roll(v, LANES - 1, 1) for v in values]
    picked = [jnp.take_along_axis(s, pick, axis=1) for s in sums]
    return [
        jnp.where(lane < LANES // 2, picked[2 * t], picked[2 * t + 1])
        for t in range(len(values) // 2)
    ]


def spread_columns(values):
    lane = lane_index()
    out = []
    for v in values:
        out.append(jnp.take_along_axis(v, lane // 2, axis=1))
        out.append(jnp.take_along_axis(v, LANES // 2 + lane // 2, axis=1))
    return out


def merge_columns(values, stride):
    even = (lane_index() // stride) % 2 == 0
    return [
        v + jnp.where(even, pltpu.roll(v, LANES - stride, 1), pltpu.roll(v, stride, 1))
        for v in values
    ]


def restrict(fine, dst, dst_at, coarse, src, src_at, b, b_at, low, high, block):
    def body(first, count):
        rows = load_rows(src, fine, 2 * first + src_at, 2 * count)
        source = load_rows(b, fine, 2 * first + b_at, 2 * count, 0)
        res = residual_rows(fine, rows, source, 2 * count)
        out = {}
        for k in range(count):
            out[k] = []
            for layer in range(2):
                pair = [x + y for x, y in zip(res[2 * k][layer], res[2 * k + 1][layer])]
                if coarse.tiles < fine.tiles:
                    pair = pack_columns(pair)
                else:
                    pair = merge_columns(pair, fine.stride)
                out[k].append([0.25 * x for x in pair])
        store_rows(dst, coarse, first + dst_at, out, count)

    row_blocks(low, high, block, body)


def correct(fine, coarse, dst, dst_at, src, src_at, add, add_at, low, high, block):
    def body(first, count):
        coarse_rows = load_rows(add, coarse, first + add_at, count, 0)
        fine_rows = load_rows(src, fine, 2 * first + src_at, 2 * count, 0)
        out = {}
        for k in range(count):
            spread = [
                spread_columns(v) if coarse.tiles < fine.tiles else v for v in coarse_rows[k]
            ]
            for half in range(2):
                out[2 * k + half] = [
                    [x + y for x, y in zip(fine_rows[2 * k + half][l], spread[l])]
                    for l in range(2)
                ]
        store_rows(dst, fine, 2 * first + dst_at, out, 2 * count)

    row_blocks(low, high, block, body)


def clear(ref, level, low, high):
    ref[:, low * level.size : high * level.size, :] = jnp.zeros(
        (ref.shape[0], (high - low) * level.size, LANES), jnp.float32
    )


def place():
    me, count = lax.axis_index("wide"), lax.axis_size("wide")
    return me, lax.rem(me, 2), me == 0, me == count - 1


def pack_kernel(level, rows, p_ref, q_ref, ext_ref, near_ref, far_ref, native, sems):
    copies = []
    for field, ref in enumerate((p_ref, q_ref)):
        for layer in range(2):
            which = 2 * field + layer
            copies.append(
                pltpu.make_async_copy(ref.at[layer], native.at[which], sems.at[which])
            )
            copies[-1].start()
    for which in range(4):
        copies[which].wait()
        for group in range(rows // SUBS):
            for t in range(level.tiles):
                tiles = [
                    native[which, group * SUBS : (group + 1) * SUBS, column_of(level, t, s)]
                    for s in range(SUBS)
                ]
                for r, tile in enumerate(transpose_tiles(tiles)):
                    ext_ref[which, at(level, HALO + group * SUBS + r, t), :] = tile
    send_edges(level, HALO, HALO, rows, ext_ref, near_ref, far_ref)


def send_edges(level, width, src_at, rows, src, near_ref, far_ref):
    _, odd, _, _ = place()
    size = width * level.size
    last = (src_at + rows - width) * level.size
    top = src_at * level.size
    near = pl.multiple_of(jnp.where(odd == 1, top, last), SUBS)
    far = pl.multiple_of(jnp.where(odd == 1, last, top), SUBS)
    near_ref[:, 0:size, :] = src[:, pl.ds(near, size), :]
    far_ref[:, 0:size, :] = src[:, pl.ds(far, size), :]


def receive_edges(level, width, dst_at, rows, dst, near_ref, far_ref):
    _, odd, first, last = place()
    size = width * level.size
    low = (dst_at + rows) * level.size
    top = (dst_at - width) * level.size
    near = pl.multiple_of(jnp.where(odd == 1, top, low), SUBS)
    far = pl.multiple_of(jnp.where(odd == 1, low, top), SUBS)
    dst[:, pl.ds(near, size), :] = near_ref[:, 0:size, :]
    outside = jnp.logical_or(first, last)
    dst[:, pl.ds(far, size), :] = jnp.where(outside, 0.0, far_ref[:, 0:size, :])


def shift_rows(level, ext, e_ref, w_ref, low, high, block):
    def body(first, count):
        for k in range(count):
            for f in range(4):
                v = load(ext, level, f, first + k)
                store(e_ref, level, f, first + k, east(v))
                store(w_ref, level, f, first + k, west(v))

    row_blocks(low, high, block, body)


def advance_rows(level, b_ref, ext, e_ref, w_ref, low, high, block):
    def body(first, count):
        for layer in range(2):
            for t in range(level.tiles):
                def grab(ref, field):
                    return {
                        k: ref[2 * field + layer, at(level, first + k, t), :]
                        for k in range(-1, count + 1)
                    }

                p, pe, pw = grab(ext, 0), grab(e_ref, 0), grab(w_ref, 0)
                q, qe, qw = grab(ext, 1), grab(e_ref, 1), grab(w_ref, 1)
                zonal = {k: pe[k] - pw[k] for k in p}
                for k in range(count):
                    n, s = k + 1, k - 1
                    v0, ve, vw = p[n] - p[s], pe[n] - pe[s], pw[n] - pw[s]
                    jac = q[n] * (zonal[k] + zonal[n]) - q[s] * (zonal[k] + zonal[s])
                    jac = jac - qe[k] * (v0 + ve) + qw[k] * (v0 + vw)
                    jac = jac + qe[n] * (pe[k] - p[n]) - qe[s] * (pe[k] - p[s])
                    jac = jac - qw[n] * (pw[k] - p[n]) + qw[s] * (pw[k] - p[s])
                    step = (TIME_STEP / 12.0) * jac + (0.5 * TIME_STEP * BETA) * zonal[k]
                    if layer == 1:
                        lap = (p[n] + p[s]) + (pe[k] + pw[k]) - 4.0 * p[k]
                        step = step + (TIME_STEP * DRAG[1]) * lap
                    b_ref[layer, at(level, first + k, t), :] = step - q[k]

    row_blocks(low, high, block, body)


def inner_kernel(level, coarse, rows, ext, e_ref, w_ref, b_ref, v_one, v_two, bc_ref):
    low, high = HALO, HALO + rows
    shift_rows(level, ext, e_ref, w_ref, low, high, 4)
    advance_rows(level, b_ref, ext, e_ref, w_ref, low + 1, high - 1, 2)
    sweep(level, v_one, 0, ext, 0, b_ref, 0, low + 2, high - 2, 4, (e_ref, w_ref))
    sweep(level, v_two, 0, v_one, 0, b_ref, 0, low + 3, high - 3, 4)
    restrict(level, bc_ref, 0, coarse, v_two, HALO, b_ref, HALO, 2, rows // 2 - 2, 2)


def outer_kernel(level, coarse, rows, *refs):
    near_ref, far_ref = refs[7:9]
    ext, e_ref, w_ref, b_ref, v_one, v_two, bc_ref, bc_near_ref, bc_far_ref = refs[9:]
    _, _, is_first, is_last = place()
    low, high = HALO, HALO + rows
    total = rows + 2 * HALO
    receive_edges(level, HALO, HALO, rows, ext, near_ref, far_ref)
    shift_rows(level, ext, e_ref, w_ref, 0, low, 3)
    shift_rows(level, ext, e_ref, w_ref, high, total, 3)
    advance_rows(level, b_ref, ext, e_ref, w_ref, 1, low + 1, 3)
    advance_rows(level, b_ref, ext, e_ref, w_ref, high - 1, total - 1, 3)
    sweep(level, v_one, 0, ext, 0, b_ref, 0, 1, low + 2, 4, (e_ref, w_ref))
    sweep(level, v_one, 0, ext, 0, b_ref, 0, high - 2, total - 1, 4, (e_ref, w_ref))

    def trim(ref):
        @pl.when(is_first)
        def _():
            clear(ref, level, 0, HALO)

        @pl.when(is_last)
        def _():
            clear(ref, level, high, total)

    trim(v_one)
    sweep(level, v_two, 0, v_one, 0, b_ref, 0, 2, low + 3, 4)
    sweep(level, v_two, 0, v_one, 0, b_ref, 0, high - 3, total - 2, 4)
    trim(v_two)
    half = rows // 2
    restrict(level, bc_ref, 0, coarse, v_two, HALO, b_ref, HALO, 0, 2, 2)
    restrict(level, bc_ref, 0, coarse, v_two, HALO, b_ref, HALO, half - 2, half, 2)
    send_edges(coarse, MID_HALO, 0, half, bc_ref, bc_near_ref, bc_far_ref)


def emit(level, rows, b_ref, next_ref, native, sems):
    copies = []
    for layer in range(2):
        for group in range(rows // SUBS):
            rows_of = pl.ds(group * SUBS, SUBS)
            to_native(level, native, group * SUBS, b_ref, layer, HALO + group * SUBS, -1)
            copies.append(
                pltpu.make_async_copy(
                    native.at[layer, rows_of], next_ref.at[layer, rows_of],
                    sems.at[layer, group],
                )
            )
            copies[-1].start()
    return copies


def middle_kernel(
    fine, level, two, three, rows, b_own, near_ref, far_ref, v0_ref,
    b_ref, v_ref, b2_ref, v2_ref, out_ref, two_near_ref, two_far_ref,
    v_one, w_two, b3,
):
    _, odd, is_first, is_last = place()
    total = rows + 2 * MID_HALO
    own = rows // 2
    edge = MID_HALO * level.size
    b_ref[:, edge : edge + rows * level.size, :] = b_own[...]
    receive_edges(level, MID_HALO, MID_HALO, rows, b_ref, near_ref, far_ref)
    start(level, v_one, 0, b_ref, 0, 0, total, 4)

    def trim(ref, of, halo, n):
        @pl.when(is_first)
        def _():
            clear(ref, of, 0, halo)

        @pl.when(is_last)
        def _():
            clear(ref, of, halo + n, 2 * halo + n)

    trim(v_one, level, MID_HALO, rows)
    sweep(level, v_ref, 0, v_one, 0, b_ref, 0, 1, total - 1, 6)
    trim(v_ref, level, MID_HALO, rows)
    restrict(
        level, b2_ref, TWO_HALO, two, v_ref, MID_HALO, b_ref, MID_HALO, -2, own + 2, 4
    )
    start(two, w_two, TWO_HALO, b2_ref, TWO_HALO, -2, own + 2, 8)
    trim(w_two, two, TWO_HALO, own)
    sweep(two, v2_ref, TWO_HALO, w_two, TWO_HALO, b2_ref, TWO_HALO, -1, own + 1, 6)
    trim(v2_ref, two, TWO_HALO, own)
    restrict(
        two, b3, 0, three, v2_ref, TWO_HALO, b2_ref, TWO_HALO, 0, own // 2, 2
    )
    even = lane_index() % 2 == 0
    for layer in range(2):
        for pair in range(own // 4):
            row = jnp.where(
                even,
                b3[layer, at(three, 2 * pair), :],
                b3[layer, at(three, 2 * pair + 1), :],
            )
            for copy in range(out_ref.shape[0]):
                out_ref[copy, layer, at(three, pair), :] = row
    up, down = pl.ds((TWO_HALO + 1) * two.size, 3 * two.size), pl.ds(
        own * two.size, 3 * two.size
    )
    up_b, down_b = at(two, TWO_HALO + 2), at(two, TWO_HALO + own - 3)
    last = pl.ds(3 * two.size, two.size)

    tail = pl.ds(4 * two.size, fine.size)
    up_0 = pl.ds((HALO + 1) * fine.size, fine.size)
    down_0 = pl.ds((HALO + 2 * rows - 2) * fine.size, fine.size)

    def send(ref, rows_v, row_b, row_0):
        ref[:, 0 : 3 * two.size, :] = v2_ref[:, rows_v, :]
        ref[:, last, :] = b2_ref[:, row_b, :]
        ref[:, tail, :] = v0_ref[:, row_0, :]

    @pl.when(odd == 1)
    def _():
        send(two_near_ref, up, up_b, up_0)
        send(two_far_ref, down, down_b, down_0)

    @pl.when(odd == 0)
    def _():
        send(two_near_ref, down, down_b, down_0)
        send(two_far_ref, up, up_b, up_0)


PAD = 4


def coarse_solve(level, dst, dst_at, b_ref, n):
    groups = level.stride
    m = n // groups
    part = lane_index() % groups
    source = []
    for layer in range(2):
        source.append([])
        for k in range(m):
            tile = load(b_ref, level, layer, k)[0]
            for g in range(1, groups):
                tile = jnp.where(part == g, load(b_ref, level, layer, g * m + k)[0], tile)
            source[layer].append(level.src[layer] * tile)
    values = source
    for _ in range(COARSE_SWEEPS - 1):
        new = []
        for layer in range(2):
            v, o = values[layer], values[1 - layer]
            below = jnp.where(part == groups - 1, 0.0, pltpu.roll(v[0], LANES - 1, 1))
            above = jnp.where(part == 0, 0.0, pltpu.roll(v[-1], 1, 1))
            out = []
            for k in range(m):
                n_row = v[k + 1] if k + 1 < m else below
                s_row = v[k - 1] if k else above
                e, w = east([v[k]], groups)[0], west([v[k]], groups)[0]
                out.append(
                    (level.keep * v[k] + level.near[layer] * ((n_row + s_row) + (e + w)))
                    + (level.other[layer] * o[k] + source[layer][k])
                )
            new.append(out)
        values = new
    for layer in range(2):
        for k in range(m):
            moved = {
                d: pltpu.roll(values[layer][k], d % LANES, 1) if d else values[layer][k]
                for d in range(1 - groups, groups)
            }
            for g in range(groups):
                tile = moved[-g]
                for j in range(1, groups):
                    tile = jnp.where(part == j, moved[j - g], tile)
                dst[layer, at(level, dst_at + g * m + k), :] = tile


def coarse_kernel(
    levels, rows, same_ref, other_ref, b0_ref, out_ref, next_ref,
    b3, v3, w3, b4, v4, native, sems,
):
    me, odd, is_first, is_last = place()
    fine, three, four = levels
    copies = emit(fine, rows, b0_ref, next_ref, native, sems)
    own = rows // 4
    chips = same_ref.shape[0]
    n3, n4 = chips * own, chips * own // 2
    for ref, level, n in ((b3, three, n3), (v3, three, n3), (w3, three, n3), (v4, four, n4)):
        clear(ref, level, 0, PAD)
        clear(ref, level, PAD + n, 2 * PAD + n)
    even = lane_index() % 2 == 0

    def gather_body(chip, carry):
        for ref, core in ((same_ref, odd), (other_ref, 1 - odd)):
            row = (2 * chip + core) * (own // 2) + PAD
            for layer in range(2):
                for pair in range(own // 4):
                    both = ref[chip, layer, at(three, pair), :]
                    first = jnp.where(even, both, pltpu.roll(both, 1, 1))
                    second = jnp.where(even, pltpu.roll(both, LANES - 1, 1), both)
                    b3[layer, at(three, row + 2 * pair), :] = first
                    b3[layer, at(three, row + 2 * pair + 1), :] = second
        return carry

    lax.fori_loop(0, chips, gather_body, 0, unroll=min(chips, 8))

    start(three, v3, PAD, b3, PAD, 0, n3, 8)
    sweep(three, w3, PAD, v3, PAD, b3, PAD, 0, n3, 16)
    restrict(three, b4, 0, four, w3, PAD, b3, PAD, 0, n4, 8)
    coarse_solve(four, v4, PAD, b4, n4)

    def trim(ref, level, n):
        @pl.when(me < 2)
        def _():
            clear(ref, level, 0, PAD)

        @pl.when(me >= 2 * chips - 2)
        def _():
            clear(ref, level, PAD + n, 2 * PAD + n)

    half, quarter = own // 2, own // 4
    correct(three, four, v3, PAD, w3, PAD, v4, PAD, me * quarter - 2, quarter + 4, 8)
    sweep(three, w3, PAD, v3, PAD, b3, PAD, me * half - 3, half + 6, 8)
    trim(w3, three, n3)
    sweep(three, out_ref, 2 - me * half, w3, PAD, b3, PAD, me * half - 2, half + 4, 8)

    @pl.when(is_first)
    def _():
        clear(out_ref, three, 0, 2)

    @pl.when(is_last)
    def _():
        clear(out_ref, three, half + 2, half + 4)

    for copy in copies:
        copy.wait()


def rise_kernel(
    levels, rows, v3_ref, near_ref, far_ref,
    b2_ref, v2_ref, b1_ref, v1_ref, b0_ref, v0_in, out_ref, v0_ref,
    b2, v2, x2, y2, x1, y1, x0, y0, z0, native, sems,
):
    _, odd, is_first, is_last = place()
    fine, mid, two, three = levels
    own = rows // 4

    b2[...] = b2_ref[...]
    v2[...] = v2_ref[...]

    def take(ref, zero):
        top_v, low_v = pl.ds(0, 3 * two.size), pl.ds((TWO_HALO + own + 1) * two.size, 3 * two.size)
        top_b, low_b = at(two, TWO_HALO - 3), at(two, TWO_HALO + own + 2)
        last = pl.ds(3 * two.size, two.size)

        tail = pl.ds(4 * two.size, fine.size)
        top_0 = pl.ds((HALO - 2) * fine.size, fine.size)
        low_0 = pl.ds((HALO + rows + 1) * fine.size, fine.size)

        def drop(values):
            return values if zero is None else jnp.where(zero, 0.0, values)

        def put(rows_v, row_b, row_0):
            v2[:, rows_v, :] = drop(ref[:, 0 : 3 * two.size, :])
            b2[:, row_b, :] = ref[:, last, :]
            v0_ref[:, row_0, :] = drop(ref[:, tail, :])

        return lambda: put(top_v, top_b, top_0), lambda: put(low_v, low_b, low_0)

    near_top, near_low = take(near_ref, None)
    far_top, far_low = take(far_ref, jnp.logical_or(is_first, is_last))

    @pl.when(odd == 1)
    def _():
        near_top()
        far_low()

    @pl.when(odd == 0)
    def _():
        near_low()
        far_top()

    def trim_own(ref, level, halo, n):
        @pl.when(is_first)
        def _():
            clear(ref, level, 0, halo)

        @pl.when(is_last)
        def _():
            clear(ref, level, halo + n, 2 * halo + n)

    total = own + 2 * TWO_HALO
    correct(two, three, x2, 0, v2, 0, v3_ref, 0, 0, total // 2, 8)
    sweep(two, y2, 0, x2, 0, b2, 0, 1, total - 1, 10)
    trim_own(y2, two, TWO_HALO, own)
    sweep(two, x2, 0, y2, 0, b2, 0, 2, total - 2, 8)
    trim_own(x2, two, TWO_HALO, own)

    n1 = rows // 2
    total = n1 + 2 * MID_HALO

    correct(
        mid, two, x1, MID_HALO - 4, v1_ref, MID_HALO - 4, x2, TWO_HALO - 2, 0, n1 // 2 + 4, 4
    )
    sweep(mid, y1, 0, x1, 0, b1_ref, 0, MID_HALO - 2, MID_HALO + n1 + 2, 6)
    trim_own(y1, mid, MID_HALO, n1)
    sweep(mid, x1, 0, y1, 0, b1_ref, 0, MID_HALO - 1, MID_HALO + n1 + 1, 5)
    trim_own(x1, mid, MID_HALO, n1)

    low, done, swept = HALO, 0, HALO - 1
    copies = []
    for group in range(rows // SUBS):
        first_row = low + group * SUBS
        rows_of = pl.ds(group * SUBS, SUBS)
        ready = SUBS // 2 * (group + 1) + 2
        correct(fine, mid, x0, HALO - 2, v0_ref, HALO - 2, x1, MID_HALO - 1, done, ready, 2)
        sweep(fine, y0, 0, x0, 0, b0_ref, 0, swept, first_row + SUBS + 1, 5 - group)
        trim_own(y0, fine, HALO, rows)
        done, swept = ready, first_row + SUBS + 1
        sweep(fine, z0, 0, y0, 0, b0_ref, 0, first_row, first_row + SUBS, 4)
        for layer in range(2):
            to_native(fine, native, group * SUBS, z0, layer, first_row)
            copies.append(
                pltpu.make_async_copy(
                    native.at[layer, rows_of], out_ref.at[layer, rows_of],
                    sems.at[layer, group],
                )
            )
            copies[-1].start()
    for copy in copies:
        copy.wait()


def shape(*dims):
    return jax.ShapeDtypeStruct(dims, jnp.float32)


def scratch(layers, rows, level):
    return pltpu.VMEM((layers, rows * level.size, LANES), jnp.float32)


HBM = pl.BlockSpec(memory_space=pltpu.HBM)
VMEM = pl.BlockSpec(memory_space=pltpu.VMEM)


def call(kernel, out_shape, scratch_shapes=(), cost=None, limit=24, **options):
    if cost is not None:
        cost = pl.CostEstimate(flops=cost, bytes_accessed=cost // 8, transcendentals=0)
    return pl.pallas_call(
        kernel,
        out_shape=out_shape,
        scratch_shapes=list(scratch_shapes),
        cost_estimate=cost,
        compiler_params=pltpu.CompilerParams(vmem_limit_bytes=limit * 1024 * 1024),
        **options,
    )


def shards(stream_now, vorticity):
    _, rows, columns = stream_now.shape
    count = lax.axis_size("wide")
    tiles = columns // (SUBS * LANES)
    fine, mid = Level(0, tiles, 1), Level(1, tiles // 2, 1)
    two, three, four = Level(2, tiles // 4, 1), Level(3, tiles // 4, 2), Level(4, tiles // 4, 4)
    core_swap = [(i, i ^ 1) for i in range(count)]
    members = lax.axis_size("member")
    inside = [(i, ((i + 1) ^ 1) - 1) for i in range(1, count - 1)]
    if members % 2:
        ends = [(0, count - 1), (count - 1, 0)]
        chip_swap = [(m * count + i, m * count + j) for m in range(members) for i, j in ends]
    else:
        chip_swap = [
            (m * count + i, (m ^ 1) * count + i) for m in range(members) for i in (0, count - 1)
        ]
    chip_swap += [(m * count + i, m * count + j) for m in range(members) for i, j in inside]
    groups = rows // SUBS

    def exchange(near, far):
        far = lax.ppermute(far, ("member", "wide"), chip_swap)
        near = lax.ppermute(near, "wide", core_swap)
        return near, far

    half, quarter = rows // 2, rows // 4
    total = rows + 2 * HALO
    ext, near, far = call(
        functools.partial(pack_kernel, fine, rows),
        [shape(4, total * fine.size, LANES)] + [shape(4, HALO * fine.size, LANES)] * 2,
        [pltpu.VMEM((4, rows, columns), jnp.float32), pltpu.SemaphoreType.DMA((4,))],
        in_specs=[HBM, HBM],
    )(*(pltpu.with_memory_space_constraint(x, pltpu.HBM) for x in (stream_now, vorticity)))
    near, far = exchange(near, far)
    state = [
        shape(4, total * fine.size, LANES),
        shape(4, total * fine.size, LANES),
        shape(2, total * fine.size, LANES),
        shape(2, total * fine.size, LANES),
        shape(2, total * fine.size, LANES),
        shape(2, half * mid.size, LANES),
    ]
    inner = call(
        functools.partial(inner_kernel, fine, mid, rows),
        state,
        cost=8000000,
    )(ext)
    edge = shape(2, MID_HALO * mid.size, LANES)
    outer = call(
        functools.partial(outer_kernel, fine, mid, rows),
        [shape(4, total * fine.size, LANES)] + state + [edge, edge],
        input_output_aliases={i: i for i in range(7)},
    )(ext, *inner, near, far)
    b0, v0, b1, near, far = outer[3], outer[5], outer[6], outer[7], outer[8]
    near, far = exchange(near, far)
    chips = count // 2
    eighth = rows // 8
    two_edge = shape(2, 4 * two.size + fine.size, LANES)
    two_all = shape(2, (quarter + 2 * TWO_HALO) * two.size, LANES)
    b1, v1, b2, v2, b3, near, far = call(
        functools.partial(middle_kernel, fine, mid, two, three, half),
        [
            shape(2, (half + 2 * MID_HALO) * mid.size, LANES),
            shape(2, (half + 2 * MID_HALO) * mid.size, LANES),
            two_all,
            two_all,
            shape(chips, 2, eighth // 2 * three.size, LANES),
            two_edge,
            two_edge,
        ],
        [
            scratch(2, half + 2 * MID_HALO, mid),
            scratch(2, quarter + 2 * TWO_HALO, two),
            scratch(2, eighth, three),
        ],
    )(b1, near, far, v0)
    cores = [[i for i in range(count) if i % 2 == c] for c in range(2)]
    same = lax.all_to_all(b3, "wide", 0, 0, axis_index_groups=cores)
    other = lax.ppermute(same, "wide", core_swap)
    near, far = exchange(near, far)
    n3, n4 = count * eighth, count * eighth // 2
    v3, vorticity_next = call(
        functools.partial(coarse_kernel, (fine, three, four), rows),
        [shape(2, (eighth + 4) * three.size, LANES), shape(2, rows, columns)],
        [scratch(2, n3 + 2 * PAD, three)] * 3
        + [scratch(2, n4, four), scratch(2, n4 + 2 * PAD, four)]
        + [pltpu.VMEM((2, rows, columns), jnp.float32), pltpu.SemaphoreType.DMA((2, groups))],
        cost=5000000,
        out_specs=[VMEM, HBM],
    )(same, other, b0)
    stream_next, _ = call(
        functools.partial(rise_kernel, (fine, mid, two, three), rows),
        [shape(2, rows, columns), shape(2, total * fine.size, LANES)],
        [scratch(2, quarter + 2 * TWO_HALO, two)] * 4
        + [scratch(2, half + 2 * MID_HALO, mid)] * 2
        + [scratch(2, total, fine)] * 3
        + [pltpu.VMEM((2, rows, columns), jnp.float32), pltpu.SemaphoreType.DMA((2, groups))],
        out_specs=[HBM, VMEM],
        input_output_aliases={8: 1},
    )(v3, near, far, b2, v2, b1, v1, b0, v0)
    return (vorticity_next, stream_next)


def solution(mesh):
    return jax.shard_map(
        shards,
        mesh=mesh,
        in_specs=(P("member", "wide", None), P("member", "wide", None)),
        out_specs=(P("member", "wide", None), P("member", "wide", None)),
        check_vma=False,
    )
```

```python
import functools

import jax
import jax.numpy as jnp
from jax import lax
from jax.experimental import pallas as pl
from jax.experimental.pallas import tpu as pltpu
from jax.sharding import PartitionSpec as P


LANES = 128
SUBS = 8
HALO = 3
MID_HALO = 6
TWO_HALO = 4
RELAX = 0.8
COUPLING = (0.02, 0.04)
TIME_STEP = 0.5
BETA = 0.05
DRAG = (0.0, 0.02)
COARSE_SWEEPS = 8


class Level:
    def __init__(self, level, tiles, stride):
        h2 = (2.0**level) ** 2
        self.tiles, self.stride = tiles, stride
        diag = [4.0 / h2 + f for f in COUPLING]
        self.keep = 1.0 - RELAX
        self.near = [RELAX / (d * h2) for d in diag]
        self.other = [RELAX * f / d for f, d in zip(COUPLING, diag)]
        self.src = [RELAX / d for d in diag]
        self.diag = diag
        self.inv_h2 = 1.0 / h2
        self.size = tiles * SUBS


def lane_index():
    return lax.broadcasted_iota(jnp.int32, (SUBS, LANES), 1)


def at(level, row, tile=0):
    base = row * level.size
    if not isinstance(row, int):
        base = pl.multiple_of(base, SUBS)
    return pl.ds(base + tile * SUBS, SUBS)


def load(ref, level, layer, row):
    return [ref[layer, at(level, row, t), :] for t in range(level.tiles)]


def store(ref, level, layer, row, values):
    for t in range(level.tiles):
        ref[layer, at(level, row, t), :] = values[t]


def east(values, stride=1):
    rolled = [pltpu.roll(v, LANES - stride, 1) for v in values]
    after = rolled[1:] + [pltpu.roll(rolled[0], SUBS - 1, 0)]
    edge = lane_index() >= LANES - stride
    return [jnp.where(edge, a, r) for a, r in zip(after, rolled)]


def west(values, stride=1):
    rolled = [pltpu.roll(v, stride, 1) for v in values]
    before = [pltpu.roll(rolled[-1], 1, 0)] + rolled[:-1]
    edge = lane_index() < stride
    return [jnp.where(edge, b, r) for b, r in zip(before, rolled)]


def transpose_tiles(tiles):
    sub = lax.broadcasted_iota(jnp.int32, (SUBS, LANES), 0)
    for k in (1, 2, 4):
        keep = (sub & k) == 0
        out = list(tiles)
        for i in range(SUBS):
            if not i & k:
                a, b = tiles[i], tiles[i + k]
                out[i] = jnp.where(keep, a, pltpu.roll(b, k, 0))
                out[i + k] = jnp.where(keep, pltpu.roll(a, SUBS - k, 0), b)
        tiles = out
    return tiles


def column_of(level, t, s):
    first = (s * level.tiles + t) * LANES
    return slice(first, first + LANES)


def to_native(level, dst, dst_row, src, layer, src_row, sign=1):
    for t in range(level.tiles):
        tiles = [src[layer, at(level, src_row + r, t), :] for r in range(SUBS)]
        for s, tile in enumerate(transpose_tiles(tiles)):
            dst[layer, dst_row : dst_row + SUBS, column_of(level, t, s)] = (
                tile if sign > 0 else -tile
            )


def row_blocks(low, high, block, body):
    count = high - low if isinstance(low, int) else high
    if count <= 48:
        block = count
    whole = count // block
    if whole > 1:
        lax.fori_loop(0, whole, lambda i, c: (body(low + i * block, block), c)[1], 0)
    elif whole == 1:
        body(low, block)
    if count % block:
        body(low + whole * block, count % block)


def star(rows, k, layer, level, sides=None):
    centre = rows[k][layer]
    if sides:
        e, w = sides[0][k][layer], sides[1][k][layer]
    else:
        e, w = east(centre, level.stride), west(centre, level.stride)
    return [
        (n + s) + (a + b)
        for n, s, a, b in zip(rows[k + 1][layer], rows[k - 1][layer], e, w)
    ]


def load_rows(ref, level, first, count, margin=1):
    return {
        k: [load(ref, level, layer, first + k) for layer in range(2)]
        for k in range(-margin, count + margin)
    }


def sweep_rows(level, rows, source, count, sides=None):
    out = {}
    for k in range(count):
        out[k] = []
        for layer in range(2):
            near = star(rows, k, layer, level, sides)
            out[k].append(
                [
                    (level.keep * c + level.near[layer] * n)
                    + (level.other[layer] * o + level.src[layer] * b)
                    for c, n, o, b in zip(
                        rows[k][layer], near, rows[k][1 - layer], source[k][layer]
                    )
                ]
            )
    return out


def residual_rows(level, rows, source, count):
    out = {}
    for k in range(count):
        out[k] = []
        for layer in range(2):
            near = star(rows, k, layer, level)
            out[k].append(
                [
                    (b - level.diag[layer] * c)
                    + (level.inv_h2 * n + COUPLING[layer] * o)
                    for c, n, o, b in zip(
                        rows[k][layer], near, rows[k][1 - layer], source[k][layer]
                    )
                ]
            )
    return out


def store_rows(ref, level, first, rows, count):
    for k in range(count):
        for layer in range(2):
            store(ref, level, layer, first + k, rows[k][layer])


def sweep(level, dst, dst_at, src, src_at, b, b_at, low, high, block, shifted=None):
    def body(first, count):
        rows = load_rows(src, level, first + src_at, count)
        source = load_rows(b, level, first + b_at, count, 0)
        sides = None
        if shifted:
            sides = [load_rows(ref, level, first + src_at, count, 0) for ref in shifted]
        out = sweep_rows(level, rows, source, count, sides)
        store_rows(dst, level, first + dst_at, out, count)

    row_blocks(low, high, block, body)


def start(level, dst, dst_at, b, b_at, low, high, block):
    def body(first, count):
        source = load_rows(b, level, first + b_at, count, 0)
        out = {
            k: [[level.src[l] * x for x in source[k][l]] for l in range(2)]
            for k in range(count)
        }
        store_rows(dst, level, first + dst_at, out, count)

    row_blocks(low, high, block, body)


def pack_columns(values):
    lane = lane_index()
    pick = (2 * lane) % LANES
    sums = [v + pltpu.roll(v, LANES - 1, 1) for v in values]
    picked = [jnp.take_along_axis(s, pick, axis=1) for s in sums]
    return [
        jnp.where(lane < LANES // 2, picked[2 * t], picked[2 * t + 1])
        for t in range(len(values) // 2)
    ]


def spread_columns(values):
    lane = lane_index()
    out = []
    for v in values:
        out.append(jnp.take_along_axis(v, lane // 2, axis=1))
        out.append(jnp.take_along_axis(v, LANES // 2 + lane // 2, axis=1))
    return out


def merge_columns(values, stride):
    even = (lane_index() // stride) % 2 == 0
    return [
        v + jnp.where(even, pltpu.roll(v, LANES - stride, 1), pltpu.roll(v, stride, 1))
        for v in values
    ]


def restrict(fine, dst, dst_at, coarse, src, src_at, b, b_at, low, high, block):
    def body(first, count):
        rows = load_rows(src, fine, 2 * first + src_at, 2 * count)
        source = load_rows(b, fine, 2 * first + b_at, 2 * count, 0)
        res = residual_rows(fine, rows, source, 2 * count)
        out = {}
        for k in range(count):
            out[k] = []
            for layer in range(2):
                pair = [x + y for x, y in zip(res[2 * k][layer], res[2 * k + 1][layer])]
                if coarse.tiles < fine.tiles:
                    pair = pack_columns(pair)
                else:
                    pair = merge_columns(pair, fine.stride)
                out[k].append([0.25 * x for x in pair])
        store_rows(dst, coarse, first + dst_at, out, count)

    row_blocks(low, high, block, body)


def correct(fine, coarse, dst, dst_at, src, src_at, add, add_at, low, high, block):
    def body(first, count):
        coarse_rows = load_rows(add, coarse, first + add_at, count, 0)
        fine_rows = load_rows(src, fine, 2 * first + src_at, 2 * count, 0)
        out = {}
        for k in range(count):
            spread = [
                spread_columns(v) if coarse.tiles < fine.tiles else v for v in coarse_rows[k]
            ]
            for half in range(2):
                out[2 * k + half] = [
                    [x + y for x, y in zip(fine_rows[2 * k + half][l], spread[l])]
                    for l in range(2)
                ]
        store_rows(dst, fine, 2 * first + dst_at, out, 2 * count)

    row_blocks(low, high, block, body)


def clear(ref, level, low, high):
    ref[:, low * level.size : high * level.size, :] = jnp.zeros(
        (ref.shape[0], (high - low) * level.size, LANES), jnp.float32
    )


def place():
    me, count = lax.axis_index("wide"), lax.axis_size("wide")
    return me, lax.rem(me, 2), me == 0, me == count - 1


def pack_kernel(level, rows, far, p_ref, q_ref, *refs):
    ext_ref, edge_ref, native, sems = refs[-4:]
    _, odd, _, _ = place()
    at_end = odd == 1 if far else odd == 0
    count = SUBS if far else rows - SUBS
    first = pl.multiple_of(jnp.where(at_end, rows - count, 0), SUBS)
    copies = []
    for field, ref in enumerate((p_ref, q_ref)):
        for layer in range(2):
            which = 2 * field + layer
            copies.append(
                pltpu.make_async_copy(
                    ref.at[layer, pl.ds(first, count)], native.at[which], sems.at[which]
                )
            )
            copies[-1].start()
    for which in range(4):
        copies[which].wait()
        for group in range(count // SUBS):
            for t in range(level.tiles):
                tiles = [
                    native[which, group * SUBS : (group + 1) * SUBS, column_of(level, t, s)]
                    for s in range(SUBS)
                ]
                for r, tile in enumerate(transpose_tiles(tiles)):
                    ext_ref[which, at(level, first + HALO + group * SUBS + r, t), :] = tile
    edge = jnp.where(at_end, rows, HALO) * level.size
    edge_ref[...] = ext_ref[:, pl.ds(pl.multiple_of(edge, SUBS), HALO * level.size), :]


def send_edges(level, width, src_at, rows, src, near_ref, far_ref):
    _, odd, _, _ = place()
    size = width * level.size
    last = (src_at + rows - width) * level.size
    top = src_at * level.size
    near = pl.multiple_of(jnp.where(odd == 1, top, last), SUBS)
    far = pl.multiple_of(jnp.where(odd == 1, last, top), SUBS)
    near_ref[:, 0:size, :] = src[:, pl.ds(near, size), :]
    far_ref[:, 0:size, :] = src[:, pl.ds(far, size), :]


def receive_edges(level, width, dst_at, rows, dst, near_ref, far_ref):
    _, odd, first, last = place()
    size = width * level.size
    low = (dst_at + rows) * level.size
    top = (dst_at - width) * level.size
    near = pl.multiple_of(jnp.where(odd == 1, top, low), SUBS)
    far = pl.multiple_of(jnp.where(odd == 1, low, top), SUBS)
    dst[:, pl.ds(near, size), :] = near_ref[:, 0:size, :]
    outside = jnp.logical_or(first, last)
    dst[:, pl.ds(far, size), :] = jnp.where(outside, 0.0, far_ref[:, 0:size, :])


def shift_rows(level, ext, e_ref, w_ref, low, high, block):
    def body(first, count):
        for k in range(count):
            for f in range(4):
                v = load(ext, level, f, first + k)
                store(e_ref, level, f, first + k, east(v))
                store(w_ref, level, f, first + k, west(v))

    row_blocks(low, high, block, body)


def advance_rows(level, b_ref, ext, e_ref, w_ref, low, high, block):
    def body(first, count):
        for layer in range(2):
            for t in range(level.tiles):
                def grab(ref, field):
                    return {
                        k: ref[2 * field + layer, at(level, first + k, t), :]
                        for k in range(-1, count + 1)
                    }

                p, pe, pw = grab(ext, 0), grab(e_ref, 0), grab(w_ref, 0)
                q, qe, qw = grab(ext, 1), grab(e_ref, 1), grab(w_ref, 1)
                zonal = {k: pe[k] - pw[k] for k in p}
                for k in range(count):
                    n, s = k + 1, k - 1
                    v0, ve, vw = p[n] - p[s], pe[n] - pe[s], pw[n] - pw[s]
                    jac = q[n] * (zonal[k] + zonal[n]) - q[s] * (zonal[k] + zonal[s])
                    jac = jac - qe[k] * (v0 + ve) + qw[k] * (v0 + vw)
                    jac = jac + qe[n] * (pe[k] - p[n]) - qe[s] * (pe[k] - p[s])
                    jac = jac - qw[n] * (pw[k] - p[n]) + qw[s] * (pw[k] - p[s])
                    step = (TIME_STEP / 12.0) * jac + (0.5 * TIME_STEP * BETA) * zonal[k]
                    if layer == 1:
                        lap = (p[n] + p[s]) + (pe[k] + pw[k]) - 4.0 * p[k]
                        step = step + (TIME_STEP * DRAG[1]) * lap
                    b_ref[layer, at(level, first + k, t), :] = step - q[k]

    row_blocks(low, high, block, body)


def inner_kernel(level, coarse, rows, ext, e_ref, w_ref, b_ref, v_one, v_two, bc_ref):
    low, high = HALO, HALO + rows
    shift_rows(level, ext, e_ref, w_ref, low, high, 4)
    advance_rows(level, b_ref, ext, e_ref, w_ref, low + 1, high - 1, 2)
    sweep(level, v_one, 0, ext, 0, b_ref, 0, low + 2, high - 2, 4, (e_ref, w_ref))
    sweep(level, v_two, 0, v_one, 0, b_ref, 0, low + 3, high - 3, 4)
    restrict(level, bc_ref, 0, coarse, v_two, HALO, b_ref, HALO, 2, rows // 2 - 2, 2)


def outer_kernel(level, coarse, rows, *refs):
    near_ref, far_ref = refs[7:9]
    ext, e_ref, w_ref, b_ref, v_one, v_two, bc_ref, bc_near_ref, bc_far_ref = refs[9:]
    _, _, is_first, is_last = place()
    low, high = HALO, HALO + rows
    total = rows + 2 * HALO
    receive_edges(level, HALO, HALO, rows, ext, near_ref, far_ref)
    shift_rows(level, ext, e_ref, w_ref, 0, low, 3)
    shift_rows(level, ext, e_ref, w_ref, high, total, 3)
    advance_rows(level, b_ref, ext, e_ref, w_ref, 1, low + 1, 3)
    advance_rows(level, b_ref, ext, e_ref, w_ref, high - 1, total - 1, 3)
    sweep(level, v_one, 0, ext, 0, b_ref, 0, 1, low + 2, 4, (e_ref, w_ref))
    sweep(level, v_one, 0, ext, 0, b_ref, 0, high - 2, total - 1, 4, (e_ref, w_ref))

    def trim(ref):
        @pl.when(is_first)
        def _():
            clear(ref, level, 0, HALO)

        @pl.when(is_last)
        def _():
            clear(ref, level, high, total)

    trim(v_one)
    sweep(level, v_two, 0, v_one, 0, b_ref, 0, 2, low + 3, 4)
    sweep(level, v_two, 0, v_one, 0, b_ref, 0, high - 3, total - 2, 4)
    trim(v_two)
    half = rows // 2
    restrict(level, bc_ref, 0, coarse, v_two, HALO, b_ref, HALO, 0, 2, 2)
    restrict(level, bc_ref, 0, coarse, v_two, HALO, b_ref, HALO, half - 2, half, 2)
    send_edges(coarse, MID_HALO, 0, half, bc_ref, bc_near_ref, bc_far_ref)


def emit(level, rows, b_ref, next_ref, native, sems):
    copies = []
    for layer in range(2):
        for group in range(rows // SUBS):
            rows_of = pl.ds(group * SUBS, SUBS)
            to_native(level, native, group * SUBS, b_ref, layer, HALO + group * SUBS, -1)
            copies.append(
                pltpu.make_async_copy(
                    native.at[layer, rows_of], next_ref.at[layer, rows_of],
                    sems.at[layer, group],
                )
            )
            copies[-1].start()
    return copies


def middle_kernel(
    fine, level, two, three, rows, b_own, near_ref, far_ref, v0_ref,
    b_ref, v_ref, b2_ref, v2_ref, out_ref, two_near_ref, two_far_ref,
    v_one, w_two, b3,
):
    _, odd, is_first, is_last = place()
    total = rows + 2 * MID_HALO
    own = rows // 2
    edge = MID_HALO * level.size
    b_ref[:, edge : edge + rows * level.size, :] = b_own[...]
    receive_edges(level, MID_HALO, MID_HALO, rows, b_ref, near_ref, far_ref)
    start(level, v_one, 0, b_ref, 0, 0, total, 4)

    def trim(ref, of, halo, n):
        @pl.when(is_first)
        def _():
            clear(ref, of, 0, halo)

        @pl.when(is_last)
        def _():
            clear(ref, of, halo + n, 2 * halo + n)

    trim(v_one, level, MID_HALO, rows)
    sweep(level, v_ref, 0, v_one, 0, b_ref, 0, 1, total - 1, 6)
    trim(v_ref, level, MID_HALO, rows)
    restrict(
        level, b2_ref, TWO_HALO, two, v_ref, MID_HALO, b_ref, MID_HALO, -2, own + 2, 4
    )
    start(two, w_two, TWO_HALO, b2_ref, TWO_HALO, -2, own + 2, 8)
    trim(w_two, two, TWO_HALO, own)
    sweep(two, v2_ref, TWO_HALO, w_two, TWO_HALO, b2_ref, TWO_HALO, -1, own + 1, 6)
    trim(v2_ref, two, TWO_HALO, own)
    restrict(
        two, b3, 0, three, v2_ref, TWO_HALO, b2_ref, TWO_HALO, 0, own // 2, 2
    )
    even = lane_index() % 2 == 0
    for layer in range(2):
        for pair in range(own // 4):
            row = jnp.where(
                even,
                b3[layer, at(three, 2 * pair), :],
                b3[layer, at(three, 2 * pair + 1), :],
            )
            for copy in range(out_ref.shape[0]):
                out_ref[copy, layer, at(three, pair), :] = row
    up, down = pl.ds((TWO_HALO + 1) * two.size, 3 * two.size), pl.ds(
        own * two.size, 3 * two.size
    )
    up_b, down_b = at(two, TWO_HALO + 2), at(two, TWO_HALO + own - 3)
    last = pl.ds(3 * two.size, two.size)

    tail = pl.ds(4 * two.size, fine.size)
    up_0 = pl.ds((HALO + 1) * fine.size, fine.size)
    down_0 = pl.ds((HALO + 2 * rows - 2) * fine.size, fine.size)

    def send(ref, rows_v, row_b, row_0):
        ref[:, 0 : 3 * two.size, :] = v2_ref[:, rows_v, :]
        ref[:, last, :] = b2_ref[:, row_b, :]
        ref[:, tail, :] = v0_ref[:, row_0, :]

    @pl.when(odd == 1)
    def _():
        send(two_near_ref, up, up_b, up_0)
        send(two_far_ref, down, down_b, down_0)

    @pl.when(odd == 0)
    def _():
        send(two_near_ref, down, down_b, down_0)
        send(two_far_ref, up, up_b, up_0)


PAD = 4


def coarse_solve(level, dst, dst_at, b_ref, n):
    groups = level.stride
    m = n // groups
    part = lane_index() % groups
    source = []
    for layer in range(2):
        source.append([])
        for k in range(m):
            tile = load(b_ref, level, layer, k)[0]
            for g in range(1, groups):
                tile = jnp.where(part == g, load(b_ref, level, layer, g * m + k)[0], tile)
            source[layer].append(level.src[layer] * tile)
    values = source
    for _ in range(COARSE_SWEEPS - 1):
        new = []
        for layer in range(2):
            v, o = values[layer], values[1 - layer]
            below = jnp.where(part == groups - 1, 0.0, pltpu.roll(v[0], LANES - 1, 1))
            above = jnp.where(part == 0, 0.0, pltpu.roll(v[-1], 1, 1))
            out = []
            for k in range(m):
                n_row = v[k + 1] if k + 1 < m else below
                s_row = v[k - 1] if k else above
                e, w = east([v[k]], groups)[0], west([v[k]], groups)[0]
                out.append(
                    (level.keep * v[k] + level.near[layer] * ((n_row + s_row) + (e + w)))
                    + (level.other[layer] * o[k] + source[layer][k])
                )
            new.append(out)
        values = new
    for layer in range(2):
        for k in range(m):
            moved = {
                d: pltpu.roll(values[layer][k], d % LANES, 1) if d else values[layer][k]
                for d in range(1 - groups, groups)
            }
            for g in range(groups):
                tile = moved[-g]
                for j in range(1, groups):
                    tile = jnp.where(part == j, moved[j - g], tile)
                dst[layer, at(level, dst_at + g * m + k), :] = tile


def coarse_kernel(
    levels, rows, same_ref, other_ref, b0_ref, out_ref, next_ref,
    b3, v3, w3, b4, v4, native, sems,
):
    me, odd, is_first, is_last = place()
    fine, three, four = levels
    copies = emit(fine, rows, b0_ref, next_ref, native, sems)
    own = rows // 4
    chips = same_ref.shape[0]
    n3, n4 = chips * own, chips * own // 2
    for ref, level, n in ((b3, three, n3), (v3, three, n3), (w3, three, n3), (v4, four, n4)):
        clear(ref, level, 0, PAD)
        clear(ref, level, PAD + n, 2 * PAD + n)
    even = lane_index() % 2 == 0

    def gather_body(chip, carry):
        for ref, core in ((same_ref, odd), (other_ref, 1 - odd)):
            row = (2 * chip + core) * (own // 2) + PAD
            for layer in range(2):
                for pair in range(own // 4):
                    both = ref[chip, layer, at(three, pair), :]
                    first = jnp.where(even, both, pltpu.roll(both, 1, 1))
                    second = jnp.where(even, pltpu.roll(both, LANES - 1, 1), both)
                    b3[layer, at(three, row + 2 * pair), :] = first
                    b3[layer, at(three, row + 2 * pair + 1), :] = second
        return carry

    lax.fori_loop(0, chips, gather_body, 0, unroll=min(chips, 8))

    start(three, v3, PAD, b3, PAD, 0, n3, 8)
    sweep(three, w3, PAD, v3, PAD, b3, PAD, 0, n3, 16)
    restrict(three, b4, 0, four, w3, PAD, b3, PAD, 0, n4, 8)
    coarse_solve(four, v4, PAD, b4, n4)

    def trim(ref, level, n):
        @pl.when(me < 2)
        def _():
            clear(ref, level, 0, PAD)

        @pl.when(me >= 2 * chips - 2)
        def _():
            clear(ref, level, PAD + n, 2 * PAD + n)

    half, quarter = own // 2, own // 4
    correct(three, four, v3, PAD, w3, PAD, v4, PAD, me * quarter - 2, quarter + 4, 8)
    sweep(three, w3, PAD, v3, PAD, b3, PAD, me * half - 3, half + 6, 8)
    trim(w3, three, n3)
    sweep(three, out_ref, 2 - me * half, w3, PAD, b3, PAD, me * half - 2, half + 4, 8)

    @pl.when(is_first)
    def _():
        clear(out_ref, three, 0, 2)

    @pl.when(is_last)
    def _():
        clear(out_ref, three, half + 2, half + 4)

    for copy in copies:
        copy.wait()


def rise_kernel(
    levels, rows, v3_ref, near_ref, far_ref,
    b2_ref, v2_ref, b1_ref, v1_ref, b0_ref, v0_in, out_ref, v0_ref,
    b2, v2, x2, y2, x1, y1, x0, y0, z0, native, sems,
):
    _, odd, is_first, is_last = place()
    fine, mid, two, three = levels
    own = rows // 4

    b2[...] = b2_ref[...]
    v2[...] = v2_ref[...]

    def take(ref, zero):
        top_v, low_v = pl.ds(0, 3 * two.size), pl.ds((TWO_HALO + own + 1) * two.size, 3 * two.size)
        top_b, low_b = at(two, TWO_HALO - 3), at(two, TWO_HALO + own + 2)
        last = pl.ds(3 * two.size, two.size)

        tail = pl.ds(4 * two.size, fine.size)
        top_0 = pl.ds((HALO - 2) * fine.size, fine.size)
        low_0 = pl.ds((HALO + rows + 1) * fine.size, fine.size)

        def drop(values):
            return values if zero is None else jnp.where(zero, 0.0, values)

        def put(rows_v, row_b, row_0):
            v2[:, rows_v, :] = drop(ref[:, 0 : 3 * two.size, :])
            b2[:, row_b, :] = ref[:, last, :]
            v0_ref[:, row_0, :] = drop(ref[:, tail, :])

        return lambda: put(top_v, top_b, top_0), lambda: put(low_v, low_b, low_0)

    near_top, near_low = take(near_ref, None)
    far_top, far_low = take(far_ref, jnp.logical_or(is_first, is_last))

    @pl.when(odd == 1)
    def _():
        near_top()
        far_low()

    @pl.when(odd == 0)
    def _():
        near_low()
        far_top()

    def trim_own(ref, level, halo, n):
        @pl.when(is_first)
        def _():
            clear(ref, level, 0, halo)

        @pl.when(is_last)
        def _():
            clear(ref, level, halo + n, 2 * halo + n)

    total = own + 2 * TWO_HALO
    correct(two, three, x2, 0, v2, 0, v3_ref, 0, 0, total // 2, 8)
    sweep(two, y2, 0, x2, 0, b2, 0, 1, total - 1, 10)
    trim_own(y2, two, TWO_HALO, own)
    sweep(two, x2, 0, y2, 0, b2, 0, 2, total - 2, 8)
    trim_own(x2, two, TWO_HALO, own)

    n1 = rows // 2
    total = n1 + 2 * MID_HALO

    correct(
        mid, two, x1, MID_HALO - 4, v1_ref, MID_HALO - 4, x2, TWO_HALO - 2, 0, n1 // 2 + 4, 4
    )
    sweep(mid, y1, 0, x1, 0, b1_ref, 0, MID_HALO - 2, MID_HALO + n1 + 2, 6)
    trim_own(y1, mid, MID_HALO, n1)
    sweep(mid, x1, 0, y1, 0, b1_ref, 0, MID_HALO - 1, MID_HALO + n1 + 1, 5)
    trim_own(x1, mid, MID_HALO, n1)

    low, done, swept = HALO, 0, HALO - 1
    copies = []
    for group in range(rows // SUBS):
        first_row = low + group * SUBS
        rows_of = pl.ds(group * SUBS, SUBS)
        ready = SUBS // 2 * (group + 1) + 2
        correct(fine, mid, x0, HALO - 2, v0_ref, HALO - 2, x1, MID_HALO - 1, done, ready, 2)
        sweep(fine, y0, 0, x0, 0, b0_ref, 0, swept, first_row + SUBS + 1, 5 - group)
        trim_own(y0, fine, HALO, rows)
        done, swept = ready, first_row + SUBS + 1
        sweep(fine, z0, 0, y0, 0, b0_ref, 0, first_row, first_row + SUBS, 4)
        for layer in range(2):
            to_native(fine, native, group * SUBS, z0, layer, first_row)
            copies.append(
                pltpu.make_async_copy(
                    native.at[layer, rows_of], out_ref.at[layer, rows_of],
                    sems.at[layer, group],
                )
            )
            copies[-1].start()
    for copy in copies:
        copy.wait()


def shape(*dims):
    return jax.ShapeDtypeStruct(dims, jnp.float32)


def scratch(layers, rows, level):
    return pltpu.VMEM((layers, rows * level.size, LANES), jnp.float32)


HBM = pl.BlockSpec(memory_space=pltpu.HBM)
VMEM = pl.BlockSpec(memory_space=pltpu.VMEM)


def call(kernel, out_shape, scratch_shapes=(), cost=None, limit=24, **options):
    if cost is not None:
        cost = pl.CostEstimate(flops=cost, bytes_accessed=cost // 8, transcendentals=0)
    return pl.pallas_call(
        kernel,
        out_shape=out_shape,
        scratch_shapes=list(scratch_shapes),
        cost_estimate=cost,
        compiler_params=pltpu.CompilerParams(vmem_limit_bytes=limit * 1024 * 1024),
        **options,
    )


def shards(stream_now, vorticity):
    _, rows, columns = stream_now.shape
    count = lax.axis_size("wide")
    tiles = columns // (SUBS * LANES)
    fine, mid = Level(0, tiles, 1), Level(1, tiles // 2, 1)
    two, three, four = Level(2, tiles // 4, 1), Level(3, tiles // 4, 2), Level(4, tiles // 4, 4)
    core_swap = [(i, i ^ 1) for i in range(count)]
    members = lax.axis_size("member")
    inside = [(i, ((i + 1) ^ 1) - 1) for i in range(1, count - 1)]
    if members % 2:
        ends = [(0, count - 1), (count - 1, 0)]
        chip_swap = [(m * count + i, m * count + j) for m in range(members) for i, j in ends]
    else:
        chip_swap = [
            (m * count + i, (m ^ 1) * count + i) for m in range(members) for i in (0, count - 1)
        ]
    chip_swap += [(m * count + i, m * count + j) for m in range(members) for i, j in inside]
    groups = rows // SUBS

    def exchange(near, far):
        far = lax.ppermute(far, ("member", "wide"), chip_swap)
        near = lax.ppermute(near, "wide", core_swap)
        return near, far

    half, quarter = rows // 2, rows // 4
    total = rows + 2 * HALO
    inputs = [pltpu.with_memory_space_constraint(x, pltpu.HBM) for x in (stream_now, vorticity)]

    def pack(far, packed):
        return call(
            functools.partial(pack_kernel, fine, rows, far),
            [
                shape(4, total * fine.size, LANES),
                shape(4, HALO * fine.size, LANES),
            ],
            [
                pltpu.VMEM((4, SUBS if far else rows - SUBS, columns), jnp.float32),
                pltpu.SemaphoreType.DMA((4,)),
            ],
            cost=2000000,
            in_specs=[HBM, HBM] + [VMEM] * len(packed),
            input_output_aliases={2: 0} if packed else {},
        )(*inputs, *packed)

    ext, far = pack(True, [])
    ext, near = pack(False, [ext])
    near, far = exchange(near, far)
    state = [
        shape(4, total * fine.size, LANES),
        shape(4, total * fine.size, LANES),
        shape(2, total * fine.size, LANES),
        shape(2, total * fine.size, LANES),
        shape(2, total * fine.size, LANES),
        shape(2, half * mid.size, LANES),
    ]
    inner = call(
        functools.partial(inner_kernel, fine, mid, rows),
        state,
        cost=8000000,
    )(ext)
    edge = shape(2, MID_HALO * mid.size, LANES)
    outer = call(
        functools.partial(outer_kernel, fine, mid, rows),
        [shape(4, total * fine.size, LANES)] + state + [edge, edge],
        input_output_aliases={i: i for i in range(7)},
    )(ext, *inner, near, far)
    b0, v0, b1, near, far = outer[3], outer[5], outer[6], outer[7], outer[8]
    near, far = exchange(near, far)
    chips = count // 2
    eighth = rows // 8
    two_edge = shape(2, 4 * two.size + fine.size, LANES)
    two_all = shape(2, (quarter + 2 * TWO_HALO) * two.size, LANES)
    b1, v1, b2, v2, b3, near, far = call(
        functools.partial(middle_kernel, fine, mid, two, three, half),
        [
            shape(2, (half + 2 * MID_HALO) * mid.size, LANES),
            shape(2, (half + 2 * MID_HALO) * mid.size, LANES),
            two_all,
            two_all,
            shape(chips, 2, eighth // 2 * three.size, LANES),
            two_edge,
            two_edge,
        ],
        [
            scratch(2, half + 2 * MID_HALO, mid),
            scratch(2, quarter + 2 * TWO_HALO, two),
            scratch(2, eighth, three),
        ],
    )(b1, near, far, v0)
    cores = [[i for i in range(count) if i % 2 == c] for c in range(2)]
    same = lax.all_to_all(b3, "wide", 0, 0, axis_index_groups=cores)
    other = lax.ppermute(same, "wide", core_swap)
    near, far = exchange(near, far)
    n3, n4 = count * eighth, count * eighth // 2
    v3, vorticity_next = call(
        functools.partial(coarse_kernel, (fine, three, four), rows),
        [shape(2, (eighth + 4) * three.size, LANES), shape(2, rows, columns)],
        [scratch(2, n3 + 2 * PAD, three)] * 3
        + [scratch(2, n4, four), scratch(2, n4 + 2 * PAD, four)]
        + [pltpu.VMEM((2, rows, columns), jnp.float32), pltpu.SemaphoreType.DMA((2, groups))],
        cost=5000000,
        out_specs=[VMEM, HBM],
    )(same, other, b0)
    stream_next, _ = call(
        functools.partial(rise_kernel, (fine, mid, two, three), rows),
        [shape(2, rows, columns), shape(2, total * fine.size, LANES)],
        [scratch(2, quarter + 2 * TWO_HALO, two)] * 4
        + [scratch(2, half + 2 * MID_HALO, mid)] * 2
        + [scratch(2, total, fine)] * 3
        + [pltpu.VMEM((2, rows, columns), jnp.float32), pltpu.SemaphoreType.DMA((2, groups))],
        out_specs=[HBM, VMEM],
        input_output_aliases={8: 1},
    )(v3, near, far, b2, v2, b1, v1, b0, v0)
    return (vorticity_next, stream_next)


def solution(mesh):
    return jax.shard_map(
        shards,
        mesh=mesh,
        in_specs=(P("member", "wide", None), P("member", "wide", None)),
        out_specs=(P("member", "wide", None), P("member", "wide", None)),
        check_vma=False,
    )
```

```python
import functools

import jax
import jax.numpy as jnp
from jax import lax
from jax.experimental import pallas as pl
from jax.experimental.pallas import tpu as pltpu
from jax.sharding import PartitionSpec as P


LANES = 128
SUBS = 8
HALO = 3
MID_HALO = 6
TWO_HALO = 4
RELAX = 0.8
COUPLING = (0.02, 0.04)
TIME_STEP = 0.5
BETA = 0.05
DRAG = (0.0, 0.02)
COARSE_SWEEPS = 8


class Level:
    def __init__(self, level, tiles, stride):
        h2 = (2.0**level) ** 2
        self.tiles, self.stride = tiles, stride
        diag = [4.0 / h2 + f for f in COUPLING]
        self.keep = 1.0 - RELAX
        self.near = [RELAX / (d * h2) for d in diag]
        self.other = [RELAX * f / d for f, d in zip(COUPLING, diag)]
        self.src = [RELAX / d for d in diag]
        self.diag = diag
        self.inv_h2 = 1.0 / h2
        self.size = tiles * SUBS


def lane_index():
    return lax.broadcasted_iota(jnp.int32, (SUBS, LANES), 1)


def at(level, row, tile=0):
    base = row * level.size
    if not isinstance(row, int):
        base = pl.multiple_of(base, SUBS)
    return pl.ds(base + tile * SUBS, SUBS)


def load(ref, level, layer, row):
    return [ref[layer, at(level, row, t), :] for t in range(level.tiles)]


def store(ref, level, layer, row, values):
    for t in range(level.tiles):
        ref[layer, at(level, row, t), :] = values[t]


def east(values, stride=1):
    rolled = [pltpu.roll(v, LANES - stride, 1) for v in values]
    after = rolled[1:] + [pltpu.roll(rolled[0], SUBS - 1, 0)]
    edge = lane_index() >= LANES - stride
    return [jnp.where(edge, a, r) for a, r in zip(after, rolled)]


def west(values, stride=1):
    rolled = [pltpu.roll(v, stride, 1) for v in values]
    before = [pltpu.roll(rolled[-1], 1, 0)] + rolled[:-1]
    edge = lane_index() < stride
    return [jnp.where(edge, b, r) for b, r in zip(before, rolled)]


def transpose_tiles(tiles):
    sub = lax.broadcasted_iota(jnp.int32, (SUBS, LANES), 0)
    for k in (1, 2, 4):
        keep = (sub & k) == 0
        out = list(tiles)
        for i in range(SUBS):
            if not i & k:
                a, b = tiles[i], tiles[i + k]
                out[i] = jnp.where(keep, a, pltpu.roll(b, k, 0))
                out[i + k] = jnp.where(keep, pltpu.roll(a, SUBS - k, 0), b)
        tiles = out
    return tiles


def column_of(level, t, s):
    first = (s * level.tiles + t) * LANES
    return slice(first, first + LANES)


def to_native(level, dst, dst_row, src, layer, src_row, sign=1):
    for t in range(level.tiles):
        tiles = [src[layer, at(level, src_row + r, t), :] for r in range(SUBS)]
        for s, tile in enumerate(transpose_tiles(tiles)):
            dst[layer, dst_row : dst_row + SUBS, column_of(level, t, s)] = (
                tile if sign > 0 else -tile
            )


def row_blocks(low, high, block, body, straight=48):
    count = high - low if isinstance(low, int) else high
    if count <= straight:
        block = count
    whole = count // block
    if whole > 1:
        lax.fori_loop(0, whole, lambda i, c: (body(low + i * block, block), c)[1], 0)
    elif whole == 1:
        body(low, block)
    if count % block:
        body(low + whole * block, count % block)


def star(rows, k, layer, level, sides=None):
    centre = rows[k][layer]
    if sides:
        e, w = sides[0][k][layer], sides[1][k][layer]
    else:
        e, w = east(centre, level.stride), west(centre, level.stride)
    return [
        (n + s) + (a + b)
        for n, s, a, b in zip(rows[k + 1][layer], rows[k - 1][layer], e, w)
    ]


def load_rows(ref, level, first, count, margin=1):
    return {
        k: [load(ref, level, layer, first + k) for layer in range(2)]
        for k in range(-margin, count + margin)
    }


def sweep_rows(level, rows, source, count, sides=None):
    out = {}
    for k in range(count):
        out[k] = []
        for layer in range(2):
            near = star(rows, k, layer, level, sides)
            out[k].append(
                [
                    (level.keep * c + level.near[layer] * n)
                    + (level.other[layer] * o + level.src[layer] * b)
                    for c, n, o, b in zip(
                        rows[k][layer], near, rows[k][1 - layer], source[k][layer]
                    )
                ]
            )
    return out


def residual_rows(level, rows, source, count):
    out = {}
    for k in range(count):
        out[k] = []
        for layer in range(2):
            near = star(rows, k, layer, level)
            out[k].append(
                [
                    (b - level.diag[layer] * c)
                    + (level.inv_h2 * n + COUPLING[layer] * o)
                    for c, n, o, b in zip(
                        rows[k][layer], near, rows[k][1 - layer], source[k][layer]
                    )
                ]
            )
    return out


def store_rows(ref, level, first, rows, count):
    for k in range(count):
        for layer in range(2):
            store(ref, level, layer, first + k, rows[k][layer])


def sweep(level, dst, dst_at, src, src_at, b, b_at, low, high, block, shifted=None, straight=48):
    def body(first, count):
        rows = load_rows(src, level, first + src_at, count)
        source = load_rows(b, level, first + b_at, count, 0)
        sides = None
        if shifted:
            sides = [load_rows(ref, level, first + src_at, count, 0) for ref in shifted]
        out = sweep_rows(level, rows, source, count, sides)
        store_rows(dst, level, first + dst_at, out, count)

    row_blocks(low, high, block, body, straight)


def start(level, dst, dst_at, b, b_at, low, high, block):
    def body(first, count):
        source = load_rows(b, level, first + b_at, count, 0)
        out = {
            k: [[level.src[l] * x for x in source[k][l]] for l in range(2)]
            for k in range(count)
        }
        store_rows(dst, level, first + dst_at, out, count)

    row_blocks(low, high, block, body)


def pack_columns(values):
    lane = lane_index()
    pick = (2 * lane) % LANES
    sums = [v + pltpu.roll(v, LANES - 1, 1) for v in values]
    picked = [jnp.take_along_axis(s, pick, axis=1) for s in sums]
    return [
        jnp.where(lane < LANES // 2, picked[2 * t], picked[2 * t + 1])
        for t in range(len(values) // 2)
    ]


def spread_columns(values):
    lane = lane_index()
    out = []
    for v in values:
        out.append(jnp.take_along_axis(v, lane // 2, axis=1))
        out.append(jnp.take_along_axis(v, LANES // 2 + lane // 2, axis=1))
    return out


def merge_columns(values, stride):
    even = (lane_index() // stride) % 2 == 0
    return [
        v + jnp.where(even, pltpu.roll(v, LANES - stride, 1), pltpu.roll(v, stride, 1))
        for v in values
    ]


def restrict(
    fine, dst, dst_at, coarse, src, src_at, b, b_at, low, high, block, straight=48
):
    def body(first, count):
        rows = load_rows(src, fine, 2 * first + src_at, 2 * count)
        source = load_rows(b, fine, 2 * first + b_at, 2 * count, 0)
        res = residual_rows(fine, rows, source, 2 * count)
        out = {}
        for k in range(count):
            out[k] = []
            for layer in range(2):
                pair = [x + y for x, y in zip(res[2 * k][layer], res[2 * k + 1][layer])]
                if coarse.tiles < fine.tiles:
                    pair = pack_columns(pair)
                else:
                    pair = merge_columns(pair, fine.stride)
                out[k].append([0.25 * x for x in pair])
        store_rows(dst, coarse, first + dst_at, out, count)

    row_blocks(low, high, block, body, straight)


def correct(fine, coarse, dst, dst_at, src, src_at, add, add_at, low, high, block):
    def body(first, count):
        coarse_rows = load_rows(add, coarse, first + add_at, count, 0)
        fine_rows = load_rows(src, fine, 2 * first + src_at, 2 * count, 0)
        out = {}
        for k in range(count):
            spread = [
                spread_columns(v) if coarse.tiles < fine.tiles else v for v in coarse_rows[k]
            ]
            for half in range(2):
                out[2 * k + half] = [
                    [x + y for x, y in zip(fine_rows[2 * k + half][l], spread[l])]
                    for l in range(2)
                ]
        store_rows(dst, fine, 2 * first + dst_at, out, 2 * count)

    row_blocks(low, high, block, body)


def clear(ref, level, low, high):
    ref[:, low * level.size : high * level.size, :] = jnp.zeros(
        (ref.shape[0], (high - low) * level.size, LANES), jnp.float32
    )


def place():
    me, count = lax.axis_index("wide"), lax.axis_size("wide")
    return me, lax.rem(me, 2), me == 0, me == count - 1


def pack_kernel(level, rows, p_ref, q_ref, ext_ref, near_ref, far_ref, native, sems):
    copies = []
    for field, ref in enumerate((p_ref, q_ref)):
        for layer in range(2):
            which = 2 * field + layer
            copies.append(
                pltpu.make_async_copy(ref.at[layer], native.at[which], sems.at[which])
            )
            copies[-1].start()
    for which in range(4):
        copies[which].wait()
        for group in range(rows // SUBS):
            for t in range(level.tiles):
                tiles = [
                    native[which, group * SUBS : (group + 1) * SUBS, column_of(level, t, s)]
                    for s in range(SUBS)
                ]
                for r, tile in enumerate(transpose_tiles(tiles)):
                    ext_ref[which, at(level, HALO + group * SUBS + r, t), :] = tile
    send_edges(level, HALO, HALO, rows, ext_ref, near_ref, far_ref)


def send_edges(level, width, src_at, rows, src, near_ref, far_ref):
    _, odd, _, _ = place()
    size = width * level.size
    last = (src_at + rows - width) * level.size
    top = src_at * level.size
    near = pl.multiple_of(jnp.where(odd == 1, top, last), SUBS)
    far = pl.multiple_of(jnp.where(odd == 1, last, top), SUBS)
    near_ref[:, 0:size, :] = src[:, pl.ds(near, size), :]
    far_ref[:, 0:size, :] = src[:, pl.ds(far, size), :]


def receive_edges(level, width, dst_at, rows, dst, near_ref, far_ref):
    _, odd, first, last = place()
    size = width * level.size
    low = (dst_at + rows) * level.size
    top = (dst_at - width) * level.size
    near = pl.multiple_of(jnp.where(odd == 1, top, low), SUBS)
    far = pl.multiple_of(jnp.where(odd == 1, low, top), SUBS)
    dst[:, pl.ds(near, size), :] = near_ref[:, 0:size, :]
    outside = jnp.logical_or(first, last)
    dst[:, pl.ds(far, size), :] = jnp.where(outside, 0.0, far_ref[:, 0:size, :])


def shift_rows(level, ext, e_ref, w_ref, low, high, block):
    def body(first, count):
        for k in range(count):
            for f in range(4):
                v = load(ext, level, f, first + k)
                store(e_ref, level, f, first + k, east(v))
                store(w_ref, level, f, first + k, west(v))

    row_blocks(low, high, block, body)


def advance_rows(level, b_ref, ext, e_ref, w_ref, low, high, block):
    def body(first, count):
        for layer in range(2):
            for t in range(level.tiles):
                def grab(ref, field):
                    return {
                        k: ref[2 * field + layer, at(level, first + k, t), :]
                        for k in range(-1, count + 1)
                    }

                p, pe, pw = grab(ext, 0), grab(e_ref, 0), grab(w_ref, 0)
                q, qe, qw = grab(ext, 1), grab(e_ref, 1), grab(w_ref, 1)
                zonal = {k: pe[k] - pw[k] for k in p}
                for k in range(count):
                    n, s = k + 1, k - 1
                    v0, ve, vw = p[n] - p[s], pe[n] - pe[s], pw[n] - pw[s]
                    jac = q[n] * (zonal[k] + zonal[n]) - q[s] * (zonal[k] + zonal[s])
                    jac = jac - qe[k] * (v0 + ve) + qw[k] * (v0 + vw)
                    jac = jac + qe[n] * (pe[k] - p[n]) - qe[s] * (pe[k] - p[s])
                    jac = jac - qw[n] * (pw[k] - p[n]) + qw[s] * (pw[k] - p[s])
                    step = (TIME_STEP / 12.0) * jac + (0.5 * TIME_STEP * BETA) * zonal[k]
                    if layer == 1:
                        lap = (p[n] + p[s]) + (pe[k] + pw[k]) - 4.0 * p[k]
                        step = step + (TIME_STEP * DRAG[1]) * lap
                    b_ref[layer, at(level, first + k, t), :] = step - q[k]

    row_blocks(low, high, block, body)


def inner_kernel(level, coarse, rows, ext, e_ref, w_ref, b_ref, v_one, v_two, bc_ref):
    low, high = HALO, HALO + rows
    shift_rows(level, ext, e_ref, w_ref, low, high, 4)
    advance_rows(level, b_ref, ext, e_ref, w_ref, low + 1, high - 1, 2)
    sweep(level, v_one, 0, ext, 0, b_ref, 0, low + 2, high - 2, 4, (e_ref, w_ref))
    sweep(level, v_two, 0, v_one, 0, b_ref, 0, low + 3, high - 3, 4)
    restrict(level, bc_ref, 0, coarse, v_two, HALO, b_ref, HALO, 2, rows // 2 - 2, 2)


def outer_kernel(level, coarse, rows, *refs):
    near_ref, far_ref = refs[7:9]
    ext, e_ref, w_ref, b_ref, v_one, v_two, bc_ref, bc_near_ref, bc_far_ref = refs[9:]
    _, _, is_first, is_last = place()
    low, high = HALO, HALO + rows
    total = rows + 2 * HALO
    receive_edges(level, HALO, HALO, rows, ext, near_ref, far_ref)
    shift_rows(level, ext, e_ref, w_ref, 0, low, 3)
    shift_rows(level, ext, e_ref, w_ref, high, total, 3)
    advance_rows(level, b_ref, ext, e_ref, w_ref, 1, low + 1, 3)
    advance_rows(level, b_ref, ext, e_ref, w_ref, high - 1, total - 1, 3)
    sweep(level, v_one, 0, ext, 0, b_ref, 0, 1, low + 2, 4, (e_ref, w_ref))
    sweep(level, v_one, 0, ext, 0, b_ref, 0, high - 2, total - 1, 4, (e_ref, w_ref))

    def trim(ref):
        @pl.when(is_first)
        def _():
            clear(ref, level, 0, HALO)

        @pl.when(is_last)
        def _():
            clear(ref, level, high, total)

    trim(v_one)
    sweep(level, v_two, 0, v_one, 0, b_ref, 0, 2, low + 3, 4)
    sweep(level, v_two, 0, v_one, 0, b_ref, 0, high - 3, total - 2, 4)
    trim(v_two)
    half = rows // 2
    restrict(level, bc_ref, 0, coarse, v_two, HALO, b_ref, HALO, 0, 2, 2)
    restrict(level, bc_ref, 0, coarse, v_two, HALO, b_ref, HALO, half - 2, half, 2)
    send_edges(coarse, MID_HALO, 0, half, bc_ref, bc_near_ref, bc_far_ref)


def emit(level, rows, b_ref, next_ref, native, sems):
    copies = []
    for layer in range(2):
        for group in range(rows // SUBS):
            rows_of = pl.ds(group * SUBS, SUBS)
            to_native(level, native, group * SUBS, b_ref, layer, HALO + group * SUBS, -1)
            copies.append(
                pltpu.make_async_copy(
                    native.at[layer, rows_of], next_ref.at[layer, rows_of],
                    sems.at[layer, group],
                )
            )
            copies[-1].start()
    return copies


def middle_kernel(
    fine, level, two, three, rows, b_own, near_ref, far_ref, v0_ref,
    b_ref, v_ref, b2_ref, v2_ref, out_ref, two_near_ref, two_far_ref,
    v_one, w_two, b3,
):
    _, odd, is_first, is_last = place()
    total = rows + 2 * MID_HALO
    own = rows // 2
    edge = MID_HALO * level.size
    b_ref[:, edge : edge + rows * level.size, :] = b_own[...]
    receive_edges(level, MID_HALO, MID_HALO, rows, b_ref, near_ref, far_ref)
    start(level, v_one, 0, b_ref, 0, 0, total, 4)

    def trim(ref, of, halo, n):
        @pl.when(is_first)
        def _():
            clear(ref, of, 0, halo)

        @pl.when(is_last)
        def _():
            clear(ref, of, halo + n, 2 * halo + n)

    trim(v_one, level, MID_HALO, rows)
    sweep(level, v_ref, 0, v_one, 0, b_ref, 0, 1, total - 1, 6)
    trim(v_ref, level, MID_HALO, rows)
    restrict(
        level, b2_ref, TWO_HALO, two, v_ref, MID_HALO, b_ref, MID_HALO, -2, own + 2, 4
    )
    start(two, w_two, TWO_HALO, b2_ref, TWO_HALO, -2, own + 2, 8)
    trim(w_two, two, TWO_HALO, own)
    sweep(two, v2_ref, TWO_HALO, w_two, TWO_HALO, b2_ref, TWO_HALO, -1, own + 1, 6)
    trim(v2_ref, two, TWO_HALO, own)
    restrict(
        two, b3, 0, three, v2_ref, TWO_HALO, b2_ref, TWO_HALO, 0, own // 2, 2
    )
    even = lane_index() % 2 == 0
    for layer in range(2):
        for pair in range(own // 4):
            row = jnp.where(
                even,
                b3[layer, at(three, 2 * pair), :],
                b3[layer, at(three, 2 * pair + 1), :],
            )
            for copy in range(out_ref.shape[0]):
                out_ref[copy, layer, at(three, pair), :] = row
    up, down = pl.ds((TWO_HALO + 1) * two.size, 3 * two.size), pl.ds(
        own * two.size, 3 * two.size
    )
    up_b, down_b = at(two, TWO_HALO + 2), at(two, TWO_HALO + own - 3)
    last = pl.ds(3 * two.size, two.size)

    tail = pl.ds(4 * two.size, fine.size)
    up_0 = pl.ds((HALO + 1) * fine.size, fine.size)
    down_0 = pl.ds((HALO + 2 * rows - 2) * fine.size, fine.size)

    def send(ref, rows_v, row_b, row_0):
        ref[:, 0 : 3 * two.size, :] = v2_ref[:, rows_v, :]
        ref[:, last, :] = b2_ref[:, row_b, :]
        ref[:, tail, :] = v0_ref[:, row_0, :]

    @pl.when(odd == 1)
    def _():
        send(two_near_ref, up, up_b, up_0)
        send(two_far_ref, down, down_b, down_0)

    @pl.when(odd == 0)
    def _():
        send(two_near_ref, down, down_b, down_0)
        send(two_far_ref, up, up_b, up_0)


PAD = 4


def coarse_solve(level, dst, dst_at, b_ref, n):
    groups = level.stride
    m = n // groups
    part = lane_index() % groups
    source = []
    for layer in range(2):
        source.append([])
        for k in range(m):
            tile = load(b_ref, level, layer, k)[0]
            for g in range(1, groups):
                tile = jnp.where(part == g, load(b_ref, level, layer, g * m + k)[0], tile)
            source[layer].append(level.src[layer] * tile)
    values = source
    for _ in range(COARSE_SWEEPS - 1):
        new = []
        for layer in range(2):
            v, o = values[layer], values[1 - layer]
            below = jnp.where(part == groups - 1, 0.0, pltpu.roll(v[0], LANES - 1, 1))
            above = jnp.where(part == 0, 0.0, pltpu.roll(v[-1], 1, 1))
            out = []
            for k in range(m):
                n_row = v[k + 1] if k + 1 < m else below
                s_row = v[k - 1] if k else above
                e, w = east([v[k]], groups)[0], west([v[k]], groups)[0]
                out.append(
                    (level.keep * v[k] + level.near[layer] * ((n_row + s_row) + (e + w)))
                    + (level.other[layer] * o[k] + source[layer][k])
                )
            new.append(out)
        values = new
    for layer in range(2):
        for k in range(m):
            moved = {
                d: pltpu.roll(values[layer][k], d % LANES, 1) if d else values[layer][k]
                for d in range(1 - groups, groups)
            }
            for g in range(groups):
                tile = moved[-g]
                for j in range(1, groups):
                    tile = jnp.where(part == j, moved[j - g], tile)
                dst[layer, at(level, dst_at + g * m + k), :] = tile


def coarse_kernel(
    levels, rows, same_ref, other_ref, b0_ref, out_ref, next_ref,
    b3, v3, w3, b4, v4, native, sems,
):
    me, odd, is_first, is_last = place()
    fine, three, four = levels
    copies = emit(fine, rows, b0_ref, next_ref, native, sems)
    own = rows // 4
    chips = same_ref.shape[0]
    n3, n4 = chips * own, chips * own // 2
    for ref, level, n in ((b3, three, n3), (v3, three, n3), (w3, three, n3), (v4, four, n4)):
        clear(ref, level, 0, PAD)
        clear(ref, level, PAD + n, 2 * PAD + n)
    even = lane_index() % 2 == 0

    def gather_body(chip, carry):
        for ref, core in ((same_ref, odd), (other_ref, 1 - odd)):
            row = (2 * chip + core) * (own // 2) + PAD
            for layer in range(2):
                for pair in range(own // 4):
                    both = ref[chip, layer, at(three, pair), :]
                    first = jnp.where(even, both, pltpu.roll(both, 1, 1))
                    second = jnp.where(even, pltpu.roll(both, LANES - 1, 1), both)
                    b3[layer, at(three, row + 2 * pair), :] = first
                    b3[layer, at(three, row + 2 * pair + 1), :] = second
        return carry

    lax.fori_loop(0, chips, gather_body, 0, unroll=min(chips, 8))

    start(three, v3, PAD, b3, PAD, 0, n3, 8)
    sweep(three, w3, PAD, v3, PAD, b3, PAD, 0, n3, 16, straight=0)
    restrict(three, b4, 0, four, w3, PAD, b3, PAD, 0, n4, 8, straight=0)
    coarse_solve(four, v4, PAD, b4, n4)

    def trim(ref, level, n):
        @pl.when(me < 2)
        def _():
            clear(ref, level, 0, PAD)

        @pl.when(me >= 2 * chips - 2)
        def _():
            clear(ref, level, PAD + n, 2 * PAD + n)

    half, quarter = own // 2, own // 4
    correct(three, four, v3, PAD, w3, PAD, v4, PAD, me * quarter - 2, quarter + 4, 8)
    sweep(three, w3, PAD, v3, PAD, b3, PAD, me * half - 3, half + 6, 8)
    trim(w3, three, n3)
    sweep(three, out_ref, 2 - me * half, w3, PAD, b3, PAD, me * half - 2, half + 4, 8)

    @pl.when(is_first)
    def _():
        clear(out_ref, three, 0, 2)

    @pl.when(is_last)
    def _():
        clear(out_ref, three, half + 2, half + 4)

    for copy in copies:
        copy.wait()


def rise_kernel(
    levels, rows, v3_ref, near_ref, far_ref,
    b2_ref, v2_ref, b1_ref, v1_ref, b0_ref, v0_in, out_ref, v0_ref,
    b2, v2, x2, y2, x1, y1, x0, y0, z0, native, sems,
):
    _, odd, is_first, is_last = place()
    fine, mid, two, three = levels
    own = rows // 4

    b2[...] = b2_ref[...]
    v2[...] = v2_ref[...]

    def take(ref, zero):
        top_v, low_v = pl.ds(0, 3 * two.size), pl.ds((TWO_HALO + own + 1) * two.size, 3 * two.size)
        top_b, low_b = at(two, TWO_HALO - 3), at(two, TWO_HALO + own + 2)
        last = pl.ds(3 * two.size, two.size)

        tail = pl.ds(4 * two.size, fine.size)
        top_0 = pl.ds((HALO - 2) * fine.size, fine.size)
        low_0 = pl.ds((HALO + rows + 1) * fine.size, fine.size)

        def drop(values):
            return values if zero is None else jnp.where(zero, 0.0, values)

        def put(rows_v, row_b, row_0):
            v2[:, rows_v, :] = drop(ref[:, 0 : 3 * two.size, :])
            b2[:, row_b, :] = ref[:, last, :]
            v0_ref[:, row_0, :] = drop(ref[:, tail, :])

        return lambda: put(top_v, top_b, top_0), lambda: put(low_v, low_b, low_0)

    near_top, near_low = take(near_ref, None)
    far_top, far_low = take(far_ref, jnp.logical_or(is_first, is_last))

    @pl.when(odd == 1)
    def _():
        near_top()
        far_low()

    @pl.when(odd == 0)
    def _():
        near_low()
        far_top()

    def trim_own(ref, level, halo, n):
        @pl.when(is_first)
        def _():
            clear(ref, level, 0, halo)

        @pl.when(is_last)
        def _():
            clear(ref, level, halo + n, 2 * halo + n)

    total = own + 2 * TWO_HALO
    correct(two, three, x2, 0, v2, 0, v3_ref, 0, 0, total // 2, 8)
    sweep(two, y2, 0, x2, 0, b2, 0, 1, total - 1, 10)
    trim_own(y2, two, TWO_HALO, own)
    sweep(two, x2, 0, y2, 0, b2, 0, 2, total - 2, 8)
    trim_own(x2, two, TWO_HALO, own)

    n1 = rows // 2
    total = n1 + 2 * MID_HALO

    correct(
        mid, two, x1, MID_HALO - 4, v1_ref, MID_HALO - 4, x2, TWO_HALO - 2, 0, n1 // 2 + 4, 4
    )
    sweep(mid, y1, 0, x1, 0, b1_ref, 0, MID_HALO - 2, MID_HALO + n1 + 2, 6)
    trim_own(y1, mid, MID_HALO, n1)
    sweep(mid, x1, 0, y1, 0, b1_ref, 0, MID_HALO - 1, MID_HALO + n1 + 1, 5)
    trim_own(x1, mid, MID_HALO, n1)

    low, done, swept = HALO, 0, HALO - 1
    copies = []
    for group in range(rows // SUBS):
        first_row = low + group * SUBS
        rows_of = pl.ds(group * SUBS, SUBS)
        ready = SUBS // 2 * (group + 1) + 2
        correct(fine, mid, x0, HALO - 2, v0_ref, HALO - 2, x1, MID_HALO - 1, done, ready, 2)
        sweep(fine, y0, 0, x0, 0, b0_ref, 0, swept, first_row + SUBS + 1, 5 - group)
        trim_own(y0, fine, HALO, rows)
        done, swept = ready, first_row + SUBS + 1
        sweep(fine, z0, 0, y0, 0, b0_ref, 0, first_row, first_row + SUBS, 4)
        for layer in range(2):
            to_native(fine, native, group * SUBS, z0, layer, first_row)
            copies.append(
                pltpu.make_async_copy(
                    native.at[layer, rows_of], out_ref.at[layer, rows_of],
                    sems.at[layer, group],
                )
            )
            copies[-1].start()
    for copy in copies:
        copy.wait()


def shape(*dims):
    return jax.ShapeDtypeStruct(dims, jnp.float32)


def scratch(layers, rows, level):
    return pltpu.VMEM((layers, rows * level.size, LANES), jnp.float32)


HBM = pl.BlockSpec(memory_space=pltpu.HBM)
VMEM = pl.BlockSpec(memory_space=pltpu.VMEM)


def call(kernel, out_shape, scratch_shapes=(), cost=None, limit=24, **options):
    if cost is not None:
        cost = pl.CostEstimate(flops=cost, bytes_accessed=cost // 8, transcendentals=0)
    return pl.pallas_call(
        kernel,
        out_shape=out_shape,
        scratch_shapes=list(scratch_shapes),
        cost_estimate=cost,
        compiler_params=pltpu.CompilerParams(vmem_limit_bytes=limit * 1024 * 1024),
        **options,
    )


def shards(stream_now, vorticity):
    _, rows, columns = stream_now.shape
    count = lax.axis_size("wide")
    tiles = columns // (SUBS * LANES)
    fine, mid = Level(0, tiles, 1), Level(1, tiles // 2, 1)
    two, three, four = Level(2, tiles // 4, 1), Level(3, tiles // 4, 2), Level(4, tiles // 4, 4)
    core_swap = [(i, i ^ 1) for i in range(count)]
    members = lax.axis_size("member")
    inside = [(i, ((i + 1) ^ 1) - 1) for i in range(1, count - 1)]
    if members % 2:
        ends = [(0, count - 1), (count - 1, 0)]
        chip_swap = [(m * count + i, m * count + j) for m in range(members) for i, j in ends]
    else:
        chip_swap = [
            (m * count + i, (m ^ 1) * count + i) for m in range(members) for i in (0, count - 1)
        ]
    chip_swap += [(m * count + i, m * count + j) for m in range(members) for i, j in inside]
    groups = rows // SUBS

    def exchange(near, far):
        far = lax.ppermute(far, ("member", "wide"), chip_swap)
        near = lax.ppermute(near, "wide", core_swap)
        return near, far

    half, quarter = rows // 2, rows // 4
    total = rows + 2 * HALO
    ext, near, far = call(
        functools.partial(pack_kernel, fine, rows),
        [shape(4, total * fine.size, LANES)] + [shape(4, HALO * fine.size, LANES)] * 2,
        [pltpu.VMEM((4, rows, columns), jnp.float32), pltpu.SemaphoreType.DMA((4,))],
        in_specs=[HBM, HBM],
    )(*(pltpu.with_memory_space_constraint(x, pltpu.HBM) for x in (stream_now, vorticity)))
    near, far = exchange(near, far)
    state = [
        shape(4, total * fine.size, LANES),
        shape(4, total * fine.size, LANES),
        shape(2, total * fine.size, LANES),
        shape(2, total * fine.size, LANES),
        shape(2, total * fine.size, LANES),
        shape(2, half * mid.size, LANES),
    ]
    inner = call(
        functools.partial(inner_kernel, fine, mid, rows),
        state,
        cost=8000000,
    )(ext)
    edge = shape(2, MID_HALO * mid.size, LANES)
    outer = call(
        functools.partial(outer_kernel, fine, mid, rows),
        [shape(4, total * fine.size, LANES)] + state + [edge, edge],
        input_output_aliases={i: i for i in range(7)},
    )(ext, *inner, near, far)
    b0, v0, b1, near, far = outer[3], outer[5], outer[6], outer[7], outer[8]
    near, far = exchange(near, far)
    chips = count // 2
    eighth = rows // 8
    two_edge = shape(2, 4 * two.size + fine.size, LANES)
    two_all = shape(2, (quarter + 2 * TWO_HALO) * two.size, LANES)
    b1, v1, b2, v2, b3, near, far = call(
        functools.partial(middle_kernel, fine, mid, two, three, half),
        [
            shape(2, (half + 2 * MID_HALO) * mid.size, LANES),
            shape(2, (half + 2 * MID_HALO) * mid.size, LANES),
            two_all,
            two_all,
            shape(chips, 2, eighth // 2 * three.size, LANES),
            two_edge,
            two_edge,
        ],
        [
            scratch(2, half + 2 * MID_HALO, mid),
            scratch(2, quarter + 2 * TWO_HALO, two),
            scratch(2, eighth, three),
        ],
    )(b1, near, far, v0)
    cores = [[i for i in range(count) if i % 2 == c] for c in range(2)]
    same = lax.all_to_all(b3, "wide", 0, 0, axis_index_groups=cores)
    other = lax.ppermute(same, "wide", core_swap)
    near, far = exchange(near, far)
    n3, n4 = count * eighth, count * eighth // 2
    v3, vorticity_next = call(
        functools.partial(coarse_kernel, (fine, three, four), rows),
        [shape(2, (eighth + 4) * three.size, LANES), shape(2, rows, columns)],
        [scratch(2, n3 + 2 * PAD, three)] * 3
        + [scratch(2, n4, four), scratch(2, n4 + 2 * PAD, four)]
        + [pltpu.VMEM((2, rows, columns), jnp.float32), pltpu.SemaphoreType.DMA((2, groups))],
        cost=5000000,
        out_specs=[VMEM, HBM],
    )(same, other, b0)
    stream_next, _ = call(
        functools.partial(rise_kernel, (fine, mid, two, three), rows),
        [shape(2, rows, columns), shape(2, total * fine.size, LANES)],
        [scratch(2, quarter + 2 * TWO_HALO, two)] * 4
        + [scratch(2, half + 2 * MID_HALO, mid)] * 2
        + [scratch(2, total, fine)] * 3
        + [pltpu.VMEM((2, rows, columns), jnp.float32), pltpu.SemaphoreType.DMA((2, groups))],
        out_specs=[HBM, VMEM],
        input_output_aliases={8: 1},
    )(v3, near, far, b2, v2, b1, v1, b0, v0)
    return (vorticity_next, stream_next)


def solution(mesh):
    return jax.shard_map(
        shards,
        mesh=mesh,
        in_specs=(P("member", "wide", None), P("member", "wide", None)),
        out_specs=(P("member", "wide", None), P("member", "wide", None)),
        check_vma=False,
    )
```

```python
import functools

import jax
import jax.numpy as jnp
from jax import lax
from jax.experimental import pallas as pl
from jax.experimental.pallas import tpu as pltpu
from jax.sharding import PartitionSpec as P


LANES = 128
SUBS = 8
HALO = 3
MID_HALO = 6
LATE = 2
TWO_HALO = 4
RELAX = 0.8
COUPLING = (0.02, 0.04)
TIME_STEP = 0.5
BETA = 0.05
DRAG = (0.0, 0.02)
COARSE_SWEEPS = 8


class Level:
    def __init__(self, level, tiles, stride):
        h2 = (2.0**level) ** 2
        self.tiles, self.stride = tiles, stride
        diag = [4.0 / h2 + f for f in COUPLING]
        self.keep = 1.0 - RELAX
        self.near = [RELAX / (d * h2) for d in diag]
        self.other = [RELAX * f / d for f, d in zip(COUPLING, diag)]
        self.src = [RELAX / d for d in diag]
        self.diag = diag
        self.inv_h2 = 1.0 / h2
        self.size = tiles * SUBS


def lane_index():
    return lax.broadcasted_iota(jnp.int32, (SUBS, LANES), 1)


def at(level, row, tile=0):
    base = row * level.size
    if not isinstance(row, int):
        base = pl.multiple_of(base, SUBS)
    return pl.ds(base + tile * SUBS, SUBS)


def load(ref, level, layer, row):
    return [ref[layer, at(level, row, t), :] for t in range(level.tiles)]


def store(ref, level, layer, row, values):
    for t in range(level.tiles):
        ref[layer, at(level, row, t), :] = values[t]


def east(values, stride=1):
    rolled = [pltpu.roll(v, LANES - stride, 1) for v in values]
    after = rolled[1:] + [pltpu.roll(rolled[0], SUBS - 1, 0)]
    edge = lane_index() >= LANES - stride
    return [jnp.where(edge, a, r) for a, r in zip(after, rolled)]


def west(values, stride=1):
    rolled = [pltpu.roll(v, stride, 1) for v in values]
    before = [pltpu.roll(rolled[-1], 1, 0)] + rolled[:-1]
    edge = lane_index() < stride
    return [jnp.where(edge, b, r) for b, r in zip(before, rolled)]


def transpose_tiles(tiles):
    sub = lax.broadcasted_iota(jnp.int32, (SUBS, LANES), 0)
    for k in (1, 2, 4):
        keep = (sub & k) == 0
        out = list(tiles)
        for i in range(SUBS):
            if not i & k:
                a, b = tiles[i], tiles[i + k]
                out[i] = jnp.where(keep, a, pltpu.roll(b, k, 0))
                out[i + k] = jnp.where(keep, pltpu.roll(a, SUBS - k, 0), b)
        tiles = out
    return tiles


def column_of(level, t, s):
    first = (s * level.tiles + t) * LANES
    return slice(first, first + LANES)


def to_native(level, dst, dst_row, src, layer, src_row, sign=1):
    for t in range(level.tiles):
        tiles = [src[layer, at(level, src_row + r, t), :] for r in range(SUBS)]
        for s, tile in enumerate(transpose_tiles(tiles)):
            dst[layer, dst_row : dst_row + SUBS, column_of(level, t, s)] = (
                tile if sign > 0 else -tile
            )


def row_blocks(low, high, block, body, straight=48):
    count = high - low if isinstance(low, int) else high
    if count <= straight:
        block = count
    whole = count // block
    if whole > 1:
        lax.fori_loop(0, whole, lambda i, c: (body(low + i * block, block), c)[1], 0)
    elif whole == 1:
        body(low, block)
    if count % block:
        body(low + whole * block, count % block)


def star(rows, k, layer, level, sides=None):
    centre = rows[k][layer]
    if sides:
        e, w = sides[0][k][layer], sides[1][k][layer]
    else:
        e, w = east(centre, level.stride), west(centre, level.stride)
    return [
        (n + s) + (a + b)
        for n, s, a, b in zip(rows[k + 1][layer], rows[k - 1][layer], e, w)
    ]


def load_rows(ref, level, first, count, margin=1):
    return {
        k: [load(ref, level, layer, first + k) for layer in range(2)]
        for k in range(-margin, count + margin)
    }


def sweep_rows(level, rows, source, count, sides=None):
    out = {}
    for k in range(count):
        out[k] = []
        for layer in range(2):
            near = star(rows, k, layer, level, sides)
            out[k].append(
                [
                    (level.keep * c + level.near[layer] * n)
                    + (level.other[layer] * o + level.src[layer] * b)
                    for c, n, o, b in zip(
                        rows[k][layer], near, rows[k][1 - layer], source[k][layer]
                    )
                ]
            )
    return out


def residual_rows(level, rows, source, count):
    out = {}
    for k in range(count):
        out[k] = []
        for layer in range(2):
            near = star(rows, k, layer, level)
            out[k].append(
                [
                    (b - level.diag[layer] * c)
                    + (level.inv_h2 * n + COUPLING[layer] * o)
                    for c, n, o, b in zip(
                        rows[k][layer], near, rows[k][1 - layer], source[k][layer]
                    )
                ]
            )
    return out


def store_rows(ref, level, first, rows, count):
    for k in range(count):
        for layer in range(2):
            store(ref, level, layer, first + k, rows[k][layer])


def sweep(level, dst, dst_at, src, src_at, b, b_at, low, high, block, shifted=None, straight=48):
    def body(first, count):
        rows = load_rows(src, level, first + src_at, count)
        source = load_rows(b, level, first + b_at, count, 0)
        sides = None
        if shifted:
            sides = [load_rows(ref, level, first + src_at, count, 0) for ref in shifted]
        out = sweep_rows(level, rows, source, count, sides)
        store_rows(dst, level, first + dst_at, out, count)

    row_blocks(low, high, block, body, straight)


def start(level, dst, dst_at, b, b_at, low, high, block):
    def body(first, count):
        source = load_rows(b, level, first + b_at, count, 0)
        out = {
            k: [[level.src[l] * x for x in source[k][l]] for l in range(2)]
            for k in range(count)
        }
        store_rows(dst, level, first + dst_at, out, count)

    row_blocks(low, high, block, body)


def pack_columns(values):
    lane = lane_index()
    pick = (2 * lane) % LANES
    sums = [v + pltpu.roll(v, LANES - 1, 1) for v in values]
    picked = [jnp.take_along_axis(s, pick, axis=1) for s in sums]
    return [
        jnp.where(lane < LANES // 2, picked[2 * t], picked[2 * t + 1])
        for t in range(len(values) // 2)
    ]


def spread_columns(values):
    lane = lane_index()
    out = []
    for v in values:
        out.append(jnp.take_along_axis(v, lane // 2, axis=1))
        out.append(jnp.take_along_axis(v, LANES // 2 + lane // 2, axis=1))
    return out


def merge_columns(values, stride):
    even = (lane_index() // stride) % 2 == 0
    return [
        v + jnp.where(even, pltpu.roll(v, LANES - stride, 1), pltpu.roll(v, stride, 1))
        for v in values
    ]


def restrict(
    fine, dst, dst_at, coarse, src, src_at, b, b_at, low, high, block, straight=48
):
    def body(first, count):
        rows = load_rows(src, fine, 2 * first + src_at, 2 * count)
        source = load_rows(b, fine, 2 * first + b_at, 2 * count, 0)
        res = residual_rows(fine, rows, source, 2 * count)
        out = {}
        for k in range(count):
            out[k] = []
            for layer in range(2):
                pair = [x + y for x, y in zip(res[2 * k][layer], res[2 * k + 1][layer])]
                if coarse.tiles < fine.tiles:
                    pair = pack_columns(pair)
                else:
                    pair = merge_columns(pair, fine.stride)
                out[k].append([0.25 * x for x in pair])
        store_rows(dst, coarse, first + dst_at, out, count)

    row_blocks(low, high, block, body, straight)


def correct(fine, coarse, dst, dst_at, src, src_at, add, add_at, low, high, block):
    def body(first, count):
        coarse_rows = load_rows(add, coarse, first + add_at, count, 0)
        fine_rows = load_rows(src, fine, 2 * first + src_at, 2 * count, 0)
        out = {}
        for k in range(count):
            spread = [
                spread_columns(v) if coarse.tiles < fine.tiles else v for v in coarse_rows[k]
            ]
            for half in range(2):
                out[2 * k + half] = [
                    [x + y for x, y in zip(fine_rows[2 * k + half][l], spread[l])]
                    for l in range(2)
                ]
        store_rows(dst, fine, 2 * first + dst_at, out, 2 * count)

    row_blocks(low, high, block, body)


def clear(ref, level, low, high):
    ref[:, low * level.size : high * level.size, :] = jnp.zeros(
        (ref.shape[0], (high - low) * level.size, LANES), jnp.float32
    )


def place():
    me, count = lax.axis_index("wide"), lax.axis_size("wide")
    return me, lax.rem(me, 2), me == 0, me == count - 1


def pack_kernel(level, rows, p_ref, q_ref, ext_ref, near_ref, far_ref, native, sems):
    copies = []
    for field, ref in enumerate((p_ref, q_ref)):
        for layer in range(2):
            which = 2 * field + layer
            copies.append(
                pltpu.make_async_copy(ref.at[layer], native.at[which], sems.at[which])
            )
            copies[-1].start()
    for which in range(4):
        copies[which].wait()
        for group in range(rows // SUBS):
            for t in range(level.tiles):
                tiles = [
                    native[which, group * SUBS : (group + 1) * SUBS, column_of(level, t, s)]
                    for s in range(SUBS)
                ]
                for r, tile in enumerate(transpose_tiles(tiles)):
                    ext_ref[which, at(level, HALO + group * SUBS + r, t), :] = tile
    send_edges(level, HALO, HALO, rows, ext_ref, near_ref, far_ref)


def send_edges(level, width, src_at, rows, src, near_ref, far_ref):
    _, odd, _, _ = place()
    size = width * level.size
    last = (src_at + rows - width) * level.size
    top = src_at * level.size
    near = pl.multiple_of(jnp.where(odd == 1, top, last), SUBS)
    far = pl.multiple_of(jnp.where(odd == 1, last, top), SUBS)
    near_ref[:, 0:size, :] = src[:, pl.ds(near, size), :]
    far_ref[:, 0:size, :] = src[:, pl.ds(far, size), :]


def receive_edges(level, width, dst_at, rows, dst, near_ref, far_ref):
    _, odd, first, last = place()
    size = width * level.size
    low = (dst_at + rows) * level.size
    top = (dst_at - width) * level.size
    near = pl.multiple_of(jnp.where(odd == 1, top, low), SUBS)
    far = pl.multiple_of(jnp.where(odd == 1, low, top), SUBS)
    dst[:, pl.ds(near, size), :] = near_ref[:, 0:size, :]
    outside = jnp.logical_or(first, last)
    dst[:, pl.ds(far, size), :] = jnp.where(outside, 0.0, far_ref[:, 0:size, :])


def shift_rows(level, ext, e_ref, w_ref, low, high, block):
    def body(first, count):
        for k in range(count):
            for f in range(4):
                v = load(ext, level, f, first + k)
                store(e_ref, level, f, first + k, east(v))
                store(w_ref, level, f, first + k, west(v))

    row_blocks(low, high, block, body)


def advance_rows(level, b_ref, ext, e_ref, w_ref, low, high, block):
    def body(first, count):
        for layer in range(2):
            for t in range(level.tiles):
                def grab(ref, field):
                    return {
                        k: ref[2 * field + layer, at(level, first + k, t), :]
                        for k in range(-1, count + 1)
                    }

                p, pe, pw = grab(ext, 0), grab(e_ref, 0), grab(w_ref, 0)
                q, qe, qw = grab(ext, 1), grab(e_ref, 1), grab(w_ref, 1)
                zonal = {k: pe[k] - pw[k] for k in p}
                for k in range(count):
                    n, s = k + 1, k - 1
                    v0, ve, vw = p[n] - p[s], pe[n] - pe[s], pw[n] - pw[s]
                    jac = q[n] * (zonal[k] + zonal[n]) - q[s] * (zonal[k] + zonal[s])
                    jac = jac - qe[k] * (v0 + ve) + qw[k] * (v0 + vw)
                    jac = jac + qe[n] * (pe[k] - p[n]) - qe[s] * (pe[k] - p[s])
                    jac = jac - qw[n] * (pw[k] - p[n]) + qw[s] * (pw[k] - p[s])
                    step = (TIME_STEP / 12.0) * jac + (0.5 * TIME_STEP * BETA) * zonal[k]
                    if layer == 1:
                        lap = (p[n] + p[s]) + (pe[k] + pw[k]) - 4.0 * p[k]
                        step = step + (TIME_STEP * DRAG[1]) * lap
                    b_ref[layer, at(level, first + k, t), :] = step - q[k]

    row_blocks(low, high, block, body)


def inner_kernel(
    level, coarse, rows, ext, e_ref, w_ref, b_ref, v_one, v_two, bc_ref, early_near, early_far
):
    low, high = HALO, HALO + rows
    shift_rows(level, ext, e_ref, w_ref, low, high, 4)
    advance_rows(level, b_ref, ext, e_ref, w_ref, low + 1, high - 1, 2)
    sweep(level, v_one, 0, ext, 0, b_ref, 0, low + 2, high - 2, 4, (e_ref, w_ref))
    sweep(level, v_two, 0, v_one, 0, b_ref, 0, low + 3, high - 3, 4)
    restrict(level, bc_ref, 0, coarse, v_two, HALO, b_ref, HALO, LATE, rows // 2 - LATE, 2)
    size = (MID_HALO - LATE) * coarse.size
    first, last = LATE * coarse.size, (rows // 2 - MID_HALO) * coarse.size
    _, odd, _, _ = place()
    near = pl.multiple_of(jnp.where(odd == 1, first, last), SUBS)
    far = pl.multiple_of(jnp.where(odd == 1, last, first), SUBS)
    early_near[...] = bc_ref[:, pl.ds(near, size), :]
    early_far[...] = bc_ref[:, pl.ds(far, size), :]


def outer_kernel(level, coarse, rows, *refs):
    near_ref, far_ref = refs[7:9]
    ext, e_ref, w_ref, b_ref, v_one, v_two, bc_ref, bc_near_ref, bc_far_ref = refs[9:]
    _, _, is_first, is_last = place()
    low, high = HALO, HALO + rows
    total = rows + 2 * HALO
    receive_edges(level, HALO, HALO, rows, ext, near_ref, far_ref)
    shift_rows(level, ext, e_ref, w_ref, 0, low, 3)
    shift_rows(level, ext, e_ref, w_ref, high, total, 3)
    advance_rows(level, b_ref, ext, e_ref, w_ref, 1, low + 1, 3)
    advance_rows(level, b_ref, ext, e_ref, w_ref, high - 1, total - 1, 3)
    sweep(level, v_one, 0, ext, 0, b_ref, 0, 1, low + 2, 4, (e_ref, w_ref))
    sweep(level, v_one, 0, ext, 0, b_ref, 0, high - 2, total - 1, 4, (e_ref, w_ref))

    def trim(ref):
        @pl.when(is_first)
        def _():
            clear(ref, level, 0, HALO)

        @pl.when(is_last)
        def _():
            clear(ref, level, high, total)

    trim(v_one)
    sweep(level, v_two, 0, v_one, 0, b_ref, 0, 2, low + 3, 4)
    sweep(level, v_two, 0, v_one, 0, b_ref, 0, high - 3, total - 2, 4)
    trim(v_two)
    half = rows // 2
    restrict(level, bc_ref, 0, coarse, v_two, HALO, b_ref, HALO, 0, LATE, 2)
    restrict(level, bc_ref, 0, coarse, v_two, HALO, b_ref, HALO, half - LATE, half, 2)
    send_edges(coarse, LATE, 0, half, bc_ref, bc_near_ref, bc_far_ref)


def emit(level, rows, b_ref, next_ref, native, sems):
    copies = []
    for layer in range(2):
        for group in range(rows // SUBS):
            rows_of = pl.ds(group * SUBS, SUBS)
            to_native(level, native, group * SUBS, b_ref, layer, HALO + group * SUBS, -1)
            copies.append(
                pltpu.make_async_copy(
                    native.at[layer, rows_of], next_ref.at[layer, rows_of],
                    sems.at[layer, group],
                )
            )
            copies[-1].start()
    return copies


def emit_kernel(level, rows, b_ref, next_ref, native, sems):
    for copy in emit(level, rows, b_ref, next_ref, native, sems):
        copy.wait()


def middle_kernel(
    fine, level, two, three, rows, b_own, early_near, early_far, near_ref, far_ref, v0_ref,
    b_ref, v_ref, b2_ref, v2_ref, out_ref, two_near_ref, two_far_ref,
    v_one, w_two, b3,
):
    _, odd, is_first, is_last = place()
    total = rows + 2 * MID_HALO
    own = rows // 2
    edge = MID_HALO * level.size
    b_ref[:, edge : edge + rows * level.size, :] = b_own[...]
    receive_edges(level, LATE, MID_HALO, rows, b_ref, near_ref, far_ref)
    early = MID_HALO - LATE
    receive_edges(level, early, early, rows + 2 * LATE, b_ref, early_near, early_far)
    start(level, v_one, 0, b_ref, 0, 0, total, 4)

    def trim(ref, of, halo, n):
        @pl.when(is_first)
        def _():
            clear(ref, of, 0, halo)

        @pl.when(is_last)
        def _():
            clear(ref, of, halo + n, 2 * halo + n)

    trim(v_one, level, MID_HALO, rows)
    sweep(level, v_ref, 0, v_one, 0, b_ref, 0, 1, total - 1, 6)
    trim(v_ref, level, MID_HALO, rows)
    restrict(
        level, b2_ref, TWO_HALO, two, v_ref, MID_HALO, b_ref, MID_HALO, -2, own + 2, 4
    )
    start(two, w_two, TWO_HALO, b2_ref, TWO_HALO, -2, own + 2, 8)
    trim(w_two, two, TWO_HALO, own)
    sweep(two, v2_ref, TWO_HALO, w_two, TWO_HALO, b2_ref, TWO_HALO, -1, own + 1, 6)
    trim(v2_ref, two, TWO_HALO, own)
    restrict(
        two, b3, 0, three, v2_ref, TWO_HALO, b2_ref, TWO_HALO, 0, own // 2, 2
    )
    even = lane_index() % 2 == 0
    for layer in range(2):
        for pair in range(own // 4):
            row = jnp.where(
                even,
                b3[layer, at(three, 2 * pair), :],
                b3[layer, at(three, 2 * pair + 1), :],
            )
            for copy in range(out_ref.shape[0]):
                out_ref[copy, layer, at(three, pair), :] = row
    up, down = pl.ds((TWO_HALO + 1) * two.size, 3 * two.size), pl.ds(
        own * two.size, 3 * two.size
    )
    up_b, down_b = at(two, TWO_HALO + 2), at(two, TWO_HALO + own - 3)
    last = pl.ds(3 * two.size, two.size)

    tail = pl.ds(4 * two.size, fine.size)
    up_0 = pl.ds((HALO + 1) * fine.size, fine.size)
    down_0 = pl.ds((HALO + 2 * rows - 2) * fine.size, fine.size)

    def send(ref, rows_v, row_b, row_0):
        ref[:, 0 : 3 * two.size, :] = v2_ref[:, rows_v, :]
        ref[:, last, :] = b2_ref[:, row_b, :]
        ref[:, tail, :] = v0_ref[:, row_0, :]

    @pl.when(odd == 1)
    def _():
        send(two_near_ref, up, up_b, up_0)
        send(two_far_ref, down, down_b, down_0)

    @pl.when(odd == 0)
    def _():
        send(two_near_ref, down, down_b, down_0)
        send(two_far_ref, up, up_b, up_0)


PAD = 4


def coarse_solve(level, dst, dst_at, b_ref, n):
    groups = level.stride
    m = n // groups
    part = lane_index() % groups
    source = []
    for layer in range(2):
        source.append([])
        for k in range(m):
            tile = load(b_ref, level, layer, k)[0]
            for g in range(1, groups):
                tile = jnp.where(part == g, load(b_ref, level, layer, g * m + k)[0], tile)
            source[layer].append(level.src[layer] * tile)
    values = source
    for _ in range(COARSE_SWEEPS - 1):
        new = []
        for layer in range(2):
            v, o = values[layer], values[1 - layer]
            below = jnp.where(part == groups - 1, 0.0, pltpu.roll(v[0], LANES - 1, 1))
            above = jnp.where(part == 0, 0.0, pltpu.roll(v[-1], 1, 1))
            out = []
            for k in range(m):
                n_row = v[k + 1] if k + 1 < m else below
                s_row = v[k - 1] if k else above
                e, w = east([v[k]], groups)[0], west([v[k]], groups)[0]
                out.append(
                    (level.keep * v[k] + level.near[layer] * ((n_row + s_row) + (e + w)))
                    + (level.other[layer] * o[k] + source[layer][k])
                )
            new.append(out)
        values = new
    for layer in range(2):
        for k in range(m):
            moved = {
                d: pltpu.roll(values[layer][k], d % LANES, 1) if d else values[layer][k]
                for d in range(1 - groups, groups)
            }
            for g in range(groups):
                tile = moved[-g]
                for j in range(1, groups):
                    tile = jnp.where(part == j, moved[j - g], tile)
                dst[layer, at(level, dst_at + g * m + k), :] = tile


def coarse_kernel(
    levels, rows, same_ref, other_ref, out_ref, b3, v3, w3, b4, v4,
):
    me, odd, is_first, is_last = place()
    three, four = levels
    own = rows // 4
    chips = same_ref.shape[0]
    n3, n4 = chips * own, chips * own // 2
    for ref, level, n in ((b3, three, n3), (v3, three, n3), (w3, three, n3), (v4, four, n4)):
        clear(ref, level, 0, PAD)
        clear(ref, level, PAD + n, 2 * PAD + n)
    even = lane_index() % 2 == 0

    def gather_body(chip, carry):
        for ref, core in ((same_ref, odd), (other_ref, 1 - odd)):
            row = (2 * chip + core) * (own // 2) + PAD
            for layer in range(2):
                for pair in range(own // 4):
                    both = ref[chip, layer, at(three, pair), :]
                    first = jnp.where(even, both, pltpu.roll(both, 1, 1))
                    second = jnp.where(even, pltpu.roll(both, LANES - 1, 1), both)
                    b3[layer, at(three, row + 2 * pair), :] = first
                    b3[layer, at(three, row + 2 * pair + 1), :] = second
        return carry

    lax.fori_loop(0, chips, gather_body, 0, unroll=min(chips, 8))

    start(three, v3, PAD, b3, PAD, 0, n3, 8)
    sweep(three, w3, PAD, v3, PAD, b3, PAD, 0, n3, 16, straight=0)
    restrict(three, b4, 0, four, w3, PAD, b3, PAD, 0, n4, 8, straight=0)
    coarse_solve(four, v4, PAD, b4, n4)

    def trim(ref, level, n):
        @pl.when(me < 2)
        def _():
            clear(ref, level, 0, PAD)

        @pl.when(me >= 2 * chips - 2)
        def _():
            clear(ref, level, PAD + n, 2 * PAD + n)

    half, quarter = own // 2, own // 4
    correct(three, four, v3, PAD, w3, PAD, v4, PAD, me * quarter - 2, quarter + 4, 8)
    sweep(three, w3, PAD, v3, PAD, b3, PAD, me * half - 3, half + 6, 8)
    trim(w3, three, n3)
    sweep(three, out_ref, 2 - me * half, w3, PAD, b3, PAD, me * half - 2, half + 4, 8)

    @pl.when(is_first)
    def _():
        clear(out_ref, three, 0, 2)

    @pl.when(is_last)
    def _():
        clear(out_ref, three, half + 2, half + 4)


def rise_kernel(
    levels, rows, v3_ref, near_ref, far_ref,
    b2_ref, v2_ref, b1_ref, v1_ref, b0_ref, v0_in, out_ref, v0_ref,
    b2, v2, x2, y2, x1, y1, x0, y0, z0, native, sems,
):
    _, odd, is_first, is_last = place()
    fine, mid, two, three = levels
    own = rows // 4

    b2[...] = b2_ref[...]
    v2[...] = v2_ref[...]

    def take(ref, zero):
        top_v, low_v = pl.ds(0, 3 * two.size), pl.ds((TWO_HALO + own + 1) * two.size, 3 * two.size)
        top_b, low_b = at(two, TWO_HALO - 3), at(two, TWO_HALO + own + 2)
        last = pl.ds(3 * two.size, two.size)

        tail = pl.ds(4 * two.size, fine.size)
        top_0 = pl.ds((HALO - 2) * fine.size, fine.size)
        low_0 = pl.ds((HALO + rows + 1) * fine.size, fine.size)

        def drop(values):
            return values if zero is None else jnp.where(zero, 0.0, values)

        def put(rows_v, row_b, row_0):
            v2[:, rows_v, :] = drop(ref[:, 0 : 3 * two.size, :])
            b2[:, row_b, :] = ref[:, last, :]
            v0_ref[:, row_0, :] = drop(ref[:, tail, :])

        return lambda: put(top_v, top_b, top_0), lambda: put(low_v, low_b, low_0)

    near_top, near_low = take(near_ref, None)
    far_top, far_low = take(far_ref, jnp.logical_or(is_first, is_last))

    @pl.when(odd == 1)
    def _():
        near_top()
        far_low()

    @pl.when(odd == 0)
    def _():
        near_low()
        far_top()

    def trim_own(ref, level, halo, n):
        @pl.when(is_first)
        def _():
            clear(ref, level, 0, halo)

        @pl.when(is_last)
        def _():
            clear(ref, level, halo + n, 2 * halo + n)

    total = own + 2 * TWO_HALO
    correct(two, three, x2, 0, v2, 0, v3_ref, 0, 0, total // 2, 8)
    sweep(two, y2, 0, x2, 0, b2, 0, 1, total - 1, 10)
    trim_own(y2, two, TWO_HALO, own)
    sweep(two, x2, 0, y2, 0, b2, 0, 2, total - 2, 8)
    trim_own(x2, two, TWO_HALO, own)

    n1 = rows // 2
    total = n1 + 2 * MID_HALO

    correct(
        mid, two, x1, MID_HALO - 4, v1_ref, MID_HALO - 4, x2, TWO_HALO - 2, 0, n1 // 2 + 4, 4
    )
    sweep(mid, y1, 0, x1, 0, b1_ref, 0, MID_HALO - 2, MID_HALO + n1 + 2, 6)
    trim_own(y1, mid, MID_HALO, n1)
    sweep(mid, x1, 0, y1, 0, b1_ref, 0, MID_HALO - 1, MID_HALO + n1 + 1, 5)
    trim_own(x1, mid, MID_HALO, n1)

    low, done, swept = HALO, 0, HALO - 1
    copies = []
    for group in range(rows // SUBS):
        first_row = low + group * SUBS
        rows_of = pl.ds(group * SUBS, SUBS)
        ready = SUBS // 2 * (group + 1) + 2
        correct(fine, mid, x0, HALO - 2, v0_ref, HALO - 2, x1, MID_HALO - 1, done, ready, 2)
        sweep(fine, y0, 0, x0, 0, b0_ref, 0, swept, first_row + SUBS + 1, 5 - group)
        trim_own(y0, fine, HALO, rows)
        done, swept = ready, first_row + SUBS + 1
        sweep(fine, z0, 0, y0, 0, b0_ref, 0, first_row, first_row + SUBS, 4)
        for layer in range(2):
            to_native(fine, native, group * SUBS, z0, layer, first_row)
            copies.append(
                pltpu.make_async_copy(
                    native.at[layer, rows_of], out_ref.at[layer, rows_of],
                    sems.at[layer, group],
                )
            )
            copies[-1].start()
    for copy in copies:
        copy.wait()


def shape(*dims):
    return jax.ShapeDtypeStruct(dims, jnp.float32)


def scratch(layers, rows, level):
    return pltpu.VMEM((layers, rows * level.size, LANES), jnp.float32)


HBM = pl.BlockSpec(memory_space=pltpu.HBM)
VMEM = pl.BlockSpec(memory_space=pltpu.VMEM)


def call(kernel, out_shape, scratch_shapes=(), cost=None, limit=24, **options):
    if cost is not None:
        cost = pl.CostEstimate(flops=cost, bytes_accessed=cost // 8, transcendentals=0)
    return pl.pallas_call(
        kernel,
        out_shape=out_shape,
        scratch_shapes=list(scratch_shapes),
        cost_estimate=cost,
        compiler_params=pltpu.CompilerParams(vmem_limit_bytes=limit * 1024 * 1024),
        **options,
    )


def shards(stream_now, vorticity):
    _, rows, columns = stream_now.shape
    count = lax.axis_size("wide")
    tiles = columns // (SUBS * LANES)
    fine, mid = Level(0, tiles, 1), Level(1, tiles // 2, 1)
    two, three, four = Level(2, tiles // 4, 1), Level(3, tiles // 4, 2), Level(4, tiles // 4, 4)
    core_swap = [(i, i ^ 1) for i in range(count)]
    members = lax.axis_size("member")
    inside = [(i, ((i + 1) ^ 1) - 1) for i in range(1, count - 1)]
    if members % 2:
        ends = [(0, count - 1), (count - 1, 0)]
        chip_swap = [(m * count + i, m * count + j) for m in range(members) for i, j in ends]
    else:
        chip_swap = [
            (m * count + i, (m ^ 1) * count + i) for m in range(members) for i in (0, count - 1)
        ]
    chip_swap += [(m * count + i, m * count + j) for m in range(members) for i, j in inside]
    groups = rows // SUBS

    def exchange(near, far):
        far = lax.ppermute(far, ("member", "wide"), chip_swap)
        near = lax.ppermute(near, "wide", core_swap)
        return near, far

    half, quarter = rows // 2, rows // 4
    total = rows + 2 * HALO
    ext, near, far = call(
        functools.partial(pack_kernel, fine, rows),
        [shape(4, total * fine.size, LANES)] + [shape(4, HALO * fine.size, LANES)] * 2,
        [pltpu.VMEM((4, rows, columns), jnp.float32), pltpu.SemaphoreType.DMA((4,))],
        in_specs=[HBM, HBM],
    )(*(pltpu.with_memory_space_constraint(x, pltpu.HBM) for x in (stream_now, vorticity)))
    near, far = exchange(near, far)
    state = [
        shape(4, total * fine.size, LANES),
        shape(4, total * fine.size, LANES),
        shape(2, total * fine.size, LANES),
        shape(2, total * fine.size, LANES),
        shape(2, total * fine.size, LANES),
        shape(2, half * mid.size, LANES),
    ]
    early = shape(2, (MID_HALO - LATE) * mid.size, LANES)
    *inner, near_early, far_early = call(
        functools.partial(inner_kernel, fine, mid, rows),
        state + [early, early],
        cost=8000000,
    )(ext)
    near_early, far_early = exchange(near_early, far_early)
    edge = shape(2, LATE * mid.size, LANES)
    outer = call(
        functools.partial(outer_kernel, fine, mid, rows),
        [shape(4, total * fine.size, LANES)] + state + [edge, edge],
        input_output_aliases={i: i for i in range(7)},
    )(ext, *inner, near, far)
    b0, v0, b1, near, far = outer[3], outer[5], outer[6], outer[7], outer[8]
    near, far = exchange(near, far)
    chips = count // 2
    eighth = rows // 8
    two_edge = shape(2, 4 * two.size + fine.size, LANES)
    two_all = shape(2, (quarter + 2 * TWO_HALO) * two.size, LANES)
    b1, v1, b2, v2, b3, near, far = call(
        functools.partial(middle_kernel, fine, mid, two, three, half),
        [
            shape(2, (half + 2 * MID_HALO) * mid.size, LANES),
            shape(2, (half + 2 * MID_HALO) * mid.size, LANES),
            two_all,
            two_all,
            shape(chips, 2, eighth // 2 * three.size, LANES),
            two_edge,
            two_edge,
        ],
        [
            scratch(2, half + 2 * MID_HALO, mid),
            scratch(2, quarter + 2 * TWO_HALO, two),
            scratch(2, eighth, three),
        ],
    )(b1, near_early, far_early, near, far, v0)
    cores = [[i for i in range(count) if i % 2 == c] for c in range(2)]
    same = lax.all_to_all(b3, "wide", 0, 0, axis_index_groups=cores)
    other = lax.ppermute(same, "wide", core_swap)
    near, far = exchange(near, far)
    vorticity_next = call(
        functools.partial(emit_kernel, fine, rows),
        shape(2, rows, columns),
        [pltpu.VMEM((2, rows, columns), jnp.float32), pltpu.SemaphoreType.DMA((2, groups))],
        cost=4000000,
        out_specs=HBM,
    )(b0)
    n3, n4 = count * eighth, count * eighth // 2
    v3 = call(
        functools.partial(coarse_kernel, (three, four), rows),
        shape(2, (eighth + 4) * three.size, LANES),
        [scratch(2, n3 + 2 * PAD, three)] * 3
        + [scratch(2, n4, four), scratch(2, n4 + 2 * PAD, four)],
        cost=5000000,
    )(same, other)
    stream_next, _ = call(
        functools.partial(rise_kernel, (fine, mid, two, three), rows),
        [shape(2, rows, columns), shape(2, total * fine.size, LANES)],
        [scratch(2, quarter + 2 * TWO_HALO, two)] * 4
        + [scratch(2, half + 2 * MID_HALO, mid)] * 2
        + [scratch(2, total, fine)] * 3
        + [pltpu.VMEM((2, rows, columns), jnp.float32), pltpu.SemaphoreType.DMA((2, groups))],
        out_specs=[HBM, VMEM],
        input_output_aliases={8: 1},
    )(v3, near, far, b2, v2, b1, v1, b0, v0)
    return (vorticity_next, stream_next)


def solution(mesh):
    return jax.shard_map(
        shards,
        mesh=mesh,
        in_specs=(P("member", "wide", None), P("member", "wide", None)),
        out_specs=(P("member", "wide", None), P("member", "wide", None)),
        check_vma=False,
    )
```

```python
import functools

import jax
import jax.numpy as jnp
from jax import lax
from jax.experimental import pallas as pl
from jax.experimental.pallas import tpu as pltpu
from jax.sharding import PartitionSpec as P


LANES = 128
SUBS = 8
HALO = 3
MID_HALO = 6
LATE = 2
TWO_HALO = 4
RELAX = 0.8
COUPLING = (0.02, 0.04)
TIME_STEP = 0.5
BETA = 0.05
DRAG = (0.0, 0.02)
COARSE_SWEEPS = 8


class Level:
    def __init__(self, level, tiles, stride):
        h2 = (2.0**level) ** 2
        self.tiles, self.stride = tiles, stride
        diag = [4.0 / h2 + f for f in COUPLING]
        self.keep = 1.0 - RELAX
        self.near = [RELAX / (d * h2) for d in diag]
        self.other = [RELAX * f / d for f, d in zip(COUPLING, diag)]
        self.src = [RELAX / d for d in diag]
        self.diag = diag
        self.inv_h2 = 1.0 / h2
        self.size = tiles * SUBS


def lane_index():
    return lax.broadcasted_iota(jnp.int32, (SUBS, LANES), 1)


def at(level, row, tile=0):
    base = row * level.size
    if not isinstance(row, int):
        base = pl.multiple_of(base, SUBS)
    return pl.ds(base + tile * SUBS, SUBS)


def load(ref, level, layer, row):
    return [ref[layer, at(level, row, t), :] for t in range(level.tiles)]


def store(ref, level, layer, row, values):
    for t in range(level.tiles):
        ref[layer, at(level, row, t), :] = values[t]


def east(values, stride=1):
    rolled = [pltpu.roll(v, LANES - stride, 1) for v in values]
    after = rolled[1:] + [pltpu.roll(rolled[0], SUBS - 1, 0)]
    edge = lane_index() >= LANES - stride
    return [jnp.where(edge, a, r) for a, r in zip(after, rolled)]


def west(values, stride=1):
    rolled = [pltpu.roll(v, stride, 1) for v in values]
    before = [pltpu.roll(rolled[-1], 1, 0)] + rolled[:-1]
    edge = lane_index() < stride
    return [jnp.where(edge, b, r) for b, r in zip(before, rolled)]


def transpose_tiles(tiles):
    sub = lax.broadcasted_iota(jnp.int32, (SUBS, LANES), 0)
    for k in (1, 2, 4):
        keep = (sub & k) == 0
        out = list(tiles)
        for i in range(SUBS):
            if not i & k:
                a, b = tiles[i], tiles[i + k]
                out[i] = jnp.where(keep, a, pltpu.roll(b, k, 0))
                out[i + k] = jnp.where(keep, pltpu.roll(a, SUBS - k, 0), b)
        tiles = out
    return tiles


def column_of(level, t, s):
    first = (s * level.tiles + t) * LANES
    return slice(first, first + LANES)


def to_native(level, dst, dst_row, src, layer, src_row, sign=1):
    for t in range(level.tiles):
        tiles = [src[layer, at(level, src_row + r, t), :] for r in range(SUBS)]
        for s, tile in enumerate(transpose_tiles(tiles)):
            dst[layer, dst_row : dst_row + SUBS, column_of(level, t, s)] = (
                tile if sign > 0 else -tile
            )


def row_blocks(low, high, block, body, straight=48):
    count = high - low if isinstance(low, int) else high
    if count <= straight:
        block = count
    whole = count // block
    if whole > 1:
        lax.fori_loop(0, whole, lambda i, c: (body(low + i * block, block), c)[1], 0)
    elif whole == 1:
        body(low, block)
    if count % block:
        body(low + whole * block, count % block)


def star(rows, k, layer, level, sides=None):
    centre = rows[k][layer]
    if sides:
        e, w = sides[0][k][layer], sides[1][k][layer]
    else:
        e, w = east(centre, level.stride), west(centre, level.stride)
    return [
        (n + s) + (a + b)
        for n, s, a, b in zip(rows[k + 1][layer], rows[k - 1][layer], e, w)
    ]


def load_rows(ref, level, first, count, margin=1):
    return {
        k: [load(ref, level, layer, first + k) for layer in range(2)]
        for k in range(-margin, count + margin)
    }


def sweep_rows(level, rows, source, count, sides=None):
    out = {}
    for k in range(count):
        out[k] = []
        for layer in range(2):
            near = star(rows, k, layer, level, sides)
            out[k].append(
                [
                    (level.keep * c + level.near[layer] * n)
                    + (level.other[layer] * o + level.src[layer] * b)
                    for c, n, o, b in zip(
                        rows[k][layer], near, rows[k][1 - layer], source[k][layer]
                    )
                ]
            )
    return out


def residual_rows(level, rows, source, count):
    out = {}
    for k in range(count):
        out[k] = []
        for layer in range(2):
            near = star(rows, k, layer, level)
            out[k].append(
                [
                    (b - level.diag[layer] * c)
                    + (level.inv_h2 * n + COUPLING[layer] * o)
                    for c, n, o, b in zip(
                        rows[k][layer], near, rows[k][1 - layer], source[k][layer]
                    )
                ]
            )
    return out


def store_rows(ref, level, first, rows, count):
    for k in range(count):
        for layer in range(2):
            store(ref, level, layer, first + k, rows[k][layer])


def sweep(level, dst, dst_at, src, src_at, b, b_at, low, high, block, shifted=None, straight=48):
    def body(first, count):
        rows = load_rows(src, level, first + src_at, count)
        source = load_rows(b, level, first + b_at, count, 0)
        sides = None
        if shifted:
            sides = [load_rows(ref, level, first + src_at, count, 0) for ref in shifted]
        out = sweep_rows(level, rows, source, count, sides)
        store_rows(dst, level, first + dst_at, out, count)

    row_blocks(low, high, block, body, straight)


def start(level, dst, dst_at, b, b_at, low, high, block):
    def body(first, count):
        source = load_rows(b, level, first + b_at, count, 0)
        out = {
            k: [[level.src[l] * x for x in source[k][l]] for l in range(2)]
            for k in range(count)
        }
        store_rows(dst, level, first + dst_at, out, count)

    row_blocks(low, high, block, body)


def pack_columns(values):
    lane = lane_index()
    pick = (2 * lane) % LANES
    sums = [v + pltpu.roll(v, LANES - 1, 1) for v in values]
    picked = [jnp.take_along_axis(s, pick, axis=1) for s in sums]
    return [
        jnp.where(lane < LANES // 2, picked[2 * t], picked[2 * t + 1])
        for t in range(len(values) // 2)
    ]


def spread_columns(values):
    lane = lane_index()
    out = []
    for v in values:
        out.append(jnp.take_along_axis(v, lane // 2, axis=1))
        out.append(jnp.take_along_axis(v, LANES // 2 + lane // 2, axis=1))
    return out


def merge_columns(values, stride):
    even = (lane_index() // stride) % 2 == 0
    return [
        v + jnp.where(even, pltpu.roll(v, LANES - stride, 1), pltpu.roll(v, stride, 1))
        for v in values
    ]


def restrict(
    fine, dst, dst_at, coarse, src, src_at, b, b_at, low, high, block, straight=48
):
    def body(first, count):
        rows = load_rows(src, fine, 2 * first + src_at, 2 * count)
        source = load_rows(b, fine, 2 * first + b_at, 2 * count, 0)
        res = residual_rows(fine, rows, source, 2 * count)
        out = {}
        for k in range(count):
            out[k] = []
            for layer in range(2):
                pair = [x + y for x, y in zip(res[2 * k][layer], res[2 * k + 1][layer])]
                if coarse.tiles < fine.tiles:
                    pair = pack_columns(pair)
                else:
                    pair = merge_columns(pair, fine.stride)
                out[k].append([0.25 * x for x in pair])
        store_rows(dst, coarse, first + dst_at, out, count)

    row_blocks(low, high, block, body, straight)


def correct(fine, coarse, dst, dst_at, src, src_at, add, add_at, low, high, block):
    def body(first, count):
        coarse_rows = load_rows(add, coarse, first + add_at, count, 0)
        fine_rows = load_rows(src, fine, 2 * first + src_at, 2 * count, 0)
        out = {}
        for k in range(count):
            spread = [
                spread_columns(v) if coarse.tiles < fine.tiles else v for v in coarse_rows[k]
            ]
            for half in range(2):
                out[2 * k + half] = [
                    [x + y for x, y in zip(fine_rows[2 * k + half][l], spread[l])]
                    for l in range(2)
                ]
        store_rows(dst, fine, 2 * first + dst_at, out, 2 * count)

    row_blocks(low, high, block, body)


def clear(ref, level, low, high):
    ref[:, low * level.size : high * level.size, :] = jnp.zeros(
        (ref.shape[0], (high - low) * level.size, LANES), jnp.float32
    )


def place():
    me, count = lax.axis_index("wide"), lax.axis_size("wide")
    return me, lax.rem(me, 2), me == 0, me == count - 1


def pack_kernel(level, rows, p_ref, q_ref, ext_ref, near_ref, far_ref, native, sems):
    copies = []
    for field, ref in enumerate((p_ref, q_ref)):
        for layer in range(2):
            which = 2 * field + layer
            copies.append(
                pltpu.make_async_copy(ref.at[layer], native.at[which], sems.at[which])
            )
            copies[-1].start()
    for which in range(4):
        copies[which].wait()
        for group in range(rows // SUBS):
            for t in range(level.tiles):
                tiles = [
                    native[which, group * SUBS : (group + 1) * SUBS, column_of(level, t, s)]
                    for s in range(SUBS)
                ]
                for r, tile in enumerate(transpose_tiles(tiles)):
                    ext_ref[which, at(level, HALO + group * SUBS + r, t), :] = tile
    send_edges(level, HALO, HALO, rows, ext_ref, near_ref, far_ref)


def send_edges(level, width, src_at, rows, src, near_ref, far_ref):
    _, odd, _, _ = place()
    size = width * level.size
    last = (src_at + rows - width) * level.size
    top = src_at * level.size
    near = pl.multiple_of(jnp.where(odd == 1, top, last), SUBS)
    far = pl.multiple_of(jnp.where(odd == 1, last, top), SUBS)
    near_ref[:, 0:size, :] = src[:, pl.ds(near, size), :]
    far_ref[:, 0:size, :] = src[:, pl.ds(far, size), :]


def receive_edges(level, width, dst_at, rows, dst, near_ref, far_ref):
    _, odd, first, last = place()
    size = width * level.size
    low = (dst_at + rows) * level.size
    top = (dst_at - width) * level.size
    near = pl.multiple_of(jnp.where(odd == 1, top, low), SUBS)
    far = pl.multiple_of(jnp.where(odd == 1, low, top), SUBS)
    dst[:, pl.ds(near, size), :] = near_ref[:, 0:size, :]
    outside = jnp.logical_or(first, last)
    dst[:, pl.ds(far, size), :] = jnp.where(outside, 0.0, far_ref[:, 0:size, :])


def shift_rows(level, ext, e_ref, w_ref, low, high, block):
    def body(first, count):
        for k in range(count):
            for f in range(4):
                v = load(ext, level, f, first + k)
                store(e_ref, level, f, first + k, east(v))
                store(w_ref, level, f, first + k, west(v))

    row_blocks(low, high, block, body)


def advance_rows(level, b_ref, ext, e_ref, w_ref, low, high, block):
    def body(first, count):
        for layer in range(2):
            for t in range(level.tiles):
                def grab(ref, field):
                    return {
                        k: ref[2 * field + layer, at(level, first + k, t), :]
                        for k in range(-1, count + 1)
                    }

                p, pe, pw = grab(ext, 0), grab(e_ref, 0), grab(w_ref, 0)
                q, qe, qw = grab(ext, 1), grab(e_ref, 1), grab(w_ref, 1)
                zonal = {k: pe[k] - pw[k] for k in p}
                for k in range(count):
                    n, s = k + 1, k - 1
                    v0, ve, vw = p[n] - p[s], pe[n] - pe[s], pw[n] - pw[s]
                    jac = q[n] * (zonal[k] + zonal[n]) - q[s] * (zonal[k] + zonal[s])
                    jac = jac - qe[k] * (v0 + ve) + qw[k] * (v0 + vw)
                    jac = jac + qe[n] * (pe[k] - p[n]) - qe[s] * (pe[k] - p[s])
                    jac = jac - qw[n] * (pw[k] - p[n]) + qw[s] * (pw[k] - p[s])
                    step = (TIME_STEP / 12.0) * jac + (0.5 * TIME_STEP * BETA) * zonal[k]
                    if layer == 1:
                        lap = (p[n] + p[s]) + (pe[k] + pw[k]) - 4.0 * p[k]
                        step = step + (TIME_STEP * DRAG[1]) * lap
                    b_ref[layer, at(level, first + k, t), :] = step - q[k]

    row_blocks(low, high, block, body)


def inner_kernel(
    level, coarse, rows, ext, e_ref, w_ref, b_ref, v_one, v_two, bc_ref, early_near, early_far
):
    low, high = HALO, HALO + rows
    shift_rows(level, ext, e_ref, w_ref, low, high, 4)
    advance_rows(level, b_ref, ext, e_ref, w_ref, low + 1, high - 1, 2)
    sweep(level, v_one, 0, ext, 0, b_ref, 0, low + 2, high - 2, 4, (e_ref, w_ref))
    sweep(level, v_two, 0, v_one, 0, b_ref, 0, low + 3, high - 3, 4)
    restrict(level, bc_ref, 0, coarse, v_two, HALO, b_ref, HALO, LATE, rows // 2 - LATE, 2)
    size = (MID_HALO - LATE) * coarse.size
    first, last = LATE * coarse.size, (rows // 2 - MID_HALO) * coarse.size
    _, odd, _, _ = place()
    near = pl.multiple_of(jnp.where(odd == 1, first, last), SUBS)
    far = pl.multiple_of(jnp.where(odd == 1, last, first), SUBS)
    early_near[...] = bc_ref[:, pl.ds(near, size), :]
    early_far[...] = bc_ref[:, pl.ds(far, size), :]


def outer_kernel(level, coarse, rows, far, *refs):
    halo_ref = refs[7]
    ext, e_ref, w_ref, b_ref, v_one, v_two, bc_ref, send_ref = refs[8:]
    _, odd, is_first, is_last = place()
    high, half = HALO + rows, rows // 2
    total = rows + 2 * HALO
    top = odd == 0 if far else odd == 1

    def pick(above, below):
        return jnp.where(top, above, below)

    outside = jnp.logical_and(far, jnp.logical_or(is_first, is_last))
    size = HALO * level.size
    edge = pl.ds(pl.multiple_of(pick(0, high) * level.size, SUBS), size)
    halo = halo_ref[...]
    ext[:, edge, :] = jnp.where(outside, 0.0, halo) if far else halo
    shift_rows(level, ext, e_ref, w_ref, pick(0, high), HALO, HALO)
    advance_rows(level, b_ref, ext, e_ref, w_ref, pick(1, high - 1), HALO, HALO)
    count = HALO + 1
    sides = (e_ref, w_ref)
    sweep(level, v_one, 0, ext, 0, b_ref, 0, pick(1, high - 2), count, count, sides)

    def trim(ref):
        if far:
            @pl.when(outside)
            def _():
                ref[:, edge, :] = jnp.zeros((2, size, LANES), jnp.float32)

    trim(v_one)
    sweep(level, v_two, 0, v_one, 0, b_ref, 0, pick(2, total - 2 - count), count, count)
    trim(v_two)
    late = pick(0, half - LATE)
    restrict(level, bc_ref, 0, coarse, v_two, HALO, b_ref, HALO, late, LATE, LATE)
    rows_of = pl.ds(pl.multiple_of(late * coarse.size, SUBS), LATE * coarse.size)
    send_ref[...] = bc_ref[:, rows_of, :]


def emit(level, rows, b_ref, next_ref, native, sems):
    copies = []
    for layer in range(2):
        for group in range(rows // SUBS):
            rows_of = pl.ds(group * SUBS, SUBS)
            to_native(level, native, group * SUBS, b_ref, layer, HALO + group * SUBS, -1)
            copies.append(
                pltpu.make_async_copy(
                    native.at[layer, rows_of], next_ref.at[layer, rows_of],
                    sems.at[layer, group],
                )
            )
            copies[-1].start()
    return copies


def emit_kernel(level, rows, b_ref, next_ref, native, sems):
    for copy in emit(level, rows, b_ref, next_ref, native, sems):
        copy.wait()


def middle_kernel(
    fine, level, two, three, rows, b_own, early_near, early_far, near_ref, far_ref, v0_ref,
    b_ref, v_ref, b2_ref, v2_ref, out_ref, two_near_ref, two_far_ref,
    v_one, w_two, b3,
):
    _, odd, is_first, is_last = place()
    total = rows + 2 * MID_HALO
    own = rows // 2
    edge = MID_HALO * level.size
    b_ref[:, edge : edge + rows * level.size, :] = b_own[...]
    receive_edges(level, LATE, MID_HALO, rows, b_ref, near_ref, far_ref)
    early = MID_HALO - LATE
    receive_edges(level, early, early, rows + 2 * LATE, b_ref, early_near, early_far)
    start(level, v_one, 0, b_ref, 0, 0, total, 4)

    def trim(ref, of, halo, n):
        @pl.when(is_first)
        def _():
            clear(ref, of, 0, halo)

        @pl.when(is_last)
        def _():
            clear(ref, of, halo + n, 2 * halo + n)

    trim(v_one, level, MID_HALO, rows)
    sweep(level, v_ref, 0, v_one, 0, b_ref, 0, 1, total - 1, 6)
    trim(v_ref, level, MID_HALO, rows)
    restrict(
        level, b2_ref, TWO_HALO, two, v_ref, MID_HALO, b_ref, MID_HALO, -2, own + 2, 4
    )
    start(two, w_two, TWO_HALO, b2_ref, TWO_HALO, -2, own + 2, 8)
    trim(w_two, two, TWO_HALO, own)
    sweep(two, v2_ref, TWO_HALO, w_two, TWO_HALO, b2_ref, TWO_HALO, -1, own + 1, 6)
    trim(v2_ref, two, TWO_HALO, own)
    restrict(
        two, b3, 0, three, v2_ref, TWO_HALO, b2_ref, TWO_HALO, 0, own // 2, 2
    )
    even = lane_index() % 2 == 0
    for layer in range(2):
        for pair in range(own // 4):
            row = jnp.where(
                even,
                b3[layer, at(three, 2 * pair), :],
                b3[layer, at(three, 2 * pair + 1), :],
            )
            for copy in range(out_ref.shape[0]):
                out_ref[copy, layer, at(three, pair), :] = row
    up, down = pl.ds((TWO_HALO + 1) * two.size, 3 * two.size), pl.ds(
        own * two.size, 3 * two.size
    )
    up_b, down_b = at(two, TWO_HALO + 2), at(two, TWO_HALO + own - 3)
    last = pl.ds(3 * two.size, two.size)

    tail = pl.ds(4 * two.size, fine.size)
    up_0 = pl.ds((HALO + 1) * fine.size, fine.size)
    down_0 = pl.ds((HALO + 2 * rows - 2) * fine.size, fine.size)

    def send(ref, rows_v, row_b, row_0):
        ref[:, 0 : 3 * two.size, :] = v2_ref[:, rows_v, :]
        ref[:, last, :] = b2_ref[:, row_b, :]
        ref[:, tail, :] = v0_ref[:, row_0, :]

    @pl.when(odd == 1)
    def _():
        send(two_near_ref, up, up_b, up_0)
        send(two_far_ref, down, down_b, down_0)

    @pl.when(odd == 0)
    def _():
        send(two_near_ref, down, down_b, down_0)
        send(two_far_ref, up, up_b, up_0)


PAD = 4


def coarse_solve(level, dst, dst_at, b_ref, n):
    groups = level.stride
    m = n // groups
    part = lane_index() % groups
    source = []
    for layer in range(2):
        source.append([])
        for k in range(m):
            tile = load(b_ref, level, layer, k)[0]
            for g in range(1, groups):
                tile = jnp.where(part == g, load(b_ref, level, layer, g * m + k)[0], tile)
            source[layer].append(level.src[layer] * tile)
    values = source
    for _ in range(COARSE_SWEEPS - 1):
        new = []
        for layer in range(2):
            v, o = values[layer], values[1 - layer]
            below = jnp.where(part == groups - 1, 0.0, pltpu.roll(v[0], LANES - 1, 1))
            above = jnp.where(part == 0, 0.0, pltpu.roll(v[-1], 1, 1))
            out = []
            for k in range(m):
                n_row = v[k + 1] if k + 1 < m else below
                s_row = v[k - 1] if k else above
                e, w = east([v[k]], groups)[0], west([v[k]], groups)[0]
                out.append(
                    (level.keep * v[k] + level.near[layer] * ((n_row + s_row) + (e + w)))
                    + (level.other[layer] * o[k] + source[layer][k])
                )
            new.append(out)
        values = new
    for layer in range(2):
        for k in range(m):
            moved = {
                d: pltpu.roll(values[layer][k], d % LANES, 1) if d else values[layer][k]
                for d in range(1 - groups, groups)
            }
            for g in range(groups):
                tile = moved[-g]
                for j in range(1, groups):
                    tile = jnp.where(part == j, moved[j - g], tile)
                dst[layer, at(level, dst_at + g * m + k), :] = tile


def coarse_kernel(
    levels, rows, same_ref, other_ref, out_ref, b3, v3, w3, b4, v4,
):
    me, odd, is_first, is_last = place()
    three, four = levels
    own = rows // 4
    chips = same_ref.shape[0]
    n3, n4 = chips * own, chips * own // 2
    for ref, level, n in ((b3, three, n3), (v3, three, n3), (w3, three, n3), (v4, four, n4)):
        clear(ref, level, 0, PAD)
        clear(ref, level, PAD + n, 2 * PAD + n)
    even = lane_index() % 2 == 0

    def gather_body(chip, carry):
        for ref, core in ((same_ref, odd), (other_ref, 1 - odd)):
            row = (2 * chip + core) * (own // 2) + PAD
            for layer in range(2):
                for pair in range(own // 4):
                    both = ref[chip, layer, at(three, pair), :]
                    first = jnp.where(even, both, pltpu.roll(both, 1, 1))
                    second = jnp.where(even, pltpu.roll(both, LANES - 1, 1), both)
                    b3[layer, at(three, row + 2 * pair), :] = first
                    b3[layer, at(three, row + 2 * pair + 1), :] = second
        return carry

    lax.fori_loop(0, chips, gather_body, 0, unroll=min(chips, 8))

    start(three, v3, PAD, b3, PAD, 0, n3, 8)
    sweep(three, w3, PAD, v3, PAD, b3, PAD, 0, n3, 16, straight=0)
    restrict(three, b4, 0, four, w3, PAD, b3, PAD, 0, n4, 8, straight=0)
    coarse_solve(four, v4, PAD, b4, n4)

    def trim(ref, level, n):
        @pl.when(me < 2)
        def _():
            clear(ref, level, 0, PAD)

        @pl.when(me >= 2 * chips - 2)
        def _():
            clear(ref, level, PAD + n, 2 * PAD + n)

    half, quarter = own // 2, own // 4
    correct(three, four, v3, PAD, w3, PAD, v4, PAD, me * quarter - 2, quarter + 4, 8)
    sweep(three, w3, PAD, v3, PAD, b3, PAD, me * half - 3, half + 6, 8)
    trim(w3, three, n3)
    sweep(three, out_ref, 2 - me * half, w3, PAD, b3, PAD, me * half - 2, half + 4, 8)

    @pl.when(is_first)
    def _():
        clear(out_ref, three, 0, 2)

    @pl.when(is_last)
    def _():
        clear(out_ref, three, half + 2, half + 4)


def rise_kernel(
    levels, rows, v3_ref, near_ref, far_ref,
    b2_ref, v2_ref, b1_ref, v1_ref, b0_ref, v0_in, out_ref, v0_ref,
    b2, v2, x2, y2, x1, y1, x0, y0, z0, native, sems,
):
    _, odd, is_first, is_last = place()
    fine, mid, two, three = levels
    own = rows // 4

    b2[...] = b2_ref[...]
    v2[...] = v2_ref[...]

    def take(ref, zero):
        top_v, low_v = pl.ds(0, 3 * two.size), pl.ds((TWO_HALO + own + 1) * two.size, 3 * two.size)
        top_b, low_b = at(two, TWO_HALO - 3), at(two, TWO_HALO + own + 2)
        last = pl.ds(3 * two.size, two.size)

        tail = pl.ds(4 * two.size, fine.size)
        top_0 = pl.ds((HALO - 2) * fine.size, fine.size)
        low_0 = pl.ds((HALO + rows + 1) * fine.size, fine.size)

        def drop(values):
            return values if zero is None else jnp.where(zero, 0.0, values)

        def put(rows_v, row_b, row_0):
            v2[:, rows_v, :] = drop(ref[:, 0 : 3 * two.size, :])
            b2[:, row_b, :] = ref[:, last, :]
            v0_ref[:, row_0, :] = drop(ref[:, tail, :])

        return lambda: put(top_v, top_b, top_0), lambda: put(low_v, low_b, low_0)

    near_top, near_low = take(near_ref, None)
    far_top, far_low = take(far_ref, jnp.logical_or(is_first, is_last))

    @pl.when(odd == 1)
    def _():
        near_top()
        far_low()

    @pl.when(odd == 0)
    def _():
        near_low()
        far_top()

    def trim_own(ref, level, halo, n):
        @pl.when(is_first)
        def _():
            clear(ref, level, 0, halo)

        @pl.when(is_last)
        def _():
            clear(ref, level, halo + n, 2 * halo + n)

    total = own + 2 * TWO_HALO
    correct(two, three, x2, 0, v2, 0, v3_ref, 0, 0, total // 2, 8)
    sweep(two, y2, 0, x2, 0, b2, 0, 1, total - 1, 10)
    trim_own(y2, two, TWO_HALO, own)
    sweep(two, x2, 0, y2, 0, b2, 0, 2, total - 2, 8)
    trim_own(x2, two, TWO_HALO, own)

    n1 = rows // 2
    total = n1 + 2 * MID_HALO

    correct(
        mid, two, x1, MID_HALO - 4, v1_ref, MID_HALO - 4, x2, TWO_HALO - 2, 0, n1 // 2 + 4, 4
    )
    sweep(mid, y1, 0, x1, 0, b1_ref, 0, MID_HALO - 2, MID_HALO + n1 + 2, 6)
    trim_own(y1, mid, MID_HALO, n1)
    sweep(mid, x1, 0, y1, 0, b1_ref, 0, MID_HALO - 1, MID_HALO + n1 + 1, 5)
    trim_own(x1, mid, MID_HALO, n1)

    low, done, swept = HALO, 0, HALO - 1
    copies = []
    for group in range(rows // SUBS):
        first_row = low + group * SUBS
        rows_of = pl.ds(group * SUBS, SUBS)
        ready = SUBS // 2 * (group + 1) + 2
        correct(fine, mid, x0, HALO - 2, v0_ref, HALO - 2, x1, MID_HALO - 1, done, ready, 2)
        sweep(fine, y0, 0, x0, 0, b0_ref, 0, swept, first_row + SUBS + 1, 5 - group)
        trim_own(y0, fine, HALO, rows)
        done, swept = ready, first_row + SUBS + 1
        sweep(fine, z0, 0, y0, 0, b0_ref, 0, first_row, first_row + SUBS, 4)
        for layer in range(2):
            to_native(fine, native, group * SUBS, z0, layer, first_row)
            copies.append(
                pltpu.make_async_copy(
                    native.at[layer, rows_of], out_ref.at[layer, rows_of],
                    sems.at[layer, group],
                )
            )
            copies[-1].start()
    for copy in copies:
        copy.wait()


def shape(*dims):
    return jax.ShapeDtypeStruct(dims, jnp.float32)


def scratch(layers, rows, level):
    return pltpu.VMEM((layers, rows * level.size, LANES), jnp.float32)


HBM = pl.BlockSpec(memory_space=pltpu.HBM)
VMEM = pl.BlockSpec(memory_space=pltpu.VMEM)


def call(kernel, out_shape, scratch_shapes=(), cost=None, limit=24, **options):
    if cost is not None:
        cost = pl.CostEstimate(flops=cost, bytes_accessed=cost // 8, transcendentals=0)
    return pl.pallas_call(
        kernel,
        out_shape=out_shape,
        scratch_shapes=list(scratch_shapes),
        cost_estimate=cost,
        compiler_params=pltpu.CompilerParams(vmem_limit_bytes=limit * 1024 * 1024),
        **options,
    )


def shards(stream_now, vorticity):
    _, rows, columns = stream_now.shape
    count = lax.axis_size("wide")
    tiles = columns // (SUBS * LANES)
    fine, mid = Level(0, tiles, 1), Level(1, tiles // 2, 1)
    two, three, four = Level(2, tiles // 4, 1), Level(3, tiles // 4, 2), Level(4, tiles // 4, 4)
    core_swap = [(i, i ^ 1) for i in range(count)]
    members = lax.axis_size("member")
    inside = [(i, ((i + 1) ^ 1) - 1) for i in range(1, count - 1)]
    if members % 2:
        ends = [(0, count - 1), (count - 1, 0)]
        chip_swap = [(m * count + i, m * count + j) for m in range(members) for i, j in ends]
    else:
        chip_swap = [
            (m * count + i, (m ^ 1) * count + i) for m in range(members) for i in (0, count - 1)
        ]
    chip_swap += [(m * count + i, m * count + j) for m in range(members) for i, j in inside]
    groups = rows // SUBS

    def exchange(near, far):
        far = lax.ppermute(far, ("member", "wide"), chip_swap)
        near = lax.ppermute(near, "wide", core_swap)
        return near, far

    half, quarter = rows // 2, rows // 4
    total = rows + 2 * HALO
    ext, near, far = call(
        functools.partial(pack_kernel, fine, rows),
        [shape(4, total * fine.size, LANES)] + [shape(4, HALO * fine.size, LANES)] * 2,
        [pltpu.VMEM((4, rows, columns), jnp.float32), pltpu.SemaphoreType.DMA((4,))],
        in_specs=[HBM, HBM],
    )(*(pltpu.with_memory_space_constraint(x, pltpu.HBM) for x in (stream_now, vorticity)))
    near, far = exchange(near, far)
    state = [
        shape(4, total * fine.size, LANES),
        shape(4, total * fine.size, LANES),
        shape(2, total * fine.size, LANES),
        shape(2, total * fine.size, LANES),
        shape(2, total * fine.size, LANES),
        shape(2, half * mid.size, LANES),
    ]
    early = shape(2, (MID_HALO - LATE) * mid.size, LANES)
    *inner, near_early, far_early = call(
        functools.partial(inner_kernel, fine, mid, rows),
        state + [early, early],
        cost=8000000,
    )(ext)
    near_early, far_early = exchange(near_early, far_early)
    edge = shape(2, LATE * mid.size, LANES)

    def outer(far, arrays, halo):
        return call(
            functools.partial(outer_kernel, fine, mid, rows, far),
            [shape(4, total * fine.size, LANES)] + state + [edge],
            cost=4000000,
            input_output_aliases={i: i for i in range(7)},
        )(*arrays, halo)

    *arrays, near = outer(False, [ext, *inner], near)
    *arrays, far = outer(True, arrays, far)
    b0, v0, b1 = arrays[3], arrays[5], arrays[6]
    near, far = exchange(near, far)
    chips = count // 2
    eighth = rows // 8
    two_edge = shape(2, 4 * two.size + fine.size, LANES)
    two_all = shape(2, (quarter + 2 * TWO_HALO) * two.size, LANES)
    b1, v1, b2, v2, b3, near, far = call(
        functools.partial(middle_kernel, fine, mid, two, three, half),
        [
            shape(2, (half + 2 * MID_HALO) * mid.size, LANES),
            shape(2, (half + 2 * MID_HALO) * mid.size, LANES),
            two_all,
            two_all,
            shape(chips, 2, eighth // 2 * three.size, LANES),
            two_edge,
            two_edge,
        ],
        [
            scratch(2, half + 2 * MID_HALO, mid),
            scratch(2, quarter + 2 * TWO_HALO, two),
            scratch(2, eighth, three),
        ],
    )(b1, near_early, far_early, near, far, v0)
    cores = [[i for i in range(count) if i % 2 == c] for c in range(2)]
    same = lax.all_to_all(b3, "wide", 0, 0, axis_index_groups=cores)
    other = lax.ppermute(same, "wide", core_swap)
    near, far = exchange(near, far)
    vorticity_next = call(
        functools.partial(emit_kernel, fine, rows),
        shape(2, rows, columns),
        [pltpu.VMEM((2, rows, columns), jnp.float32), pltpu.SemaphoreType.DMA((2, groups))],
        cost=4000000,
        out_specs=HBM,
    )(b0)
    n3, n4 = count * eighth, count * eighth // 2
    v3 = call(
        functools.partial(coarse_kernel, (three, four), rows),
        shape(2, (eighth + 4) * three.size, LANES),
        [scratch(2, n3 + 2 * PAD, three)] * 3
        + [scratch(2, n4, four), scratch(2, n4 + 2 * PAD, four)],
        cost=5000000,
    )(same, other)
    stream_next, _ = call(
        functools.partial(rise_kernel, (fine, mid, two, three), rows),
        [shape(2, rows, columns), shape(2, total * fine.size, LANES)],
        [scratch(2, quarter + 2 * TWO_HALO, two)] * 4
        + [scratch(2, half + 2 * MID_HALO, mid)] * 2
        + [scratch(2, total, fine)] * 3
        + [pltpu.VMEM((2, rows, columns), jnp.float32), pltpu.SemaphoreType.DMA((2, groups))],
        out_specs=[HBM, VMEM],
        input_output_aliases={8: 1},
    )(v3, near, far, b2, v2, b1, v1, b0, v0)
    return (vorticity_next, stream_next)


def solution(mesh):
    return jax.shard_map(
        shards,
        mesh=mesh,
        in_specs=(P("member", "wide", None), P("member", "wide", None)),
        out_specs=(P("member", "wide", None), P("member", "wide", None)),
        check_vma=False,
    )
```
